32 devices in a mesh: fsdp: 8 (over z, y), ctx: 4 (over x, core).
Axes of the slice: x: 2, y: 2, z: 4, core: 2. Of those that a mesh axis runs over, the one named last changes fastest.
Arguments:
- block_input: bfloat16 [8192, 1024], P(('fsdp', 'ctx')), may hold values from -6 to 6
- ln1_gain: bfloat16 [1024], P('fsdp'), may hold values from 0.5 to 1.5
- ln1_bias: bfloat16 [1024], P('fsdp'), may hold values from -1.5 to 1.5
- qkv_weight: bfloat16 [1024, 3, 1024], P('fsdp', None, 'ctx'), may hold values from -0.1875 to 0.1875
- qv_bias: bfloat16 [2, 1024], P(None, 'fsdp'), may hold values from -2.5 to 2.5
- out_weight: bfloat16 [1024, 1024], P(('ctx', 'fsdp')), may hold values from -1.5 to 1.5
- out_bias: bfloat16 [1024], P('fsdp'), may hold values from -1.5 to 1.5
- ln2_gain: bfloat16 [1024], P('fsdp'), may hold values from 0.5 to 1.5
- ln2_bias: bfloat16 [1024], P('fsdp'), may hold values from -1.5 to 1.5
- up_weight: bfloat16 [1024, 4096], P('fsdp', 'ctx'), may hold values from -0.1875 to 0.1875
- up_bias: bfloat16 [4096], P('fsdp'), may hold values from -2.5 to 2.5
- down_weight: bfloat16 [4096, 1024], P(('ctx', 'fsdp')), may hold values from -0.1875 to 0.1875
- down_bias: bfloat16 [1024], P('fsdp'), may hold values from -1.5 to 1.5
- doc_ids: int32 [8, 1024], P('fsdp'), may hold values from -1 to 7, as said below
- cotangent: bfloat16 [8192, 1024], P(('fsdp', 'ctx')), may hold values from -6 to 6
Outputs:
- output: bfloat16 [8192, 1024], P(('fsdp', 'ctx'))
- input_grad: float32 [8192, 1024], P(('fsdp', 'ctx'))
- ln1_gain_grad: float32 [1024], P('fsdp')
- ln1_bias_grad: float32 [1024], P('fsdp')
- qkv_weight_grad: float32 [1024, 3, 1024], P('fsdp', None, 'ctx')
- qv_bias_grad: float32 [2, 1024], P(None, 'fsdp')
- out_weight_grad: float32 [1024, 1024], P(('ctx', 'fsdp'))
- out_bias_grad: float32 [1024], P('fsdp')
- ln2_gain_grad: float32 [1024], P('fsdp')
- ln2_bias_grad: float32 [1024], P('fsdp')
- up_weight_grad: float32 [1024, 4096], P('fsdp', 'ctx')
- up_bias_grad: float32 [4096], P('fsdp')
- down_weight_grad: float32 [4096, 1024], P(('ctx', 'fsdp'))
- down_bias_grad: float32 [1024], P('fsdp')
The draws below stay inside these ranges and needn't reach their ends.
Inputs may be any that keep to these rules, and one draw needn't show every extreme that they name: `doc_ids`: along each group, numbers start at 0 and rise by one from one sequence to the next; padding (-1) only at a group's end. A sequence holds 128 to 1024 positions, except that a group's last sequence may be cut short; some sequence holds exactly 1024; some group has no padding and some group is half padding.
All inputs are finite; a program needn't handle non-finite values.
Results may differ from the reference program's by a relative error of at most 0.02.
Values may be sent and summed in bfloat16 or wider, within the bound.
A program may use at most 128 MiB of HBM per device.

```python
import jax
import jax.numpy as jnp
from jax import lax

D = 1024
HEADS = 16
HD = 64
FF = 4096
SEQ_MAX = 1024
CAP = 1024
TOKENS = 8192
QB = 512
SLOTS = 10
N_FSDP = 8


def draw_doc_ids(key, part):
    least = max(1, SEQ_MAX // 8)
    key_lengths, key_chosen, key_cuts = jax.random.split(key, 3)
    lengths = jax.random.randint(key_lengths, (N_FSDP, SLOTS), least, SEQ_MAX + 1, dtype=jnp.int32)
    chosen = jax.random.randint(key_chosen, (), 0, N_FSDP, dtype=jnp.int32)
    group_index = jnp.arange(N_FSDP, dtype=jnp.int32)
    column = jnp.arange(SLOTS, dtype=jnp.int32)
    shortest = (chosen + 2) % N_FSDP
    lengths = jnp.where((group_index == shortest)[:, None], least, lengths)
    first = (group_index[:, None] == chosen) & (column[None, :] == 0)
    lengths = jnp.where(first, SEQ_MAX, lengths)
    cuts = jax.random.randint(key_cuts, (N_FSDP,), 0, CAP // 2 + 1, dtype=jnp.int32)
    filled = CAP - cuts
    filled = jnp.where(group_index == chosen, CAP, filled)
    filled = jnp.where(group_index == (chosen + 1) % N_FSDP, CAP // 2, filled)
    filled = jnp.where(group_index == shortest, CAP, filled)
    ends = jnp.cumsum(lengths, axis=1)
    places = jnp.arange(CAP, dtype=jnp.int32)
    numbers = jnp.sum((places[None, :, None] >= ends[:, None, :]).astype(jnp.int32), axis=2)
    return jnp.where(places[None, :] < filled[:, None], numbers, -1).astype(jnp.int32)


def level_of(stream_key, extent, cuts, low, high):
    level, own = 1.0, jax.random.fold_in(stream_key, 6)
    for dim, parts in cuts:
        steps = jnp.exp(jax.random.uniform(jax.random.fold_in(own, dim), (parts,), jnp.float32, low / len(cuts), high / len(cuts)))
        level = level * jnp.repeat(steps, extent[dim] // parts).reshape([-1 if axis == dim else 1 for axis in range(len(extent))])
    return level


def bell_draw(rng, shape, deviation, most, cuts=(), held_as=jnp.bfloat16):
    drawn = deviation * jax.random.normal(rng, shape, jnp.float32)
    if cuts:
        drawn = drawn * level_of(rng, shape, cuts, -0.22, 0.18)
    return jnp.clip(drawn, -most, most).astype(held_as)


def setup_inputs(seed: int = 0) -> dict:
    streams_of = jax.random.split(jax.random.key(seed), 16)
    return {
        "block_input": bell_draw(streams_of[0], (TOKENS, D), 1.0, 6.0, ((0, 32),)),
        "ln1_gain": jnp.clip(1.0 + 0.1 * jax.random.normal(streams_of[1], (D,), jnp.float32), 0.5, 1.5).astype(jnp.bfloat16),
        "ln1_bias": bell_draw(streams_of[2], (D,), 0.3, 1.5, ((0, 8),)),
        "qkv_weight": bell_draw(streams_of[3], (D, 3, D), D ** -0.5, 0.1875, ((0, 8), (2, 4))),
        "qv_bias": bell_draw(streams_of[4], (2, D), 0.5, 2.5, ((1, 8),)),
        "out_weight": bell_draw(streams_of[5], (D, D), (D // 64) ** -0.5, 1.5, ((0, 32),)),
        "out_bias": bell_draw(streams_of[6], (D,), 0.3, 1.5, ((0, 8),)),
        "ln2_gain": jnp.clip(1.0 + 0.1 * jax.random.normal(streams_of[7], (D,), jnp.float32), 0.5, 1.5).astype(jnp.bfloat16),
        "ln2_bias": bell_draw(streams_of[8], (D,), 0.3, 1.5, ((0, 8),)),
        "up_weight": bell_draw(streams_of[9], (D, FF), D ** -0.5, 0.1875, ((0, 8), (1, 4))),
        "up_bias": bell_draw(streams_of[10], (FF,), 0.5, 2.5, ((0, 8),)),
        "down_weight": bell_draw(streams_of[11], (FF, D), (FF // 4) ** -0.5, 0.1875, ((0, 32),)),
        "down_bias": bell_draw(streams_of[12], (D,), 0.3, 1.5, ((0, 8),)),
        "doc_ids": draw_doc_ids(jax.random.fold_in(streams_of[15], 71), 0),
        "cotangent": bell_draw(streams_of[14], (TOKENS, D), 1.0, 6.0, ((0, 32),)),
    }


eps = 1e-05

@jax.custom_vjp
def low(v):
    return lax.optimization_barrier(v.astype(jnp.bfloat16)).astype(jnp.float32)

@jax.custom_vjp
def low_back(v):
    return v

def low_keep(v):
    return (low(v), None)

def low_pass(kept, grad):
    return (grad,)

def back_keep(v):
    return (v, None)

def back_low(kept, grad):
    return (low(grad),)
low.defvjp(low_keep, low_pass)
low_back.defvjp(back_keep, back_low)

def layer_norm(values, gain, shift):
    centre = values - lax.optimization_barrier(jnp.mean(values, axis=-1, keepdims=True))
    spread = lax.optimization_barrier(jnp.mean(centre * centre, axis=-1, keepdims=True))
    return centre * lax.rsqrt(spread + eps) * gain + shift

def gelu_tanh(values):
    return 0.5 * values * (1.0 + jnp.tanh(0.7978845608028654 * (values + 0.044715 * values * values * values)))

def matmul(left, right):
    return jnp.dot(left, right, precision=lax.Precision.HIGHEST, preferred_element_type=jnp.float32)

def forward_group(params, inputs, seq_ids):
    gain_one, shift_one, w_qkv, qv_shift, w_out, out_shift, gain_two, shift_two, w_up, up_shift, w_down, down_shift = params
    h_one = low(layer_norm(inputs, gain_one, shift_one))
    qkv_shift = jnp.concatenate([qv_shift[0], jnp.zeros((D,), jnp.float32), qv_shift[1]])
    qkv = low(low_back(matmul(h_one, w_qkv.reshape(D, 3 * D)) + qkv_shift))
    queries = qkv[:, :D].reshape(CAP, HEADS, HD)
    keys_all = qkv[:, D:2 * D].reshape(CAP, HEADS, HD)
    values_all = qkv[:, 2 * D:].reshape(CAP, HEADS, HD)
    places = jnp.arange(CAP, dtype=jnp.int32)
    factor = 1.0 / HD ** 0.5

    def one_block(start):
        query_blk = lax.dynamic_slice_in_dim(queries, start, QB, 0)
        ids_blk = lax.dynamic_slice_in_dim(seq_ids, start, QB, 0)
        rows_blk = start + jnp.arange(QB, dtype=jnp.int32)
        scores = jnp.einsum('qhd,khd->hqk', query_blk, keys_all, precision=lax.Precision.HIGHEST)
        scores = low_back(scores * factor)
        allowed = (ids_blk[:, None] == seq_ids[None, :]) & (places[None, :] <= rows_blk[:, None])
        scores = jnp.where(allowed[None], scores, -1000000000.0)
        top = lax.optimization_barrier(jnp.max(scores, axis=-1, keepdims=True))
        expo = jnp.exp(scores - top)
        probs = expo / lax.optimization_barrier(jnp.sum(expo, axis=-1, keepdims=True))
        return jnp.einsum('hqk,khd->qhd', low(probs), values_all, precision=lax.Precision.HIGHEST)
    starts = jnp.arange(CAP // QB, dtype=jnp.int32) * QB
    attended = lax.map(jax.checkpoint(one_block), starts).reshape(CAP, D)
    attended = low(low_back(attended))
    resid = inputs + low_back(matmul(attended, w_out) + out_shift)
    h_two = low(layer_norm(resid, gain_two, shift_two))
    pre_act = low_back(matmul(h_two, w_up) + up_shift)
    act_low = low(gelu_tanh(pre_act))
    return resid + low_back(matmul(act_low, w_down) + down_shift)

def reference(block_input, ln1_gain, ln1_bias, qkv_weight, qv_bias, out_weight, out_bias, ln2_gain, ln2_bias, up_weight, up_bias, down_weight, down_bias, doc_ids, cotangent):
    params = (ln1_gain.astype(jnp.float32), ln1_bias.astype(jnp.float32), qkv_weight.astype(jnp.float32), qv_bias.astype(jnp.float32), out_weight.astype(jnp.float32), out_bias.astype(jnp.float32), ln2_gain.astype(jnp.float32), ln2_bias.astype(jnp.float32), up_weight.astype(jnp.float32), up_bias.astype(jnp.float32), down_weight.astype(jnp.float32), down_bias.astype(jnp.float32))
    inputs_all = block_input.astype(jnp.float32).reshape(N_FSDP, CAP, D)
    live = (doc_ids >= 0).astype(jnp.float32)
    grads_in = cotangent.astype(jnp.float32).reshape(N_FSDP, CAP, D) * live[:, :, None]

    def step(totals, item):
        inputs, seq_ids, grad_in = item

        def apply_group(weights, values):
            return forward_group(weights, values, seq_ids)
        result, pull = jax.vjp(apply_group, params, inputs)
        grad_params, grad_inputs = pull(grad_in)
        summed = tuple((left + right for left, right in zip(totals, grad_params)))
        return (summed, (result.astype(jnp.bfloat16), grad_inputs))
    start_totals = tuple((jnp.zeros_like(weight) for weight in params))
    totals, (results, input_grads) = lax.scan(step, start_totals, (inputs_all, doc_ids, grads_in))
    return (results.reshape(TOKENS, D), input_grads.reshape(TOKENS, D), totals[0], totals[1], totals[2], totals[3], totals[4], totals[5], totals[6], totals[7], totals[8], totals[9], totals[10], totals[11])
```

```python
import functools

import jax
import jax.numpy as jnp
from jax import lax
from jax.experimental import pallas as pl
from jax.experimental.pallas import tpu as pltpu
from jax.sharding import PartitionSpec as P

HD = 64
FF = 4096


eps = 1e-05


def normalize(values):
    centre = values - jnp.mean(values, axis=-1, keepdims=True)
    spread = jnp.mean(centre * centre, axis=-1, keepdims=True)
    return centre * lax.rsqrt(spread + eps)


def contract_rows(left, right):
    return lax.dot_general(
        left, right, (((0,), (0,)), ((), ())), preferred_element_type=jnp.float32
    )


def contract_cols(left, right):
    return lax.dot_general(
        left, right, (((1,), (1,)), ((), ())), preferred_element_type=jnp.float32
    )


def split_fsdp():
    total = lax.axis_size("fsdp")
    inner = 2 if total <= 8 else 8
    return total // inner, inner


def move_fsdp(values, outer_step, inner_step):
    outer, inner = split_fsdp()
    pairs = [
        (a * inner + b, (a + outer_step) % outer * inner + (b + inner_step) % inner)
        for a in range(outer)
        for b in range(inner)
    ]
    return lax.ppermute(values, "fsdp", pairs)


def move_ctx(values, chip_step, core_step):
    chips = lax.axis_size("ctx") // 2
    pairs = [
        (x * 2 + c, (x + chip_step) % chips * 2 + (c + core_step) % 2)
        for x in range(chips)
        for c in range(2)
    ]
    return lax.ppermute(values, "ctx", pairs)


def put(buffer, values, place, axis):
    return lax.dynamic_update_index_in_dim(buffer, values, place, axis)


def pick(buffer, place, axis):
    return lax.dynamic_index_in_dim(buffer, place, axis, keepdims=False)


def gather_weight(shard):
    outer, inner = split_fsdp()
    place = lax.axis_index("fsdp")
    a, b = place // inner, place % inner
    held = put(jnp.zeros((outer,) + shard.shape, shard.dtype), shard, a, 0)
    for step in range(1, outer):
        held = put(held, move_fsdp(shard, step, 0), (a + outer - step) % outer, 0)
    if inner == 2:
        other = move_fsdp(held, 0, 1)
        first = b == 0
        whole = jnp.stack([jnp.where(first, held, other), jnp.where(first, other, held)], 1)
    else:
        whole = put(jnp.zeros((outer, inner) + shard.shape, shard.dtype), held, b, 1)
        for step in range(1, inner):
            whole = put(whole, move_fsdp(held, 0, step), (b + inner - step) % inner, 1)
    return whole.reshape((outer * inner,) + shard.shape)


def scatter_fsdp(parts, sent_type):
    outer, inner = split_fsdp()
    place = lax.axis_index("fsdp")
    a, b = place // inner, place % inner
    parts = parts.reshape((outer, inner) + parts.shape[1:])
    held = pick(parts, b, 1).astype(jnp.float32)
    for step in range(1, inner):
        sent = pick(parts, (b + step) % inner, 1).astype(sent_type)
        held = held + move_fsdp(sent, 0, step).astype(jnp.float32)
    summed = pick(held, a, 0)
    for step in range(1, outer):
        sent = pick(held, (a + step) % outer, 0).astype(sent_type)
        summed = summed + move_fsdp(sent, step, 0).astype(jnp.float32)
    return summed


def gather_rows(values):
    groups = lax.axis_size("ctx")
    chips = groups // 2
    place = lax.axis_index("ctx")
    x, core = place // 2, place % 2
    whole = jnp.zeros((groups,) + values.shape, values.dtype)
    for step in range(chips):
        got = values if step == 0 else move_ctx(values, step, 0)
        origin = (x + chips - step) % chips * 2
        whole = put(whole, got, origin + core, 0)
        whole = put(whole, move_ctx(got, 0, 1), origin + 1 - core, 0)
    return whole.reshape((groups * values.shape[0],) + values.shape[1:])


def reduce_rows(parts):
    groups = lax.axis_size("ctx")
    chips = groups // 2
    place = lax.axis_index("ctx")
    x, core = place // 2, place % 2
    parts = parts.reshape((chips, 2, parts.shape[0] // groups) + parts.shape[1:])
    sent = pick(parts, 1 - core, 1).astype(jnp.bfloat16)
    held = pick(parts, core, 1).astype(jnp.float32) + move_ctx(sent, 0, 1).astype(jnp.float32)
    summed = pick(held, x, 0)
    for step in range(1, chips):
        sent = pick(held, (x + step) % chips, 0).astype(jnp.bfloat16)
        summed = summed + move_ctx(sent, step, 0).astype(jnp.float32)
    return summed


def sum_ctx(values):
    chips = lax.axis_size("ctx") // 2
    total = values + move_ctx(values, 0, 1)
    whole = total
    for step in range(1, chips):
        whole = whole + move_ctx(total, step, 0)
    return whole


def project(inputs, weight):
    return jnp.dot(inputs, weight, preferred_element_type=jnp.float32)


def project_back(grad_low, weight):
    return contract_cols(grad_low, weight)


def weight_grad(inputs, grad_low):
    shards = lax.axis_size("fsdp")
    full = contract_rows(inputs, grad_low)
    return scatter_fsdp(
        full.reshape(shards, full.shape[0] // shards, full.shape[1]), jnp.bfloat16
    )


BLOCK = 256
MASKED = -1000000000.0


def masked_scores(queries, keys, ids_row_ref, ids_col_ref, start, stop):
    scores = contract_cols(keys, queries)
    same = ids_col_ref[:stop, :] == ids_row_ref[:, start:stop]
    key_place = lax.broadcasted_iota(jnp.int32, scores.shape, 0)
    query_place = lax.broadcasted_iota(jnp.int32, scores.shape, 1) + start
    return jnp.where(same & (key_place <= query_place), scores, MASKED)


def attend_kernel(heads, block, factor, qkv_ref, ids_row_ref, ids_col_ref, out_ref, lse_ref):
    rows = qkv_ref.shape[0]
    width = heads * HD
    for start in range(0, rows, block):
        stop = start + block
        for head in range(heads):
            lo, hi = head * HD, (head + 1) * HD
            queries = qkv_ref[start:stop, lo:hi] * jnp.asarray(factor, jnp.bfloat16)
            keys = qkv_ref[:stop, width + lo : width + hi]
            values = qkv_ref[:stop, 2 * width + lo : 2 * width + hi]
            scores = masked_scores(queries, keys, ids_row_ref, ids_col_ref, start, stop)
            top = jnp.max(scores, axis=0, keepdims=True)
            expo = jnp.exp(scores - top)
            summed = jnp.sum(expo, axis=0, keepdims=True)
            probs_low = (expo * (1.0 / summed)).astype(jnp.bfloat16)
            out_ref[start:stop, lo:hi] = contract_rows(values, probs_low).T.astype(jnp.bfloat16)
            lse_ref[head : head + 1, start:stop] = top + jnp.log(summed)


def attend_back_kernel(
    heads, block, factor, qkv_ref, grad_ref, lse_ref, ids_row_ref, ids_col_ref, out_ref, key_acc, value_acc
):
    rows = qkv_ref.shape[0]
    width = heads * HD
    for head in range(heads):
        lo, hi = head * HD, (head + 1) * HD
        for start in reversed(range(0, rows, block)):
            stop = start + block
            queries = qkv_ref[start:stop, lo:hi] * jnp.asarray(factor, jnp.bfloat16)
            keys = qkv_ref[:stop, width + lo : width + hi]
            values = qkv_ref[:stop, 2 * width + lo : 2 * width + hi]
            grads = grad_ref[start:stop, lo:hi]
            scores = masked_scores(queries, keys, ids_row_ref, ids_col_ref, start, stop)
            probs = jnp.exp(scores - lse_ref[head : head + 1, start:stop])
            grad_probs = contract_cols(values, grads)
            delta = jnp.sum(probs * grad_probs, axis=0, keepdims=True)
            grad_scores = (probs * (grad_probs - delta)).astype(jnp.bfloat16)
            query_grad = contract_rows(keys, grad_scores).T * factor
            out_ref[start:stop, lo:hi] = query_grad.astype(jnp.bfloat16)
            key_grad = jnp.dot(grad_scores, queries, preferred_element_type=jnp.float32)
            value_grad = jnp.dot(
                probs.astype(jnp.bfloat16), grads, preferred_element_type=jnp.float32
            )
            if stop == rows:
                key_acc[...] = key_grad
                value_acc[...] = value_grad
            else:
                key_acc[:stop, :] += key_grad
                value_acc[:stop, :] += value_grad
        out_ref[:, width + lo : width + hi] = key_acc[...].astype(jnp.bfloat16)
        out_ref[:, 2 * width + lo : 2 * width + hi] = value_acc[...].astype(jnp.bfloat16)


def attend(qkv, seq_ids, heads, factor):
    rows = qkv.shape[0]
    block = min(BLOCK, rows)
    return pl.pallas_call(
        functools.partial(attend_kernel, heads, block, factor),
        out_shape=(
            jax.ShapeDtypeStruct((rows, heads * HD), jnp.bfloat16),
            jax.ShapeDtypeStruct((heads, rows), jnp.float32),
        ),
        compiler_params=pltpu.CompilerParams(vmem_limit_bytes=40 * 2**20),
        cost_estimate=pl.CostEstimate(
            flops=4 * rows * rows * 256 * heads,
            bytes_accessed=8 * rows * heads * HD,
            transcendentals=rows * rows * heads,
        ),
        name="attend",
    )(qkv, seq_ids[None, :], seq_ids[:, None])


def attend_back(qkv, grads, log_sums, seq_ids, heads, factor):
    rows = qkv.shape[0]
    block = min(BLOCK, rows)
    return pl.pallas_call(
        functools.partial(attend_back_kernel, heads, block, factor),
        out_shape=jax.ShapeDtypeStruct(qkv.shape, jnp.bfloat16),
        scratch_shapes=[pltpu.VMEM((rows, HD), jnp.float32)] * 2,
        compiler_params=pltpu.CompilerParams(vmem_limit_bytes=40 * 2**20),
        cost_estimate=pl.CostEstimate(
            flops=10 * rows * rows * 256 * heads,
            bytes_accessed=14 * rows * heads * HD,
            transcendentals=rows * rows * heads,
        ),
        name="attend_back",
    )(qkv, grads, log_sums, seq_ids[None, :], seq_ids[:, None])


def mlp_kernel(
    in_ref,
    grad_ref,
    up_ref,
    shift_ref,
    down_ref,
    act_ref,
    pre_ref,
    sums_ref,
    out_ref,
    back_ref,
    out_acc,
    back_acc,
):
    step = pl.program_id(0)
    u = jnp.dot(in_ref[...], up_ref[...], preferred_element_type=jnp.float32) + shift_ref[...]
    square = u * u
    bent = jnp.tanh(0.7978845608028654 * (u * (1.0 + 0.044715 * square)))
    half = 0.5 * (1.0 + bent)
    act = (u * half).astype(jnp.bfloat16)
    act_ref[...] = act
    slope = half + 0.5 * u * (1.0 - bent * bent) * (
        0.7978845608028654 * (1.0 + 0.134145 * square)
    )
    grad_pre = (contract_cols(grad_ref[...], down_ref[...]) * slope).astype(jnp.bfloat16)
    pre_ref[...] = grad_pre
    sums_ref[...] = jnp.sum(grad_pre.astype(jnp.float32), axis=0, keepdims=True)
    out_part = jnp.dot(act, down_ref[...], preferred_element_type=jnp.float32)
    back_part = contract_cols(grad_pre, up_ref[...])

    @pl.when(step == 0)
    def _():
        out_acc[...] = out_part
        back_acc[...] = back_part

    @pl.when(step > 0)
    def _():
        out_acc[...] += out_part
        back_acc[...] += back_part

    @pl.when(step == pl.num_programs(0) - 1)
    def _():
        out_ref[...] = out_acc[...].astype(jnp.bfloat16)
        back_ref[...] = back_acc[...].astype(jnp.bfloat16)


def mlp(inputs, grads, up, shift, down):
    rows, model = inputs.shape
    hidden = up.shape[1]
    block = min(256, hidden)
    whole = pl.BlockSpec((rows, model), lambda i: (0, 0))
    columns = pl.BlockSpec((rows, block), lambda i: (0, i))
    line = pl.BlockSpec((1, block), lambda i: (0, i))
    return pl.pallas_call(
        mlp_kernel,
        grid=(hidden // block,),
        in_specs=[
            whole,
            whole,
            pl.BlockSpec((model, block), lambda i: (0, i)),
            line,
            pl.BlockSpec((block, model), lambda i: (i, 0)),
        ],
        out_specs=(columns, columns, line, whole, whole),
        out_shape=(
            jax.ShapeDtypeStruct((rows, hidden), jnp.bfloat16),
            jax.ShapeDtypeStruct((rows, hidden), jnp.bfloat16),
            jax.ShapeDtypeStruct((1, hidden), jnp.float32),
            jax.ShapeDtypeStruct((rows, model), jnp.bfloat16),
            jax.ShapeDtypeStruct((rows, model), jnp.bfloat16),
        ),
        scratch_shapes=[pltpu.VMEM((rows, model), jnp.float32)] * 2,
        compiler_params=pltpu.CompilerParams(vmem_limit_bytes=52 * 2**20),
        cost_estimate=pl.CostEstimate(
            flops=8 * rows * model * hidden,
            bytes_accessed=8 * rows * model + 4 * rows * hidden + 4 * model * hidden,
            transcendentals=rows * hidden,
        ),
        name="mlp",
    )(inputs, grads, up, shift[None, :], down)


MESH = pl.DeviceIdType.MESH
PLANES = 4


def remote(source, target, sent, landed, device):
    return pltpu.make_async_remote_copy(
        src_ref=source,
        dst_ref=target,
        send_sem=sent,
        recv_sem=landed,
        device_id=device,
        device_id_type=MESH,
    )


def seat():
    place = lax.axis_index("fsdp")
    ctx = lax.axis_index("ctx")
    z, y = place // 2, lax.rem(place, 2)
    x, core = ctx // 2, lax.rem(ctx, 2)
    return place, ctx, z, y, x, core


def centre_of(values):
    centre = values - jnp.mean(values, axis=-1, keepdims=True)
    spread = jnp.mean(centre * centre, axis=-1, keepdims=True)
    return centre * lax.rsqrt(spread + eps)


class RowGather:
    def __init__(self, target, sent, landed):
        self.target, self.sent, self.landed = target, sent, landed
        self.place, self.ctx, z, y, x, core = seat()
        self.mate = self.ctx + 1 - 2 * core
        self.across = self.ctx + 2 - 4 * x
        self.rows = target.shape[0] // 4
        self.sends = []

    def at(self, ctx):
        return self.target.at[pl.ds(pl.multiple_of(ctx * self.rows, self.rows), self.rows), :]

    def move(self, ctx, slot, device):
        return remote(
            self.at(ctx), self.at(ctx), self.sent.at[slot], self.landed.at[slot],
            (self.place, device),
        )

    def send(self, ctx, slot, device):
        copy = self.move(ctx, slot, device)
        copy.start()
        self.sends.append(copy)

    def begin(self):
        self.send(self.ctx, 1, self.across)
        self.send(self.ctx, 0, self.mate)

    def forward(self):
        self.move(self.across, 1, self.across).wait_recv()
        self.send(self.across, 2, self.mate)

    def end(self):
        opposite = self.across + self.mate - self.ctx
        self.move(self.mate, 0, self.mate).wait_recv()
        self.move(opposite, 2, self.mate).wait_recv()
        for copy in self.sends:
            copy.wait_send()


def forward_kernel(
    heads, factor,
    x_ref, cot_ref, live_ref, small_ref, qkvw_ref, outw_ref, upw_ref, downw_ref, ids_row_ref, ids_col_ref,
    up_all, down_all, qkvw_all, outw_all, grad_all, vec_ref, h_one_all, qkv_ref, mixed_ref, lse_ref,
    resid_ref, h_two_all,
    small_all, mate_out, mate_in, kept, cross_out, cross_in,
    zsent, zlanded, ysent, ylanded, local_sem, row_sent, row_landed, red_sent, red_landed,
):
    place, ctx, z, y, x, core = seat()
    flip = place + 1 - 2 * y
    mate = ctx + 1 - 2 * core
    across = ctx + 2 - 4 * x
    rows = x_ref.shape[0]
    width = heads * HD

    barrier = pltpu.get_barrier_semaphore()

    def greet(device):
        pl.semaphore_signal(barrier, inc=1, device_id=device, device_id_type=MESH)

    greet((flip, ctx))
    greet((place, mate))
    greet((place, across))

    @pl.when(z > 0)
    def _():
        greet((place - 2, ctx))

    @pl.when(z < PLANES - 1)
    def _():
        greet((place + 2, ctx))

    pl.semaphore_wait(
        barrier, 3 + (z > 0).astype(jnp.int32) + (z < PLANES - 1).astype(jnp.int32)
    )

    half = upw_ref.shape[0] // 2
    pieces = (
        (small_ref, small_all, 0, small_ref.shape[0]),
        (qkvw_ref, qkvw_all, 0, qkvw_ref.shape[0]),
        (outw_ref, outw_all, 0, outw_ref.shape[0]),
        (upw_ref, up_all, 0, half),
        (downw_ref, down_all, 0, half),
        (upw_ref, up_all, half, half),
        (downw_ref, down_all, half, half),
    )

    def spot(piece, shard):
        source, target, start, count = pieces[piece]
        first = pl.multiple_of(shard * source.shape[0] + start, count)
        return target.at[pl.ds(first, count), :]

    def zcopy(piece, shard, right, hop, source=None):
        slot = (0 if right else 3) + hop - 1
        spot_ = spot(piece, shard)
        device = (place + 2 if right else place - 2, ctx)
        return remote(
            spot_ if source is None else source, spot_, zsent.at[piece, slot], zlanded.at[piece, slot], device
        )

    def ycopy(piece, shard, slot, source=None):
        spot_ = spot(piece, shard)
        return remote(
            spot_ if source is None else source, spot_, ysent.at[piece, slot], ylanded.at[piece, slot],
            (flip, ctx),
        )

    def own(piece):
        source, target, start, count = pieces[piece]
        return source.at[pl.ds(start, count), :]

    def can(right):
        return z < PLANES - 1 if right else z > 0

    def arrived(right, hop):
        return z >= hop if right else z < PLANES - hop

    def local(piece):
        return pltpu.make_async_copy(own(piece), spot(piece, place), local_sem.at[piece])

    def launch(piece):
        for right in (True, False):

            @pl.when(can(right))
            def _():
                zcopy(piece, place, right, 1, own(piece)).start()

        ycopy(piece, place, 6, own(piece)).start()
        local(piece).start()

    def origin(right, hop):
        return place - 2 * hop if right else place + 2 * hop

    def pump(piece, hop):
        for right in (True, False):

            @pl.when(arrived(right, hop))
            def _():
                shard = origin(right, hop)
                zcopy(piece, shard, right, hop).wait_recv()
                if hop < PLANES - 1:

                    @pl.when(can(right))
                    def _():
                        zcopy(piece, shard, right, hop + 1).start()

                ycopy(piece, shard, (0 if right else 3) + hop - 1).start()

    def collect(piece):
        local(piece).wait()
        ycopy(piece, flip, 6).wait_recv()
        for hop in range(1, PLANES):
            for right in (True, False):

                @pl.when(arrived(right, hop))
                def _():
                    shard = origin(right, hop) + flip - place
                    ycopy(piece, shard, (0 if right else 3) + hop - 1).wait_recv()

    def settle(piece):
        ycopy(piece, place, 6, own(piece)).wait_send()
        for hop in range(1, PLANES):
            for right in (True, False):

                @pl.when(arrived(right, hop))
                def _():
                    ycopy(piece, origin(right, hop), (0 if right else 3) + hop - 1).wait_send()

        for hop in range(0, PLANES - 1):
            for right in (True, False):
                have = can(right) if hop == 0 else can(right) & arrived(right, hop)

                @pl.when(have)
                def _():
                    zcopy(piece, origin(right, hop), right, hop + 1).wait_send()

    for piece in (0, 1, 2):
        launch(piece)
    h_one = RowGather(h_one_all, row_sent.at[0], row_landed.at[0])
    h_two = RowGather(h_two_all, row_sent.at[1], row_landed.at[1])
    grads = RowGather(grad_all, row_sent.at[2], row_landed.at[2])
    own_rows = pl.ds(pl.multiple_of(ctx * rows, rows), rows)

    norm_one = centre_of(x_ref[...].astype(jnp.float32))
    for hop in (1, 2, 3):
        pump(0, hop)
    collect(0)
    count = small_ref.shape[0]

    def shard_vectors(shard):
        return small_all[pl.ds(pl.multiple_of(shard * count, count), count), :].astype(jnp.float32)

    vec_ref[...] = jnp.concatenate([shard_vectors(q) for q in range(8)], axis=1)
    low_vec, high_vec = shard_vectors(2 * ctx), shard_vectors(2 * ctx + 1)
    vec_ref[8:9, :] = jnp.concatenate(
        [low_vec[8 + i : 9 + i] for i in range(4)] + [high_vec[8 + i : 9 + i] for i in range(4)], axis=1
    )
    h_one_all[own_rows, :] = (norm_one * vec_ref[0:1, :] + vec_ref[1:2, :]).astype(jnp.bfloat16)
    h_one.begin()
    pump(1, 1)
    pump(2, 1)
    pump(1, 2)
    for piece in (3, 4, 5, 6):
        launch(piece)
    pump(2, 2)
    pump(1, 3)
    pump(2, 3)
    live = (live_ref[...] >= 0).astype(jnp.float32)
    grad_all[own_rows, :] = (cot_ref[...].astype(jnp.float32) * live).astype(jnp.bfloat16)
    pump(3, 1)
    h_one.forward()
    collect(1)
    pump(4, 1)
    h_one.end()
    shift = jnp.concatenate(
        [
            low_vec[2:3], high_vec[2:3], jnp.zeros((1, width), jnp.float32), low_vec[3:4], high_vec[3:4],
        ],
        axis=1,
    )

    @pl.loop(0, 4)
    def _(step):
        some = pl.ds(pl.multiple_of(step * 256, 256), 256)
        qkv_ref[some, :] = (
            jnp.dot(h_one_all[some, :], qkvw_all[...], preferred_element_type=jnp.float32) + shift
        ).astype(jnp.bfloat16)

    def send_mate(side):
        return remote(
            mate_out.at[side], mate_in.at[side], red_sent.at[side], red_landed.at[side], (place, mate)
        )

    send_cross = remote(cross_out, cross_in, red_sent.at[2], red_landed.at[2], (place, across))

    def attend_rows(block):
        start, stop = block * rows, (block + 1) * rows
        for head in range(heads):
            lo, hi = head * HD, (head + 1) * HD
            queries = qkv_ref[start:stop, lo:hi] * jnp.asarray(factor, jnp.bfloat16)
            keys = qkv_ref[:stop, width + lo : width + hi]
            values = qkv_ref[:stop, 2 * width + lo : 2 * width + hi]
            scores = masked_scores(queries, keys, ids_row_ref, ids_col_ref, start, stop)
            top = jnp.max(scores, axis=0, keepdims=True)
            expo = jnp.exp(scores - top)
            summed = jnp.sum(expo, axis=0, keepdims=True)
            probs_low = (expo * (1.0 / summed)).astype(jnp.bfloat16)
            mixed_ref[start:stop, lo:hi] = contract_rows(values, probs_low).T.astype(jnp.bfloat16)
            lse_ref[head : head + 1, start:stop] = top + jnp.log(summed)

    def project_rows(block):
        side, owner_core = block // 2, block % 2
        part = jnp.dot(
            mixed_ref[block * rows : (block + 1) * rows, :], outw_all[...],
            preferred_element_type=jnp.float32,
        )

        @pl.when(core != owner_core)
        def _():
            mate_out[side] = part.astype(jnp.bfloat16)
            send_mate(side).start()

        @pl.when(core == owner_core)
        def _():
            kept[side] = part

    def pass_rows(block):
        side, owner_core = block // 2, block % 2

        @pl.when(core == owner_core)
        def _():
            send_mate(side).wait_recv()
            total = kept[side] + mate_in[side].astype(jnp.float32)

            @pl.when(x == side)
            def _():
                resid_ref[...] = total

            @pl.when(x != side)
            def _():
                cross_out[...] = total.astype(jnp.bfloat16)
                send_cross.start()

    attend_rows(3)
    pump(5, 1)
    pump(6, 1)
    collect(2)
    project_rows(3)
    attend_rows(1)
    project_rows(1)
    pass_rows(3)
    pump(3, 2)
    attend_rows(2)
    project_rows(2)
    pass_rows(1)
    pump(4, 2)
    attend_rows(0)
    project_rows(0)
    pass_rows(2)
    pass_rows(0)
    pump(5, 2)
    send_cross.wait_recv()
    resid = (
        x_ref[...].astype(jnp.float32)
        + (resid_ref[...] + cross_in[...].astype(jnp.float32))
        + vec_ref[4:5, :]
    )
    resid_ref[...] = resid
    h_two_all[own_rows, :] = (centre_of(resid) * vec_ref[5:6, :] + vec_ref[6:7, :]).astype(jnp.bfloat16)
    h_two.begin()
    grads.begin()
    pump(6, 2)
    pump(3, 3)
    pump(4, 3)
    h_two.forward()
    pump(5, 3)
    pump(6, 3)
    grads.forward()
    h_two.end()
    grads.end()
    for piece in (3, 4, 5, 6):
        collect(piece)
    send_cross.wait_send()
    for side in range(2):
        send_mate(side).wait_send()

    for piece in range(7):
        settle(piece)


def forward_pass(block_input, cotangent, own_ids, small, qkv_weight, out_weight, up_weight, down_weight, seq_ids, heads, factor):
    rows, model = block_input.shape
    cap = seq_ids.shape[0]
    width = heads * HD
    hidden = up_weight.shape[1]
    low, wide = jnp.bfloat16, jnp.float32
    anywhere = pl.BlockSpec(memory_space=pl.ANY)
    vmem = pl.BlockSpec(memory_space=pltpu.VMEM)
    shape = jax.ShapeDtypeStruct
    return pl.pallas_call(
        functools.partial(forward_kernel, heads, factor),
        out_shape=(
            shape((model, hidden), low),
            shape((hidden, model), low),
            shape((model, 3 * width), low),
            shape((width, model), low),
            shape((cap, model), low),
            shape((16, model), wide),
            shape((cap, model), low),
            shape((cap, 3 * width), low),
            shape((cap, width), low),
            shape((heads, cap), wide),
            shape((rows, model), wide),
            shape((cap, model), low),
        ),
        in_specs=[vmem] * 3 + [anywhere] * 5 + [vmem] * 2,
        out_specs=(anywhere,) * 2 + (vmem,) * 10,
        scratch_shapes=[
            pltpu.VMEM((8 * 16, 128), low),
            pltpu.VMEM((2, rows, model), low),
            pltpu.VMEM((2, rows, model), low),
            pltpu.VMEM((2, rows, model), wide),
            pltpu.VMEM((rows, model), low),
            pltpu.VMEM((rows, model), low),
            pltpu.SemaphoreType.DMA((7, 6)),
            pltpu.SemaphoreType.DMA((7, 6)),
            pltpu.SemaphoreType.DMA((7, 7)),
            pltpu.SemaphoreType.DMA((7, 7)),
            pltpu.SemaphoreType.DMA((7,)),
            pltpu.SemaphoreType.DMA((3, 3)),
            pltpu.SemaphoreType.DMA((3, 3)),
            pltpu.SemaphoreType.DMA((3,)),
            pltpu.SemaphoreType.DMA((3,)),
        ],
        compiler_params=pltpu.CompilerParams(
            collective_id=1, has_side_effects=True, vmem_limit_bytes=56 * 2**20
        ),
        cost_estimate=pl.CostEstimate(
            flops=2 * cap * model * 4 * width + 4 * cap * cap * width,
            bytes_accessed=32 * 2**20,
            transcendentals=cap * cap * heads,
        ),
        name="forward_pass",
    )(
        block_input, cotangent, own_ids[:, None], small, qkv_weight, out_weight, up_weight, down_weight,
        seq_ids[None, :], seq_ids[:, None],
    )


def on_device_general(
    block_input,
    ln1_gain,
    ln1_bias,
    qkv_weight,
    qv_bias,
    out_weight,
    out_bias,
    ln2_gain,
    ln2_bias,
    up_weight,
    up_bias,
    down_weight,
    down_bias,
    doc_ids,
    cotangent,
):
    shards = lax.axis_size("fsdp")
    small = jnp.concatenate(
        [
            ln1_gain,
            ln1_bias,
            qv_bias[0],
            qv_bias[1],
            out_bias,
            ln2_gain,
            ln2_bias,
            down_bias,
            up_bias,
        ]
    )
    rows = block_input.shape[0]
    model = block_input.shape[1]
    groups = lax.axis_size("ctx")
    place = lax.axis_index("ctx")
    capacity = rows * groups
    width = qkv_weight.shape[2]
    heads_here = width // HD
    hidden_here = up_weight.shape[1]
    factor = 1.0 / HD**0.5
    group_ids = doc_ids[0]
    own_ids = lax.dynamic_slice_in_dim(group_ids, place * rows, rows)
    input_all = gather_rows(block_input)
    qkv_rows = qkv_weight.shape[0]
    small_rows = -(-small.shape[0] // (3 * width * 16)) * 16
    first = jnp.concatenate(
        [
            qkv_weight.reshape(qkv_rows, 3 * width),
            jnp.pad(small, (0, small_rows * 3 * width - small.shape[0])).reshape(
                small_rows, 3 * width
            ),
        ]
    )
    first_all = gather_weight(first)
    small_all = first_all[:, qkv_rows:].reshape(shards, -1)[:, : small.shape[0]]
    piece = model // shards
    gain_one, shift_one, query_shift, value_shift, out_shift, gain_two, shift_two, down_shift = (
        small_all[:, i * piece : (i + 1) * piece].reshape(model) for i in range(8)
    )
    up_shift = small_all[:, 8 * piece :].reshape(-1)
    qv_full = jnp.stack([query_shift, value_shift])
    qkv_flat = first_all[:, :qkv_rows].reshape(model, 3 * width)
    out_full = gather_weight(out_weight).reshape(width, model)
    up_full = gather_weight(up_weight).reshape(model, hidden_here)
    down_full = gather_weight(down_weight).reshape(hidden_here, model)
    cot_all = gather_rows(cotangent)
    qv_here = lax.dynamic_slice_in_dim(qv_full.astype(jnp.float32), place * width, width, 1)
    qkv_shift = jnp.concatenate([qv_here[0], jnp.zeros((width,), jnp.float32), qv_here[1]])
    up_here = lax.dynamic_slice_in_dim(
        up_shift.astype(jnp.float32), place * hidden_here, hidden_here, 0
    )
    input_float = block_input.astype(jnp.float32)
    norm_one_all = normalize(input_all.astype(jnp.float32))
    h_one_all = (norm_one_all * gain_one + shift_one).astype(jnp.bfloat16)
    qkv_proj = project(h_one_all, qkv_flat)
    qkv = (qkv_proj + qkv_shift).astype(jnp.bfloat16)
    mixed_all, log_sums = attend(qkv, group_ids, heads_here, factor)
    out_part = project(mixed_all, out_full)
    resid = input_float + reduce_rows(out_part) + out_shift
    norm_two = normalize(resid)
    h_two = (norm_two * gain_two + shift_two).astype(jnp.bfloat16)
    h_two_all = gather_rows(h_two)
    live = (own_ids >= 0).astype(jnp.float32)
    grad_out = cotangent.astype(jnp.float32) * live[:, None]
    grad_low = grad_out.astype(jnp.bfloat16)
    down_shift_grad = jnp.sum(grad_low.astype(jnp.float32), axis=0)
    grad_all = jnp.where(group_ids[:, None] >= 0, cot_all, jnp.zeros_like(cot_all))
    act_low, grad_pre, up_sums, down_part, back_part = mlp(
        h_two_all, grad_all, up_full, up_here, down_full
    )
    grad_h_two = reduce_rows(back_part)
    output = (resid + reduce_rows(down_part) + down_shift).astype(jnp.bfloat16)
    down_grad = weight_grad(act_low, grad_all)
    up_grad = weight_grad(h_two_all, grad_pre)
    up_sums = up_sums[0]
    up_shift_grad = lax.dynamic_update_slice_in_dim(
        jnp.zeros((FF,), jnp.float32), up_sums, place * hidden_here, 0
    )
    gain_two_grad = jnp.sum(grad_h_two * norm_two, axis=0)
    shift_two_grad = jnp.sum(grad_h_two, axis=0)
    unused_two, norm_back_two = jax.vjp(normalize, resid)
    grad_resid = grad_out + norm_back_two(grad_h_two * gain_two.astype(jnp.float32))[0]
    resid_low = grad_resid.astype(jnp.bfloat16)
    out_shift_grad = jnp.sum(resid_low.astype(jnp.float32), axis=0)
    resid_all = gather_rows(resid_low)
    out_grad = weight_grad(mixed_all, resid_all)
    grad_heads = project_back(resid_all, out_full).astype(jnp.bfloat16)
    grad_qkv = attend_back(qkv, grad_heads, log_sums, group_ids, heads_here, factor)
    qkv_grad = weight_grad(h_one_all, grad_qkv).reshape(qkv_weight.shape[0], 3, width)
    column_sums = jnp.sum(grad_qkv.astype(jnp.float32), axis=0).reshape(3, width)
    qv_local = jnp.stack([column_sums[0], column_sums[2]])
    qv_grad = lax.dynamic_update_slice_in_dim(
        jnp.zeros((2, model), jnp.float32), qv_local, place * width, 1
    )
    grad_h_one_part = project_back(grad_qkv, qkv_flat)
    gain_one_grad = jnp.sum(grad_h_one_part * norm_one_all, axis=0)
    shift_one_grad = jnp.sum(grad_h_one_part, axis=0)
    grad_h_one = reduce_rows(grad_h_one_part)
    unused_one, norm_back_one = jax.vjp(normalize, input_float)
    input_grad = grad_resid + norm_back_one(grad_h_one * gain_one.astype(jnp.float32))[0]
    packed = jnp.concatenate(
        [
            part.reshape(shards, -1)
            for part in (
                gain_one_grad,
                shift_one_grad,
                qv_grad[0],
                qv_grad[1],
                out_shift_grad,
                gain_two_grad,
                shift_two_grad,
                down_shift_grad,
                up_shift_grad,
            )
        ],
        1,
    )
    sums = sum_ctx(scatter_fsdp(packed.reshape(shards, -1, 128), jnp.float32)).reshape(-1)
    (
        gain_one_sum,
        shift_one_sum,
        query_sum,
        value_sum,
        out_shift_sum,
        gain_two_sum,
        shift_two_sum,
        down_shift_sum,
    ) = (sums[i * piece : (i + 1) * piece] for i in range(8))
    qv_sum = jnp.stack([query_sum, value_sum])
    up_shift_sum = sums[8 * piece :]
    return (
        output,
        input_grad,
        gain_one_sum,
        shift_one_sum,
        qkv_grad,
        qv_sum,
        out_grad,
        out_shift_sum,
        gain_two_sum,
        shift_two_sum,
        up_grad,
        up_shift_sum,
        down_grad,
        down_shift_sum,
    )


def on_device(
    block_input,
    ln1_gain,
    ln1_bias,
    qkv_weight,
    qv_bias,
    out_weight,
    out_bias,
    ln2_gain,
    ln2_bias,
    up_weight,
    up_bias,
    down_weight,
    down_bias,
    doc_ids,
    cotangent,
):
    model = block_input.shape[1]
    if lax.axis_size("fsdp") != 8 or lax.axis_size("ctx") != 4:
        return on_device_general(
            block_input, ln1_gain, ln1_bias, qkv_weight, qv_bias, out_weight, out_bias, ln2_gain,
            ln2_bias, up_weight, up_bias, down_weight, down_bias, doc_ids, cotangent,
        )
    shards = lax.axis_size("fsdp")
    rows = block_input.shape[0]
    place = lax.axis_index("ctx")
    width = qkv_weight.shape[2]
    heads_here = width // HD
    hidden_here = up_weight.shape[1]
    piece = model // shards
    factor = 1.0 / HD**0.5
    group_ids = doc_ids[0]
    own_ids = lax.dynamic_slice_in_dim(group_ids, place * rows, rows)
    small = jnp.concatenate(
        [ln1_gain, ln1_bias, qv_bias[0], qv_bias[1], out_bias, ln2_gain, ln2_bias, down_bias, up_bias]
    )
    small = jnp.pad(small, (0, 16 * 128 - small.shape[0])).reshape(16, 128)
    (
        up_full, down_full, qkv_flat, out_full, grad_all, vectors, h_one_all, qkv, mixed_all, log_sums,
        resid, h_two_all,
    ) = forward_pass(
        block_input, cotangent, own_ids, small, qkv_weight.reshape(-1, 3 * width), out_weight, up_weight,
        down_weight, group_ids, heads_here, factor,
    )
    gain_one, gain_two, down_shift, up_here = vectors[0], vectors[5], vectors[7], vectors[8]
    input_float = block_input.astype(jnp.float32)
    norm_one = normalize(input_float)
    norm_two = normalize(resid)
    live = (own_ids >= 0).astype(jnp.float32)
    grad_out = cotangent.astype(jnp.float32) * live[:, None]
    down_shift_grad = jnp.sum(grad_out, axis=0)
    act_low, grad_pre, up_sums, down_part, back_part = mlp(
        h_two_all, grad_all, up_full, up_here, down_full
    )
    grad_h_two = reduce_rows(back_part)
    output = (resid + reduce_rows(down_part) + down_shift).astype(jnp.bfloat16)
    down_grad = weight_grad(act_low, grad_all)
    up_grad = weight_grad(h_two_all, grad_pre)
    up_sums = up_sums[0]
    up_shift_grad = lax.dynamic_update_slice_in_dim(
        jnp.zeros((FF,), jnp.float32), up_sums, place * hidden_here, 0
    )
    gain_two_grad = jnp.sum(grad_h_two * norm_two, axis=0)
    shift_two_grad = jnp.sum(grad_h_two, axis=0)
    unused_two, norm_back_two = jax.vjp(normalize, resid)
    grad_resid = grad_out + norm_back_two(grad_h_two * gain_two.astype(jnp.float32))[0]
    resid_low = grad_resid.astype(jnp.bfloat16)
    out_shift_grad = jnp.sum(resid_low.astype(jnp.float32), axis=0)
    resid_all = gather_rows(resid_low)
    out_grad = weight_grad(mixed_all, resid_all)
    grad_heads = project_back(resid_all, out_full).astype(jnp.bfloat16)
    grad_qkv = attend_back(qkv, grad_heads, log_sums, group_ids, heads_here, factor)
    qkv_grad = weight_grad(h_one_all, grad_qkv).reshape(qkv_weight.shape[0], 3, width)
    column_sums = jnp.sum(grad_qkv.astype(jnp.float32), axis=0).reshape(3, width)
    qv_local = jnp.stack([column_sums[0], column_sums[2]])
    qv_grad = lax.dynamic_update_slice_in_dim(
        jnp.zeros((2, model), jnp.float32), qv_local, place * width, 1
    )
    grad_h_one_part = project_back(grad_qkv, qkv_flat)
    grad_h_one = reduce_rows(grad_h_one_part)
    gain_one_grad = jnp.sum(grad_h_one * norm_one, axis=0)
    shift_one_grad = jnp.sum(grad_h_one, axis=0)
    unused_one, norm_back_one = jax.vjp(normalize, input_float)
    input_grad = grad_resid + norm_back_one(grad_h_one * gain_one.astype(jnp.float32))[0]
    packed = jnp.concatenate(
        [
            part.reshape(shards, -1)
            for part in (
                gain_one_grad,
                shift_one_grad,
                qv_grad[0],
                qv_grad[1],
                out_shift_grad,
                gain_two_grad,
                shift_two_grad,
                down_shift_grad,
                up_shift_grad,
            )
        ],
        1,
    )
    sums = sum_ctx(scatter_fsdp(packed.reshape(shards, -1, 128), jnp.float32)).reshape(-1)
    (
        gain_one_sum,
        shift_one_sum,
        query_sum,
        value_sum,
        out_shift_sum,
        gain_two_sum,
        shift_two_sum,
        down_shift_sum,
    ) = (sums[i * piece : (i + 1) * piece] for i in range(8))
    qv_sum = jnp.stack([query_sum, value_sum])
    up_shift_sum = sums[8 * piece :]
    return (
        output,
        input_grad,
        gain_one_sum,
        shift_one_sum,
        qkv_grad,
        qv_sum,
        out_grad,
        out_shift_sum,
        gain_two_sum,
        shift_two_sum,
        up_grad,
        up_shift_sum,
        down_grad,
        down_shift_sum,
    )


def solution(mesh):
    placed = (
        P(("fsdp", "ctx"), None),
        P("fsdp"),
        P("fsdp"),
        P("fsdp", None, "ctx"),
        P(None, "fsdp"),
        P(("ctx", "fsdp"), None),
        P("fsdp"),
        P("fsdp"),
        P("fsdp"),
        P("fsdp", "ctx"),
        P("fsdp"),
        P(("ctx", "fsdp"), None),
        P("fsdp"),
        P("fsdp", None),
        P(("fsdp", "ctx"), None),
    )
    return jax.shard_map(
        on_device,
        mesh=mesh,
        in_specs=placed,
        out_specs=(
            P(("fsdp", "ctx"), None),
            P(("fsdp", "ctx"), None),
            P("fsdp"),
            P("fsdp"),
            P("fsdp", None, "ctx"),
            P(None, "fsdp"),
            P(("ctx", "fsdp"), None),
            P("fsdp"),
            P("fsdp"),
            P("fsdp"),
            P("fsdp", "ctx"),
            P("fsdp"),
            P(("ctx", "fsdp"), None),
            P("fsdp"),
        ),
        check_vma=False,
    )
```

```python
import functools

import jax
import jax.numpy as jnp
from jax import lax
from jax.experimental import pallas as pl
from jax.experimental.pallas import tpu as pltpu
from jax.sharding import PartitionSpec as P

HD = 64
FF = 4096


eps = 1e-05


def normalize(values):
    centre = values - jnp.mean(values, axis=-1, keepdims=True)
    spread = jnp.mean(centre * centre, axis=-1, keepdims=True)
    return centre * lax.rsqrt(spread + eps)


def contract_rows(left, right):
    return lax.dot_general(
        left, right, (((0,), (0,)), ((), ())), preferred_element_type=jnp.float32
    )


def contract_cols(left, right):
    return lax.dot_general(
        left, right, (((1,), (1,)), ((), ())), preferred_element_type=jnp.float32
    )


def split_fsdp():
    total = lax.axis_size("fsdp")
    inner = 2 if total <= 8 else 8
    return total // inner, inner


def move_fsdp(values, outer_step, inner_step):
    outer, inner = split_fsdp()
    pairs = [
        (a * inner + b, (a + outer_step) % outer * inner + (b + inner_step) % inner)
        for a in range(outer)
        for b in range(inner)
    ]
    return lax.ppermute(values, "fsdp", pairs)


def move_ctx(values, chip_step, core_step):
    chips = lax.axis_size("ctx") // 2
    pairs = [
        (x * 2 + c, (x + chip_step) % chips * 2 + (c + core_step) % 2)
        for x in range(chips)
        for c in range(2)
    ]
    return lax.ppermute(values, "ctx", pairs)


def put(buffer, values, place, axis):
    return lax.dynamic_update_index_in_dim(buffer, values, place, axis)


def pick(buffer, place, axis):
    return lax.dynamic_index_in_dim(buffer, place, axis, keepdims=False)


def gather_weight(shard):
    outer, inner = split_fsdp()
    place = lax.axis_index("fsdp")
    a, b = place // inner, place % inner
    held = put(jnp.zeros((outer,) + shard.shape, shard.dtype), shard, a, 0)
    for step in range(1, outer):
        held = put(held, move_fsdp(shard, step, 0), (a + outer - step) % outer, 0)
    if inner == 2:
        other = move_fsdp(held, 0, 1)
        first = b == 0
        whole = jnp.stack([jnp.where(first, held, other), jnp.where(first, other, held)], 1)
    else:
        whole = put(jnp.zeros((outer, inner) + shard.shape, shard.dtype), held, b, 1)
        for step in range(1, inner):
            whole = put(whole, move_fsdp(held, 0, step), (b + inner - step) % inner, 1)
    return whole.reshape((outer * inner,) + shard.shape)


def scatter_fsdp(parts, sent_type):
    outer, inner = split_fsdp()
    place = lax.axis_index("fsdp")
    a, b = place // inner, place % inner
    parts = parts.reshape((outer, inner) + parts.shape[1:])
    held = pick(parts, b, 1).astype(jnp.float32)
    for step in range(1, inner):
        sent = pick(parts, (b + step) % inner, 1).astype(sent_type)
        held = held + move_fsdp(sent, 0, step).astype(jnp.float32)
    summed = pick(held, a, 0)
    for step in range(1, outer):
        sent = pick(held, (a + step) % outer, 0).astype(sent_type)
        summed = summed + move_fsdp(sent, step, 0).astype(jnp.float32)
    return summed


def gather_rows(values):
    groups = lax.axis_size("ctx")
    chips = groups // 2
    place = lax.axis_index("ctx")
    x, core = place // 2, place % 2
    whole = jnp.zeros((groups,) + values.shape, values.dtype)
    for step in range(chips):
        got = values if step == 0 else move_ctx(values, step, 0)
        origin = (x + chips - step) % chips * 2
        whole = put(whole, got, origin + core, 0)
        whole = put(whole, move_ctx(got, 0, 1), origin + 1 - core, 0)
    return whole.reshape((groups * values.shape[0],) + values.shape[1:])


def reduce_rows(parts):
    groups = lax.axis_size("ctx")
    chips = groups // 2
    place = lax.axis_index("ctx")
    x, core = place // 2, place % 2
    parts = parts.reshape((chips, 2, parts.shape[0] // groups) + parts.shape[1:])
    sent = pick(parts, 1 - core, 1).astype(jnp.bfloat16)
    held = pick(parts, core, 1).astype(jnp.float32) + move_ctx(sent, 0, 1).astype(jnp.float32)
    summed = pick(held, x, 0)
    for step in range(1, chips):
        sent = pick(held, (x + step) % chips, 0).astype(jnp.bfloat16)
        summed = summed + move_ctx(sent, step, 0).astype(jnp.float32)
    return summed


def sum_ctx(values):
    chips = lax.axis_size("ctx") // 2
    total = values + move_ctx(values, 0, 1)
    whole = total
    for step in range(1, chips):
        whole = whole + move_ctx(total, step, 0)
    return whole


def project(inputs, weight):
    return jnp.dot(inputs, weight, preferred_element_type=jnp.float32)


def project_back(grad_low, weight):
    return contract_cols(grad_low, weight)


def weight_grad(inputs, grad_low):
    shards = lax.axis_size("fsdp")
    full = contract_rows(inputs, grad_low)
    return scatter_fsdp(
        full.reshape(shards, full.shape[0] // shards, full.shape[1]), jnp.bfloat16
    )


BLOCK = 256
MASKED = -1000000000.0


def masked_scores(queries, keys, ids_row_ref, ids_col_ref, start, stop):
    scores = contract_cols(keys, queries)
    same = ids_col_ref[:stop, :] == ids_row_ref[:, start:stop]
    key_place = lax.broadcasted_iota(jnp.int32, scores.shape, 0)
    query_place = lax.broadcasted_iota(jnp.int32, scores.shape, 1) + start
    return jnp.where(same & (key_place <= query_place), scores, MASKED)


def attend_kernel(heads, block, factor, qkv_ref, ids_row_ref, ids_col_ref, out_ref, lse_ref):
    rows = qkv_ref.shape[0]
    width = heads * HD
    for start in range(0, rows, block):
        stop = start + block
        for head in range(heads):
            lo, hi = head * HD, (head + 1) * HD
            queries = qkv_ref[start:stop, lo:hi] * jnp.asarray(factor, jnp.bfloat16)
            keys = qkv_ref[:stop, width + lo : width + hi]
            values = qkv_ref[:stop, 2 * width + lo : 2 * width + hi]
            scores = masked_scores(queries, keys, ids_row_ref, ids_col_ref, start, stop)
            top = jnp.max(scores, axis=0, keepdims=True)
            expo = jnp.exp(scores - top)
            summed = jnp.sum(expo, axis=0, keepdims=True)
            probs_low = (expo * (1.0 / summed)).astype(jnp.bfloat16)
            out_ref[start:stop, lo:hi] = contract_rows(values, probs_low).T.astype(jnp.bfloat16)
            lse_ref[head : head + 1, start:stop] = top + jnp.log(summed)


def attend_back_kernel(
    heads, block, factor, qkv_ref, grad_ref, lse_ref, ids_row_ref, ids_col_ref, out_ref, key_acc, value_acc
):
    rows = qkv_ref.shape[0]
    width = heads * HD
    for head in range(heads):
        lo, hi = head * HD, (head + 1) * HD
        for start in reversed(range(0, rows, block)):
            stop = start + block
            queries = qkv_ref[start:stop, lo:hi] * jnp.asarray(factor, jnp.bfloat16)
            keys = qkv_ref[:stop, width + lo : width + hi]
            values = qkv_ref[:stop, 2 * width + lo : 2 * width + hi]
            grads = grad_ref[start:stop, lo:hi]
            scores = masked_scores(queries, keys, ids_row_ref, ids_col_ref, start, stop)
            probs = jnp.exp(scores - lse_ref[head : head + 1, start:stop])
            grad_probs = contract_cols(values, grads)
            delta = jnp.sum(probs * grad_probs, axis=0, keepdims=True)
            grad_scores = (probs * (grad_probs - delta)).astype(jnp.bfloat16)
            query_grad = contract_rows(keys, grad_scores).T * factor
            out_ref[start:stop, lo:hi] = query_grad.astype(jnp.bfloat16)
            key_grad = jnp.dot(grad_scores, queries, preferred_element_type=jnp.float32)
            value_grad = jnp.dot(
                probs.astype(jnp.bfloat16), grads, preferred_element_type=jnp.float32
            )
            if stop == rows:
                key_acc[...] = key_grad
                value_acc[...] = value_grad
            else:
                key_acc[:stop, :] += key_grad
                value_acc[:stop, :] += value_grad
        out_ref[:, width + lo : width + hi] = key_acc[...].astype(jnp.bfloat16)
        out_ref[:, 2 * width + lo : 2 * width + hi] = value_acc[...].astype(jnp.bfloat16)


def attend(qkv, seq_ids, heads, factor):
    rows = qkv.shape[0]
    block = min(BLOCK, rows)
    return pl.pallas_call(
        functools.partial(attend_kernel, heads, block, factor),
        out_shape=(
            jax.ShapeDtypeStruct((rows, heads * HD), jnp.bfloat16),
            jax.ShapeDtypeStruct((heads, rows), jnp.float32),
        ),
        compiler_params=pltpu.CompilerParams(vmem_limit_bytes=40 * 2**20),
        cost_estimate=pl.CostEstimate(
            flops=4 * rows * rows * 256 * heads,
            bytes_accessed=8 * rows * heads * HD,
            transcendentals=rows * rows * heads,
        ),
        name="attend",
    )(qkv, seq_ids[None, :], seq_ids[:, None])


def attend_back(qkv, grads, log_sums, seq_ids, heads, factor):
    rows = qkv.shape[0]
    block = min(BLOCK, rows)
    return pl.pallas_call(
        functools.partial(attend_back_kernel, heads, block, factor),
        out_shape=jax.ShapeDtypeStruct(qkv.shape, jnp.bfloat16),
        scratch_shapes=[pltpu.VMEM((rows, HD), jnp.float32)] * 2,
        compiler_params=pltpu.CompilerParams(vmem_limit_bytes=40 * 2**20),
        cost_estimate=pl.CostEstimate(
            flops=10 * rows * rows * 256 * heads,
            bytes_accessed=14 * rows * heads * HD,
            transcendentals=rows * rows * heads,
        ),
        name="attend_back",
    )(qkv, grads, log_sums, seq_ids[None, :], seq_ids[:, None])


def mlp_kernel(
    in_ref,
    grad_ref,
    up_ref,
    shift_ref,
    down_ref,
    act_ref,
    pre_ref,
    sums_ref,
    out_ref,
    back_ref,
    out_acc,
    back_acc,
):
    step = pl.program_id(0)
    u = jnp.dot(in_ref[...], up_ref[...], preferred_element_type=jnp.float32) + shift_ref[...]
    square = u * u
    bent = jnp.tanh(0.7978845608028654 * (u * (1.0 + 0.044715 * square)))
    half = 0.5 * (1.0 + bent)
    act = (u * half).astype(jnp.bfloat16)
    act_ref[...] = act
    slope = half + 0.5 * u * (1.0 - bent * bent) * (
        0.7978845608028654 * (1.0 + 0.134145 * square)
    )
    grad_pre = (contract_cols(grad_ref[...], down_ref[...]) * slope).astype(jnp.bfloat16)
    pre_ref[...] = grad_pre
    sums_ref[...] = jnp.sum(grad_pre.astype(jnp.float32), axis=0, keepdims=True)
    out_part = jnp.dot(act, down_ref[...], preferred_element_type=jnp.float32)
    back_part = contract_cols(grad_pre, up_ref[...])

    @pl.when(step == 0)
    def _():
        out_acc[...] = out_part
        back_acc[...] = back_part

    @pl.when(step > 0)
    def _():
        out_acc[...] += out_part
        back_acc[...] += back_part

    @pl.when(step == pl.num_programs(0) - 1)
    def _():
        out_ref[...] = out_acc[...].astype(jnp.bfloat16)
        back_ref[...] = back_acc[...].astype(jnp.bfloat16)


def mlp(inputs, grads, up, shift, down):
    rows, model = inputs.shape
    hidden = up.shape[1]
    block = min(256, hidden)
    whole = pl.BlockSpec((rows, model), lambda i: (0, 0))
    columns = pl.BlockSpec((rows, block), lambda i: (0, i))
    line = pl.BlockSpec((1, block), lambda i: (0, i))
    return pl.pallas_call(
        mlp_kernel,
        grid=(hidden // block,),
        in_specs=[
            whole,
            whole,
            pl.BlockSpec((model, block), lambda i: (0, i)),
            line,
            pl.BlockSpec((block, model), lambda i: (i, 0)),
        ],
        out_specs=(columns, columns, line, whole, whole),
        out_shape=(
            jax.ShapeDtypeStruct((rows, hidden), jnp.bfloat16),
            jax.ShapeDtypeStruct((rows, hidden), jnp.bfloat16),
            jax.ShapeDtypeStruct((1, hidden), jnp.float32),
            jax.ShapeDtypeStruct((rows, model), jnp.bfloat16),
            jax.ShapeDtypeStruct((rows, model), jnp.bfloat16),
        ),
        scratch_shapes=[pltpu.VMEM((rows, model), jnp.float32)] * 2,
        compiler_params=pltpu.CompilerParams(vmem_limit_bytes=52 * 2**20),
        cost_estimate=pl.CostEstimate(
            flops=8 * rows * model * hidden,
            bytes_accessed=8 * rows * model + 4 * rows * hidden + 4 * model * hidden,
            transcendentals=rows * hidden,
        ),
        name="mlp",
    )(inputs, grads, up, shift[None, :], down)


MESH = pl.DeviceIdType.MESH
PLANES = 4


def remote(source, target, sent, landed, device):
    return pltpu.make_async_remote_copy(
        src_ref=source,
        dst_ref=target,
        send_sem=sent,
        recv_sem=landed,
        device_id=device,
        device_id_type=MESH,
    )


def seat():
    place = lax.axis_index("fsdp")
    ctx = lax.axis_index("ctx")
    z, y = place // 2, lax.rem(place, 2)
    x, core = ctx // 2, lax.rem(ctx, 2)
    return place, ctx, z, y, x, core


def centre_of(values):
    centre = values - jnp.mean(values, axis=-1, keepdims=True)
    spread = jnp.mean(centre * centre, axis=-1, keepdims=True)
    return centre * lax.rsqrt(spread + eps)


class RowGather:
    def __init__(self, target, sent, landed):
        self.target, self.sent, self.landed = target, sent, landed
        self.place, self.ctx, z, y, x, core = seat()
        self.mate = self.ctx + 1 - 2 * core
        self.across = self.ctx + 2 - 4 * x
        self.rows = target.shape[0] // 4
        self.sends = []

    def at(self, ctx):
        return self.target.at[pl.ds(pl.multiple_of(ctx * self.rows, self.rows), self.rows), :]

    def move(self, ctx, slot, device):
        return remote(
            self.at(ctx), self.at(ctx), self.sent.at[slot], self.landed.at[slot],
            (self.place, device),
        )

    def send(self, ctx, slot, device):
        copy = self.move(ctx, slot, device)
        copy.start()
        self.sends.append(copy)

    def begin(self):
        self.send(self.ctx, 1, self.across)
        self.send(self.ctx, 0, self.mate)

    def forward(self):
        self.move(self.across, 1, self.across).wait_recv()
        self.send(self.across, 2, self.mate)

    def end(self):
        opposite = self.across + self.mate - self.ctx
        self.move(self.mate, 0, self.mate).wait_recv()
        self.move(opposite, 2, self.mate).wait_recv()
        for copy in self.sends:
            copy.wait_send()


def forward_kernel(
    heads, factor,
    x_ref, cot_ref, live_ref, small_ref, qkvw_ref, outw_ref, upw_ref, downw_ref, ids_row_ref, ids_col_ref,
    up_all, down_all, qkvw_all, outw_all, grad_all, vec_ref, h_one_all, qkv_ref, mixed_ref, lse_ref,
    resid_ref, h_two_all,
    small_all, mate_out, mate_in, kept, cross_out, cross_in,
    zsent, zlanded, ysent, ylanded, local_sem, row_sent, row_landed, red_sent, red_landed,
):
    place, ctx, z, y, x, core = seat()
    flip = place + 1 - 2 * y
    mate = ctx + 1 - 2 * core
    across = ctx + 2 - 4 * x
    rows = x_ref.shape[0]
    width = heads * HD

    barrier = pltpu.get_barrier_semaphore()

    def greet(device):
        pl.semaphore_signal(barrier, inc=1, device_id=device, device_id_type=MESH)

    greet((flip, ctx))
    greet((place, mate))
    greet((place, across))

    @pl.when(z > 0)
    def _():
        greet((place - 2, ctx))

    @pl.when(z < PLANES - 1)
    def _():
        greet((place + 2, ctx))

    pl.semaphore_wait(
        barrier, 3 + (z > 0).astype(jnp.int32) + (z < PLANES - 1).astype(jnp.int32)
    )

    half = upw_ref.shape[0] // 2
    pieces = (
        (small_ref, small_all, 0, small_ref.shape[0]),
        (qkvw_ref, qkvw_all, 0, qkvw_ref.shape[0]),
        (outw_ref, outw_all, 0, outw_ref.shape[0]),
        (upw_ref, up_all, 0, half),
        (downw_ref, down_all, 0, half),
        (upw_ref, up_all, half, half),
        (downw_ref, down_all, half, half),
    )

    def spot(piece, shard):
        source, target, start, count = pieces[piece]
        first = pl.multiple_of(shard * source.shape[0] + start, count)
        return target.at[pl.ds(first, count), :]

    def zcopy(piece, shard, right, hop, source=None):
        slot = (0 if right else 3) + hop - 1
        spot_ = spot(piece, shard)
        device = (place + 2 if right else place - 2, ctx)
        return remote(
            spot_ if source is None else source, spot_, zsent.at[piece, slot], zlanded.at[piece, slot], device
        )

    def ycopy(piece, shard, slot, source=None):
        spot_ = spot(piece, shard)
        return remote(
            spot_ if source is None else source, spot_, ysent.at[piece, slot], ylanded.at[piece, slot],
            (flip, ctx),
        )

    def own(piece):
        source, target, start, count = pieces[piece]
        return source.at[pl.ds(start, count), :]

    def can(right):
        return z < PLANES - 1 if right else z > 0

    def arrived(right, hop):
        return z >= hop if right else z < PLANES - hop

    def local(piece):
        return pltpu.make_async_copy(own(piece), spot(piece, place), local_sem.at[piece])

    def launch(piece):
        for right in (True, False):

            @pl.when(can(right))
            def _():
                zcopy(piece, place, right, 1, own(piece)).start()

        ycopy(piece, place, 6, own(piece)).start()
        local(piece).start()

    def origin(right, hop):
        return place - 2 * hop if right else place + 2 * hop

    def pump(piece, hop):
        for right in (True, False):

            @pl.when(arrived(right, hop))
            def _():
                shard = origin(right, hop)
                zcopy(piece, shard, right, hop).wait_recv()
                if hop < PLANES - 1:

                    @pl.when(can(right))
                    def _():
                        zcopy(piece, shard, right, hop + 1).start()

                ycopy(piece, shard, (0 if right else 3) + hop - 1).start()

    def collect(piece):
        local(piece).wait()
        ycopy(piece, flip, 6).wait_recv()
        for hop in range(1, PLANES):
            for right in (True, False):

                @pl.when(arrived(right, hop))
                def _():
                    shard = origin(right, hop) + flip - place
                    ycopy(piece, shard, (0 if right else 3) + hop - 1).wait_recv()

    def settle(piece):
        ycopy(piece, place, 6, own(piece)).wait_send()
        for hop in range(1, PLANES):
            for right in (True, False):

                @pl.when(arrived(right, hop))
                def _():
                    ycopy(piece, origin(right, hop), (0 if right else 3) + hop - 1).wait_send()

        for hop in range(0, PLANES - 1):
            for right in (True, False):
                have = can(right) if hop == 0 else can(right) & arrived(right, hop)

                @pl.when(have)
                def _():
                    zcopy(piece, origin(right, hop), right, hop + 1).wait_send()

    for piece in (0, 1, 2):
        launch(piece)
    h_one = RowGather(h_one_all, row_sent.at[0], row_landed.at[0])
    h_two = RowGather(h_two_all, row_sent.at[1], row_landed.at[1])
    grads = RowGather(grad_all, row_sent.at[2], row_landed.at[2])
    own_rows = pl.ds(pl.multiple_of(ctx * rows, rows), rows)

    norm_one = centre_of(x_ref[...].astype(jnp.float32))
    for hop in (1, 2, 3):
        pump(0, hop)
    collect(0)
    count = small_ref.shape[0]

    def shard_vectors(shard):
        return small_all[pl.ds(pl.multiple_of(shard * count, count), count), :].astype(jnp.float32)

    vec_ref[...] = jnp.concatenate([shard_vectors(q) for q in range(8)], axis=1)
    low_vec, high_vec = shard_vectors(2 * ctx), shard_vectors(2 * ctx + 1)
    vec_ref[8:9, :] = jnp.concatenate(
        [low_vec[8 + i : 9 + i] for i in range(4)] + [high_vec[8 + i : 9 + i] for i in range(4)], axis=1
    )
    h_one_all[own_rows, :] = (norm_one * vec_ref[0:1, :] + vec_ref[1:2, :]).astype(jnp.bfloat16)
    h_one.begin()
    pump(1, 1)
    pump(2, 1)
    pump(1, 2)
    for piece in (3, 4, 5, 6):
        launch(piece)
    pump(2, 2)
    pump(1, 3)
    pump(2, 3)
    live = (live_ref[...] >= 0).astype(jnp.float32)
    grad_all[own_rows, :] = (cot_ref[...].astype(jnp.float32) * live).astype(jnp.bfloat16)
    pump(3, 1)
    h_one.forward()
    collect(1)
    pump(4, 1)
    h_one.end()
    shift = jnp.concatenate(
        [
            low_vec[2:3], high_vec[2:3], jnp.zeros((1, width), jnp.float32), low_vec[3:4], high_vec[3:4],
        ],
        axis=1,
    )

    @pl.loop(0, 4)
    def _(step):
        some = pl.ds(pl.multiple_of(step * 256, 256), 256)
        qkv_ref[some, :] = (
            jnp.dot(h_one_all[some, :], qkvw_all[...], preferred_element_type=jnp.float32) + shift
        ).astype(jnp.bfloat16)

    def send_mate(side):
        return remote(
            mate_out.at[side], mate_in.at[side], red_sent.at[side], red_landed.at[side], (place, mate)
        )

    send_cross = remote(cross_out, cross_in, red_sent.at[2], red_landed.at[2], (place, across))

    def attend_rows(block):
        start, stop = block * rows, (block + 1) * rows
        for head in range(heads):
            lo, hi = head * HD, (head + 1) * HD
            queries = qkv_ref[start:stop, lo:hi] * jnp.asarray(factor, jnp.bfloat16)
            keys = qkv_ref[:stop, width + lo : width + hi]
            values = qkv_ref[:stop, 2 * width + lo : 2 * width + hi]
            scores = masked_scores(queries, keys, ids_row_ref, ids_col_ref, start, stop)
            top = jnp.max(scores, axis=0, keepdims=True)
            expo = jnp.exp(scores - top)
            summed = jnp.sum(expo, axis=0, keepdims=True)
            probs_low = (expo * (1.0 / summed)).astype(jnp.bfloat16)
            mixed_ref[start:stop, lo:hi] = contract_rows(values, probs_low).T.astype(jnp.bfloat16)
            lse_ref[head : head + 1, start:stop] = top + jnp.log(summed)

    def project_rows(block):
        side, owner_core = block // 2, block % 2
        part = jnp.dot(
            mixed_ref[block * rows : (block + 1) * rows, :], outw_all[...],
            preferred_element_type=jnp.float32,
        )

        @pl.when(core != owner_core)
        def _():
            mate_out[side] = part.astype(jnp.bfloat16)
            send_mate(side).start()

        @pl.when(core == owner_core)
        def _():
            kept[side] = part

    def pass_rows(block):
        side, owner_core = block // 2, block % 2

        @pl.when(core == owner_core)
        def _():
            send_mate(side).wait_recv()
            total = kept[side] + mate_in[side].astype(jnp.float32)

            @pl.when(x == side)
            def _():
                resid_ref[...] = total

            @pl.when(x != side)
            def _():
                cross_out[...] = total.astype(jnp.bfloat16)
                send_cross.start()

    attend_rows(3)
    pump(5, 1)
    pump(6, 1)
    collect(2)
    project_rows(3)
    attend_rows(1)
    project_rows(1)
    pass_rows(3)
    pump(3, 2)
    attend_rows(2)
    project_rows(2)
    pass_rows(1)
    pump(4, 2)
    attend_rows(0)
    project_rows(0)
    pass_rows(2)
    pass_rows(0)
    pump(5, 2)
    send_cross.wait_recv()
    resid = (
        x_ref[...].astype(jnp.float32)
        + (resid_ref[...] + cross_in[...].astype(jnp.float32))
        + vec_ref[4:5, :]
    )
    resid_ref[...] = resid
    h_two_all[own_rows, :] = (centre_of(resid) * vec_ref[5:6, :] + vec_ref[6:7, :]).astype(jnp.bfloat16)
    h_two.begin()
    grads.begin()
    pump(6, 2)
    pump(3, 3)
    pump(4, 3)
    h_two.forward()
    pump(5, 3)
    pump(6, 3)
    grads.forward()
    h_two.end()
    grads.end()
    for piece in (3, 4, 5, 6):
        collect(piece)
    send_cross.wait_send()
    for side in range(2):
        send_mate(side).wait_send()

    for piece in range(7):
        settle(piece)


def forward_pass(block_input, cotangent, own_ids, small, qkv_weight, out_weight, up_weight, down_weight, seq_ids, heads, factor):
    rows, model = block_input.shape
    cap = seq_ids.shape[0]
    width = heads * HD
    hidden = up_weight.shape[1]
    low, wide = jnp.bfloat16, jnp.float32
    anywhere = pl.BlockSpec(memory_space=pl.ANY)
    vmem = pl.BlockSpec(memory_space=pltpu.VMEM)
    shape = jax.ShapeDtypeStruct
    return pl.pallas_call(
        functools.partial(forward_kernel, heads, factor),
        out_shape=(
            shape((model, hidden), low),
            shape((hidden, model), low),
            shape((model, 3 * width), low),
            shape((width, model), low),
            shape((cap, model), low),
            shape((16, model), wide),
            shape((cap, model), low),
            shape((cap, 3 * width), low),
            shape((cap, width), low),
            shape((heads, cap), wide),
            shape((rows, model), wide),
            shape((cap, model), low),
        ),
        in_specs=[vmem] * 3 + [anywhere] * 5 + [vmem] * 2,
        out_specs=(anywhere,) * 2 + (vmem,) * 10,
        scratch_shapes=[
            pltpu.VMEM((8 * 16, 128), low),
            pltpu.VMEM((2, rows, model), low),
            pltpu.VMEM((2, rows, model), low),
            pltpu.VMEM((2, rows, model), wide),
            pltpu.VMEM((rows, model), low),
            pltpu.VMEM((rows, model), low),
            pltpu.SemaphoreType.DMA((7, 6)),
            pltpu.SemaphoreType.DMA((7, 6)),
            pltpu.SemaphoreType.DMA((7, 7)),
            pltpu.SemaphoreType.DMA((7, 7)),
            pltpu.SemaphoreType.DMA((7,)),
            pltpu.SemaphoreType.DMA((3, 3)),
            pltpu.SemaphoreType.DMA((3, 3)),
            pltpu.SemaphoreType.DMA((3,)),
            pltpu.SemaphoreType.DMA((3,)),
        ],
        compiler_params=pltpu.CompilerParams(
            collective_id=1, has_side_effects=True, vmem_limit_bytes=56 * 2**20
        ),
        cost_estimate=pl.CostEstimate(
            flops=2 * cap * model * 4 * width + 4 * cap * cap * width,
            bytes_accessed=32 * 2**20,
            transcendentals=cap * cap * heads,
        ),
        name="forward_pass",
    )(
        block_input, cotangent, own_ids[:, None], small, qkv_weight, out_weight, up_weight, down_weight,
        seq_ids[None, :], seq_ids[:, None],
    )


CHUNK = 512


class RowReduce:
    def __init__(self, total, mate_out, mate_in, cross_out, cross_in, sent, landed):
        self.total, self.mate_out, self.mate_in = total, mate_out, mate_in
        self.cross_out, self.cross_in, self.sent, self.landed = cross_out, cross_in, sent, landed
        self.place, self.ctx, z, y, self.x, self.core = seat()
        self.rows = total.shape[0] // 4

    def part(self, side, core):
        first = pl.multiple_of((side * 2 + core) * self.rows, self.rows)
        return self.total[pl.ds(first, self.rows), :]

    def mate_copy(self, slot):
        return remote(
            self.mate_out.at[slot], self.mate_in.at[slot], self.sent.at[slot], self.landed.at[slot],
            (self.place, self.ctx + 1 - 2 * self.core),
        )

    def cross_copy(self):
        return remote(
            self.cross_out, self.cross_in, self.sent.at[2], self.landed.at[2],
            (self.place, self.ctx + 2 - 4 * self.x),
        )

    def begin(self):
        for slot, side in ((0, 1 - self.x), (1, self.x)):
            self.mate_out[slot] = self.part(side, 1 - self.core).astype(jnp.bfloat16)
            self.mate_copy(slot).start()

    def relay(self):
        self.mate_copy(0).wait_recv()
        self.cross_out[...] = (
            self.part(1 - self.x, self.core) + self.mate_in[0].astype(jnp.float32)
        ).astype(jnp.bfloat16)
        self.cross_copy().start()

    def finish(self):
        self.mate_copy(1).wait_recv()
        held = self.part(self.x, self.core) + self.mate_in[1].astype(jnp.float32)
        self.cross_copy().wait_recv()
        return held + self.cross_in[...].astype(jnp.float32)

    def settle(self):
        for slot in range(2):
            self.mate_copy(slot).wait_send()
        self.cross_copy().wait_send()


class Scatter:
    def __init__(self, keep, out, yin, zin, sent, landed):
        self.keep, self.yout, self.yin, self.zout, self.zin = keep, out, yin, out, zin
        self.sent, self.landed = sent, landed
        self.place, self.ctx, self.z, self.y, x, core = seat()

    def store(self, plane, even, odd):
        first = self.y == 0
        self.keep[plane] = jnp.where(first, even, odd)
        self.yout[plane] = jnp.where(first, odd, even).astype(jnp.bfloat16)

    def ycopy(self):
        return remote(
            self.yout, self.yin, self.sent.at[0], self.landed.at[0], (self.place + 1 - 2 * self.y, self.ctx)
        )

    def zcopy(self, step):
        return remote(
            self.zout.at[step - 1], self.zin.at[step - 1], self.sent.at[step], self.landed.at[step],
            (lax.rem(self.z + step, PLANES) * 2 + self.y, self.ctx),
        )

    def begin(self):
        self.ycopy().start()

    def relay(self):
        self.ycopy().wait()
        for step in (2, 1, 3):
            plane = lax.rem(self.z + step, PLANES)
            self.zout[step - 1] = (self.keep[plane] + self.yin[plane].astype(jnp.float32)).astype(
                jnp.bfloat16
            )
            self.zcopy(step).start()

    def finish(self):
        total = self.keep[self.z] + self.yin[self.z].astype(jnp.float32)
        for step in (1, 3, 2):
            self.zcopy(step).wait_recv()
            total = total + self.zin[step - 1].astype(jnp.float32)
        return total

    def settle(self):
        for step in (1, 2, 3):
            self.zcopy(step).wait_send()


class PlaneScatter:
    def __init__(self, keep, out, yin, zin, sent, landed, zlanded):
        self.keep, self.yout, self.yin, self.zout, self.zin = keep, out, yin, out, zin
        self.sent, self.landed, self.zlanded = sent, landed, zlanded
        self.place, self.ctx, self.z, self.y, x, core = seat()

    def store(self, block, even, odd):
        first = self.y == 0
        self.keep[block] = jnp.where(first, even, odd)
        self.yout[block] = jnp.where(first, odd, even).astype(jnp.bfloat16)

    def ycopy(self, block):
        return remote(
            self.yout.at[block], self.yin.at[block], self.sent.at[0, block], self.landed.at[block],
            (self.place + 1 - 2 * self.y, self.ctx),
        )

    def zcopy(self, block):
        slot = lax.rem(self.z - block + PLANES, PLANES) - 1
        return remote(
            self.zout.at[block], self.zin.at[slot], self.sent.at[1, block], self.zlanded.at[slot],
            (block * 2 + self.y, self.ctx),
        )

    def begin(self, block):
        self.ycopy(block).start()

    def relay(self, block):
        self.ycopy(block).wait()

        @pl.when(self.z != block)
        def _():
            self.zout[block] = (self.keep[block] + self.yin[block].astype(jnp.float32)).astype(jnp.bfloat16)
            self.zcopy(block).start()

    def finish(self):
        total = self.keep[self.z] + self.yin[self.z].astype(jnp.float32)
        for slot in range(3):
            remote(
                self.zin.at[slot], self.zin.at[slot], self.sent.at[1, 0], self.zlanded.at[slot],
                (self.place + 1 - 2 * self.y, self.ctx),
            ).wait_recv()
            total = total + self.zin[slot].astype(jnp.float32)
        return total

    def settle(self):
        for block in range(PLANES):

            @pl.when(self.z != block)
            def _():
                self.zcopy(block).wait_send()


def norm_back(values, grads):
    centre = values - jnp.mean(values, axis=-1, keepdims=True)
    scale = lax.rsqrt(jnp.mean(centre * centre, axis=-1, keepdims=True) + eps)
    unit = centre * scale
    along = jnp.mean(grads * unit, axis=-1, keepdims=True)
    return (grads - jnp.mean(grads, axis=-1, keepdims=True) - unit * along) * scale


def backward_kernel(
    heads, factor,
    h_two_ref, grad_ref, up_ref, down_ref, vec_ref, resid_ref, x_ref, cot_ref, live_ref, lse_ref,
    ids_row_ref, ids_col_ref, qkv_any, mixed_any, h_one_any, qkvw_any, outw_any,
    output_ref, input_grad_ref, qkv_grad_ref, out_grad_ref, up_grad_ref, down_grad_ref, sums_ref,
    qkv_ref, mixed_ref, h_one_ref, qkvw_ref, outw_ref, out_acc, back_acc, up_sums, resid_all,
    grad_heads, grad_qkv, key_acc, value_acc, act_ref, grad_pre_ref,
    mate_out, mate_in, cross_out, cross_in,
    up_keep, up_out, up_yin, up_zin, down_keep, down_out, down_yin, down_zin,
    out_keep, out_out, out_yin, out_zin, qkv_keep, qkv_out, qkv_yin, qkv_zin,
    vec_out, vec_in, vec_ctx,
    load_sem, red_sent, red_landed, up_sent, up_landed, down_sent, down_landed, down_zlanded, out_sent,
    out_landed, qkv_sent, qkv_landed, row_sent, row_landed, vec_sent, vec_landed, ctx_sent, ctx_landed,
):
    place, ctx, z, y, x, core = seat()
    rows = x_ref.shape[0]
    cap = h_two_ref.shape[0]
    width = heads * HD
    loads = [
        pltpu.make_async_copy(source, target, load_sem.at[i])
        for i, (source, target) in enumerate(
            (
                (qkv_any, qkv_ref), (mixed_any, mixed_ref), (h_one_any, h_one_ref), (qkvw_any, qkvw_ref),
                (outw_any, outw_ref),
            )
        )
    ]
    for load in loads:
        load.start()
    out_acc[...] = jnp.zeros_like(out_acc)
    back_acc[...] = jnp.zeros_like(back_acc)
    barrier = pltpu.get_barrier_semaphore()
    for step in range(1, 8):
        pl.semaphore_signal(
            barrier, inc=1, device_id=(lax.rem(place + step, 8), ctx), device_id_type=MESH
        )
    for step in range(1, 4):
        pl.semaphore_signal(
            barrier, inc=1, device_id=(place, lax.rem(ctx + step, 4)), device_id_type=MESH
        )
    pl.semaphore_wait(barrier, 10)

    down_scatter = PlaneScatter(
        down_keep, down_out, down_yin, down_zin, down_sent, down_landed, down_zlanded
    )

    def up_scatter(block):
        return Scatter(
            up_keep.at[block], up_out.at[block], up_yin.at[block], up_zin.at[block],
            up_sent.at[block], up_landed.at[block],
        )

    @pl.loop(0, 4)
    def _(block):
        some = pl.ds(pl.multiple_of(block * 256, 256), 256)
        up = up_ref[:, some]
        down = down_ref[some, :]
        sums = []
        for chunk in range(cap // CHUNK):
            here = slice(chunk * CHUNK, (chunk + 1) * CHUNK)
            u = jnp.dot(h_two_ref[here, :], up, preferred_element_type=jnp.float32) + vec_ref[8:9, some]
            square = u * u
            bent = jnp.tanh(0.7978845608028654 * (u * (1.0 + 0.044715 * square)))
            half = 0.5 * (1.0 + bent)
            act = (u * half).astype(jnp.bfloat16)
            act_ref[here, :] = act
            slope = half + 0.5 * u * (1.0 - bent * bent) * (
                0.7978845608028654 * (1.0 + 0.134145 * square)
            )
            grad_pre = (contract_cols(grad_ref[here, :], down) * slope).astype(jnp.bfloat16)
            grad_pre_ref[here, :] = grad_pre
            sums.append(jnp.sum(grad_pre.astype(jnp.float32), axis=0, keepdims=True))
            out_acc[here, :] += jnp.dot(act, down, preferred_element_type=jnp.float32)
            back_acc[here, :] += contract_cols(grad_pre, up)
        up_sums[block] = sum(sums)
        down_part = contract_rows(act_ref[...], grad_ref[...])
        down_scatter.store(block, down_part[:128], down_part[128:])
        down_scatter.begin(block)
        up_part = contract_rows(grad_pre_ref[...], h_two_ref[...])
        scatter = up_scatter(block)
        for plane in range(PLANES):
            lo = plane * 256
            scatter.store(plane, up_part[:, lo : lo + 128], up_part[:, lo + 128 : lo + 256])
        scatter.begin()

    def row_reduce(total, use):
        room = use % 2
        return RowReduce(
            total, mate_out.at[room], mate_in.at[room], cross_out.at[room], cross_in.at[room],
            red_sent.at[use], red_landed.at[use],
        )

    back = row_reduce(back_acc, 0)
    back.begin()
    outs = row_reduce(out_acc, 1)
    outs.begin()
    back.relay()
    down_scatter.relay(0)
    up_scatter(0).relay()
    down_scatter.relay(1)
    up_scatter(1).relay()
    resid = resid_ref[...]
    grad_out = cot_ref[...].astype(jnp.float32) * (live_ref[...] >= 0).astype(jnp.float32)
    vec_out[...] = jnp.zeros_like(vec_out)

    def put_vector(row, vector):
        for q in range(8):
            vec_out[q, row : row + 1, :] = vector[:, q * 128 : (q + 1) * 128]

    def column_sum(values):
        return jnp.sum(values, axis=0, keepdims=True)

    put_vector(7, column_sum(grad_out))
    grad_h_two = back.finish()
    put_vector(6, column_sum(grad_h_two))
    put_vector(5, column_sum(grad_h_two * centre_of(resid)))
    grad_back = grad_out + norm_back(resid, grad_h_two * vec_ref[5:6, :])
    input_grad_ref[...] = grad_back
    resid_low = grad_back.astype(jnp.bfloat16)
    resid_all[pl.ds(pl.multiple_of(ctx * rows, rows), rows), :] = resid_low
    gather = RowGather(resid_all, row_sent, row_landed)
    gather.begin()
    outs.relay()
    put_vector(4, column_sum(resid_low.astype(jnp.float32)))
    for block in range(4):
        for i in range(2):
            vec_out[2 * ctx + block // 2, 8 + block % 2 * 2 + i : 9 + block % 2 * 2 + i, :] = up_sums[block][
                :, i * 128 : (i + 1) * 128
            ]
    down_scatter.relay(2)
    up_scatter(2).relay()
    gather.forward()
    gather.end()
    for load in loads:
        load.wait()
    grad_heads[...] = contract_cols(resid_all[...], outw_ref[...]).astype(jnp.bfloat16)
    down_scatter.relay(3)
    up_scatter(3).relay()
    out_scatter = Scatter(out_keep, out_out, out_yin, out_zin, out_sent, out_landed)
    out_part = contract_rows(mixed_ref[...], resid_all[...])
    for plane in range(PLANES):
        lo = plane * 64
        out_scatter.store(plane, out_part[lo : lo + 32], out_part[lo + 32 : lo + 64])
    out_scatter.begin()

    def attend_back_head(head):
        pair, side = head // 2, head % 2
        lo, hi = head * HD, (head + 1) * HD
        for start in reversed(range(0, cap, rows)):
            stop = start + rows
            queries = qkv_ref[start:stop, lo:hi] * jnp.asarray(factor, jnp.bfloat16)
            keys = qkv_ref[:stop, width + lo : width + hi]
            values = qkv_ref[:stop, 2 * width + lo : 2 * width + hi]
            grads = grad_heads[start:stop, lo:hi]
            scores = masked_scores(queries, keys, ids_row_ref, ids_col_ref, start, stop)
            probs = jnp.exp(scores - lse_ref[head : head + 1, start:stop])
            grad_probs = contract_cols(values, grads)
            delta = jnp.sum(probs * grad_probs, axis=0, keepdims=True)
            grad_scores = (probs * (grad_probs - delta)).astype(jnp.bfloat16)
            query_grad = contract_rows(keys, grad_scores).T * factor
            grad_qkv[pair, start:stop, side * HD : side * HD + HD] = query_grad.astype(jnp.bfloat16)
            key_grad = jnp.dot(grad_scores, queries, preferred_element_type=jnp.float32)
            value_grad = jnp.dot(probs.astype(jnp.bfloat16), grads, preferred_element_type=jnp.float32)
            if stop == cap:
                key_acc[...] = key_grad
                value_acc[...] = value_grad
            else:
                key_acc[:stop, :] += key_grad
                value_acc[:stop, :] += value_grad
        lo = 128 + side * HD
        grad_qkv[pair, :, lo : lo + HD] = key_acc[...].astype(jnp.bfloat16)
        grad_qkv[pair, :, lo + 128 : lo + 128 + HD] = value_acc[...].astype(jnp.bfloat16)

    def qkv_scatter(pair):
        return Scatter(
            qkv_keep.at[pair], qkv_out.at[pair], qkv_yin.at[pair], qkv_zin.at[pair],
            qkv_sent.at[pair], qkv_landed.at[pair],
        )

    def pair_grads(pair):
        part = contract_rows(grad_qkv[pair], h_one_ref[...])
        scatter = qkv_scatter(pair)
        for plane in range(PLANES):
            lo = plane * 256
            scatter.store(plane, part[:, lo : lo + 128], part[:, lo + 128 : lo + 256])
        scatter.begin()
        sums = column_sum(grad_qkv[pair].astype(jnp.float32))
        vec_out[2 * ctx + pair, 2:3, :] = sums[:, :128]
        vec_out[2 * ctx + pair, 3:4, :] = sums[:, 256:]

    def pair_back(pair):
        weight = jnp.concatenate(
            [qkvw_ref[:, i * width + pair * 128 : i * width + pair * 128 + 128] for i in range(3)], axis=1
        )
        for chunk in range(4):
            here = slice(chunk * 256, (chunk + 1) * 256)
            part = contract_cols(grad_qkv[pair, here, :], weight)
            if pair == 0:
                back_acc[here, :] = part
            else:
                back_acc[here, :] += part

    attend_back_head(0)
    attend_back_head(1)
    pair_grads(0)
    pair_back(0)
    out_scatter.relay()
    output_ref[...] = (resid_ref[...] + outs.finish() + vec_ref[7:8, :]).astype(jnp.bfloat16)
    attend_back_head(2)
    attend_back_head(3)
    pair_back(1)
    back.settle()
    last = row_reduce(back_acc, 2)
    last.begin()
    pair_grads(1)
    last.relay()
    qkv_scatter(0).relay()
    for block in range(4):
        up_grad_ref[:, block * 256 : (block + 1) * 256] = up_scatter(block).finish().T
    down_grad_ref[...] = down_scatter.finish()
    out_grad_ref[...] = out_scatter.finish()
    values = x_ref[...].astype(jnp.float32)
    qkv_scatter(1).relay()
    grad_h_one = last.finish()
    put_vector(0, column_sum(grad_h_one * centre_of(values)))
    put_vector(1, column_sum(grad_h_one))

    def vec_copy(step):
        target = lax.rem(place + step, 8)
        return remote(
            vec_out.at[target], vec_in.at[step - 1], vec_sent.at[step - 1], vec_landed.at[step - 1],
            (target, ctx),
        )

    def ctx_copy(step):
        return remote(
            vec_ctx.at[ctx], vec_ctx.at[ctx], ctx_sent.at[step - 1], ctx_landed.at[step - 1],
            (place, lax.rem(ctx + step, 4)),
        )

    for step in range(1, 8):
        vec_copy(step).start()
    input_grad_ref[...] += norm_back(values, grad_h_one * vec_ref[0:1, :])
    total = vec_out[place]
    for step in range(1, 8):
        vec_copy(step).wait_recv()
        total = total + vec_in[step - 1]
    vec_ctx[ctx] = total
    for step in range(1, 4):
        ctx_copy(step).start()
    for pair in range(2):
        done = qkv_scatter(pair).finish().T
        for i in range(3):
            lo = i * width + pair * 128
            qkv_grad_ref[:, lo : lo + 128] = done[:, i * 128 : (i + 1) * 128]
    for step in range(1, 4):
        source = lax.rem(ctx + 4 - step, 4)
        remote(
            vec_ctx.at[source], vec_ctx.at[source], ctx_sent.at[step - 1], ctx_landed.at[step - 1],
            (place, source),
        ).wait_recv()
    sums_ref[...] = ((vec_ctx[0] + vec_ctx[1]) + vec_ctx[2]) + vec_ctx[3]
    for use in (outs, last):
        use.settle()
    for block in range(4):
        up_scatter(block).settle()
    down_scatter.settle()
    out_scatter.settle()
    for pair in range(2):
        qkv_scatter(pair).settle()
    for step in range(1, 8):
        vec_copy(step).wait_send()
    for step in range(1, 4):
        ctx_copy(step).wait_send()


def backward_pass(
    block_input, cotangent, own_ids, seq_ids, up_full, down_full, qkvw_full, outw_full, grad_all, vectors,
    h_one_all, qkv, mixed, lse, resid, h_two_all, heads, factor,
):
    rows, model = block_input.shape
    cap = seq_ids.shape[0]
    width = heads * HD
    hidden = up_full.shape[1]
    low, wide = jnp.bfloat16, jnp.float32
    anywhere = pl.BlockSpec(memory_space=pl.ANY)
    vmem = pl.BlockSpec(memory_space=pltpu.VMEM)
    shape = jax.ShapeDtypeStruct
    room, sems = pltpu.VMEM, pltpu.SemaphoreType.DMA

    def scatter_room(*lead_and_tail):
        lead, tail = lead_and_tail
        return [
            room(lead + (4,) + tail, wide),
            room(lead + (4,) + tail, low),
            room(lead + (4,) + tail, low),
            room(lead + (3,) + tail, low),
        ]

    return pl.pallas_call(
        functools.partial(backward_kernel, heads, factor),
        out_shape=(
            shape((rows, model), low),
            shape((rows, model), wide),
            shape((model // 8, 3 * width), wide),
            shape((width // 8, model), wide),
            shape((model // 8, hidden), wide),
            shape((hidden // 8, model), wide),
            shape((16, 128), wide),
        ),
        in_specs=[vmem] * 12 + [anywhere] * 5,
        out_specs=(vmem,) * 7,
        scratch_shapes=[
            room((cap, 3 * width), low),
            room((cap, width), low),
            room((cap, model), low),
            room((model, 3 * width), low),
            room((width, model), low),
            room((cap, model), wide),
            room((cap, model), wide),
            room((4, 1, 256), wide),
            room((cap, model), low),
            room((cap, width), low),
            room((2, cap, 384), low),
            room((cap, HD), wide),
            room((cap, HD), wide),
            room((cap, 256), low),
            room((cap, 256), low),
            room((2, 2, rows, model), low),
            room((2, 2, rows, model), low),
            room((2, rows, model), low),
            room((2, rows, model), low),
        ]
        + scatter_room((4,), (256, 128))
        + [
            room((4, 128, model), wide),
            room((4, 128, model), low),
            room((4, 128, model), low),
            room((3, 128, model), low),
        ]
        + scatter_room((), (32, model))
        + scatter_room((2,), (384, 128))
        + [
            room((8, 16, 128), wide),
            room((7, 16, 128), wide),
            room((4, 16, 128), wide),
            sems((5,)),
            sems((3, 3)),
            sems((3, 3)),
            sems((4, 4)),
            sems((4, 4)),
            sems((2, 4)),
            sems((4,)),
            sems((3,)),
            sems((4,)),
            sems((4,)),
            sems((2, 4)),
            sems((2, 4)),
            sems((3,)),
            sems((3,)),
            sems((7,)),
            sems((7,)),
            sems((3,)),
            sems((3,)),
        ],
        compiler_params=pltpu.CompilerParams(
            collective_id=2, has_side_effects=True, vmem_limit_bytes=62 * 2**20
        ),
        cost_estimate=pl.CostEstimate(
            flops=14 * cap * model * hidden,
            bytes_accessed=32 * 2**20,
            transcendentals=cap * cap * heads,
        ),
        name="backward_pass",
    )(
        h_two_all, grad_all, up_full, down_full, vectors, resid, block_input, cotangent, own_ids[:, None],
        lse, seq_ids[None, :], seq_ids[:, None], qkv, mixed, h_one_all, qkvw_full, outw_full,
    )


def on_device_general(
    block_input,
    ln1_gain,
    ln1_bias,
    qkv_weight,
    qv_bias,
    out_weight,
    out_bias,
    ln2_gain,
    ln2_bias,
    up_weight,
    up_bias,
    down_weight,
    down_bias,
    doc_ids,
    cotangent,
):
    shards = lax.axis_size("fsdp")
    small = jnp.concatenate(
        [
            ln1_gain,
            ln1_bias,
            qv_bias[0],
            qv_bias[1],
            out_bias,
            ln2_gain,
            ln2_bias,
            down_bias,
            up_bias,
        ]
    )
    rows = block_input.shape[0]
    model = block_input.shape[1]
    groups = lax.axis_size("ctx")
    place = lax.axis_index("ctx")
    capacity = rows * groups
    width = qkv_weight.shape[2]
    heads_here = width // HD
    hidden_here = up_weight.shape[1]
    factor = 1.0 / HD**0.5
    group_ids = doc_ids[0]
    own_ids = lax.dynamic_slice_in_dim(group_ids, place * rows, rows)
    input_all = gather_rows(block_input)
    qkv_rows = qkv_weight.shape[0]
    small_rows = -(-small.shape[0] // (3 * width * 16)) * 16
    first = jnp.concatenate(
        [
            qkv_weight.reshape(qkv_rows, 3 * width),
            jnp.pad(small, (0, small_rows * 3 * width - small.shape[0])).reshape(
                small_rows, 3 * width
            ),
        ]
    )
    first_all = gather_weight(first)
    small_all = first_all[:, qkv_rows:].reshape(shards, -1)[:, : small.shape[0]]
    piece = model // shards
    gain_one, shift_one, query_shift, value_shift, out_shift, gain_two, shift_two, down_shift = (
        small_all[:, i * piece : (i + 1) * piece].reshape(model) for i in range(8)
    )
    up_shift = small_all[:, 8 * piece :].reshape(-1)
    qv_full = jnp.stack([query_shift, value_shift])
    qkv_flat = first_all[:, :qkv_rows].reshape(model, 3 * width)
    out_full = gather_weight(out_weight).reshape(width, model)
    up_full = gather_weight(up_weight).reshape(model, hidden_here)
    down_full = gather_weight(down_weight).reshape(hidden_here, model)
    cot_all = gather_rows(cotangent)
    qv_here = lax.dynamic_slice_in_dim(qv_full.astype(jnp.float32), place * width, width, 1)
    qkv_shift = jnp.concatenate([qv_here[0], jnp.zeros((width,), jnp.float32), qv_here[1]])
    up_here = lax.dynamic_slice_in_dim(
        up_shift.astype(jnp.float32), place * hidden_here, hidden_here, 0
    )
    input_float = block_input.astype(jnp.float32)
    norm_one_all = normalize(input_all.astype(jnp.float32))
    h_one_all = (norm_one_all * gain_one + shift_one).astype(jnp.bfloat16)
    qkv_proj = project(h_one_all, qkv_flat)
    qkv = (qkv_proj + qkv_shift).astype(jnp.bfloat16)
    mixed_all, log_sums = attend(qkv, group_ids, heads_here, factor)
    out_part = project(mixed_all, out_full)
    resid = input_float + reduce_rows(out_part) + out_shift
    norm_two = normalize(resid)
    h_two = (norm_two * gain_two + shift_two).astype(jnp.bfloat16)
    h_two_all = gather_rows(h_two)
    live = (own_ids >= 0).astype(jnp.float32)
    grad_out = cotangent.astype(jnp.float32) * live[:, None]
    grad_low = grad_out.astype(jnp.bfloat16)
    down_shift_grad = jnp.sum(grad_low.astype(jnp.float32), axis=0)
    grad_all = jnp.where(group_ids[:, None] >= 0, cot_all, jnp.zeros_like(cot_all))
    act_low, grad_pre, up_sums, down_part, back_part = mlp(
        h_two_all, grad_all, up_full, up_here, down_full
    )
    grad_h_two = reduce_rows(back_part)
    output = (resid + reduce_rows(down_part) + down_shift).astype(jnp.bfloat16)
    down_grad = weight_grad(act_low, grad_all)
    up_grad = weight_grad(h_two_all, grad_pre)
    up_sums = up_sums[0]
    up_shift_grad = lax.dynamic_update_slice_in_dim(
        jnp.zeros((FF,), jnp.float32), up_sums, place * hidden_here, 0
    )
    gain_two_grad = jnp.sum(grad_h_two * norm_two, axis=0)
    shift_two_grad = jnp.sum(grad_h_two, axis=0)
    unused_two, norm_back_two = jax.vjp(normalize, resid)
    grad_resid = grad_out + norm_back_two(grad_h_two * gain_two.astype(jnp.float32))[0]
    resid_low = grad_resid.astype(jnp.bfloat16)
    out_shift_grad = jnp.sum(resid_low.astype(jnp.float32), axis=0)
    resid_all = gather_rows(resid_low)
    out_grad = weight_grad(mixed_all, resid_all)
    grad_heads = project_back(resid_all, out_full).astype(jnp.bfloat16)
    grad_qkv = attend_back(qkv, grad_heads, log_sums, group_ids, heads_here, factor)
    qkv_grad = weight_grad(h_one_all, grad_qkv).reshape(qkv_weight.shape[0], 3, width)
    column_sums = jnp.sum(grad_qkv.astype(jnp.float32), axis=0).reshape(3, width)
    qv_local = jnp.stack([column_sums[0], column_sums[2]])
    qv_grad = lax.dynamic_update_slice_in_dim(
        jnp.zeros((2, model), jnp.float32), qv_local, place * width, 1
    )
    grad_h_one_part = project_back(grad_qkv, qkv_flat)
    gain_one_grad = jnp.sum(grad_h_one_part * norm_one_all, axis=0)
    shift_one_grad = jnp.sum(grad_h_one_part, axis=0)
    grad_h_one = reduce_rows(grad_h_one_part)
    unused_one, norm_back_one = jax.vjp(normalize, input_float)
    input_grad = grad_resid + norm_back_one(grad_h_one * gain_one.astype(jnp.float32))[0]
    packed = jnp.concatenate(
        [
            part.reshape(shards, -1)
            for part in (
                gain_one_grad,
                shift_one_grad,
                qv_grad[0],
                qv_grad[1],
                out_shift_grad,
                gain_two_grad,
                shift_two_grad,
                down_shift_grad,
                up_shift_grad,
            )
        ],
        1,
    )
    sums = sum_ctx(scatter_fsdp(packed.reshape(shards, -1, 128), jnp.float32)).reshape(-1)
    (
        gain_one_sum,
        shift_one_sum,
        query_sum,
        value_sum,
        out_shift_sum,
        gain_two_sum,
        shift_two_sum,
        down_shift_sum,
    ) = (sums[i * piece : (i + 1) * piece] for i in range(8))
    qv_sum = jnp.stack([query_sum, value_sum])
    up_shift_sum = sums[8 * piece :]
    return (
        output,
        input_grad,
        gain_one_sum,
        shift_one_sum,
        qkv_grad,
        qv_sum,
        out_grad,
        out_shift_sum,
        gain_two_sum,
        shift_two_sum,
        up_grad,
        up_shift_sum,
        down_grad,
        down_shift_sum,
    )


def on_device(
    block_input,
    ln1_gain,
    ln1_bias,
    qkv_weight,
    qv_bias,
    out_weight,
    out_bias,
    ln2_gain,
    ln2_bias,
    up_weight,
    up_bias,
    down_weight,
    down_bias,
    doc_ids,
    cotangent,
):
    model = block_input.shape[1]
    if lax.axis_size("fsdp") != 8 or lax.axis_size("ctx") != 4:
        return on_device_general(
            block_input, ln1_gain, ln1_bias, qkv_weight, qv_bias, out_weight, out_bias, ln2_gain,
            ln2_bias, up_weight, up_bias, down_weight, down_bias, doc_ids, cotangent,
        )
    rows = block_input.shape[0]
    place = lax.axis_index("ctx")
    width = qkv_weight.shape[2]
    heads_here = width // HD
    factor = 1.0 / HD**0.5
    group_ids = doc_ids[0]
    own_ids = lax.dynamic_slice_in_dim(group_ids, place * rows, rows)
    small = jnp.concatenate(
        [ln1_gain, ln1_bias, qv_bias[0], qv_bias[1], out_bias, ln2_gain, ln2_bias, down_bias, up_bias]
    )
    small = jnp.pad(small, (0, 16 * 128 - small.shape[0])).reshape(16, 128)
    (
        up_full, down_full, qkv_flat, out_full, grad_all, vectors, h_one_all, qkv, mixed_all, log_sums,
        resid, h_two_all,
    ) = forward_pass(
        block_input, cotangent, own_ids, small, qkv_weight.reshape(-1, 3 * width), out_weight, up_weight,
        down_weight, group_ids, heads_here, factor,
    )
    output, input_grad, qkv_grad, out_grad, up_grad, down_grad, sums = backward_pass(
        block_input, cotangent, own_ids, group_ids, up_full, down_full, qkv_flat, out_full, grad_all,
        vectors, h_one_all, qkv, mixed_all, log_sums, resid, h_two_all, heads_here, factor,
    )
    return (
        output,
        input_grad,
        sums[0],
        sums[1],
        qkv_grad.reshape(qkv_weight.shape),
        sums[2:4],
        out_grad,
        sums[4],
        sums[5],
        sums[6],
        up_grad,
        sums[8:12].reshape(-1),
        down_grad,
        sums[7],
    )


def solution(mesh):
    placed = (
        P(("fsdp", "ctx"), None),
        P("fsdp"),
        P("fsdp"),
        P("fsdp", None, "ctx"),
        P(None, "fsdp"),
        P(("ctx", "fsdp"), None),
        P("fsdp"),
        P("fsdp"),
        P("fsdp"),
        P("fsdp", "ctx"),
        P("fsdp"),
        P(("ctx", "fsdp"), None),
        P("fsdp"),
        P("fsdp", None),
        P(("fsdp", "ctx"), None),
    )
    return jax.shard_map(
        on_device,
        mesh=mesh,
        in_specs=placed,
        out_specs=(
            P(("fsdp", "ctx"), None),
            P(("fsdp", "ctx"), None),
            P("fsdp"),
            P("fsdp"),
            P("fsdp", None, "ctx"),
            P(None, "fsdp"),
            P(("ctx", "fsdp"), None),
            P("fsdp"),
            P("fsdp"),
            P("fsdp"),
            P("fsdp", "ctx"),
            P("fsdp"),
            P(("ctx", "fsdp"), None),
            P("fsdp"),
        ),
        check_vma=False,
    )
```

```python
import functools

import jax
import jax.numpy as jnp
from jax import lax
from jax.experimental import pallas as pl
from jax.experimental.pallas import tpu as pltpu
from jax.sharding import PartitionSpec as P

HD = 64
FF = 4096


eps = 1e-05


def normalize(values):
    centre = values - jnp.mean(values, axis=-1, keepdims=True)
    spread = jnp.mean(centre * centre, axis=-1, keepdims=True)
    return centre * lax.rsqrt(spread + eps)


def contract_rows(left, right):
    return lax.dot_general(
        left, right, (((0,), (0,)), ((), ())), preferred_element_type=jnp.float32
    )


def contract_cols(left, right):
    return lax.dot_general(
        left, right, (((1,), (1,)), ((), ())), preferred_element_type=jnp.float32
    )


def split_fsdp():
    total = lax.axis_size("fsdp")
    inner = 2 if total <= 8 else 8
    return total // inner, inner


def move_fsdp(values, outer_step, inner_step):
    outer, inner = split_fsdp()
    pairs = [
        (a * inner + b, (a + outer_step) % outer * inner + (b + inner_step) % inner)
        for a in range(outer)
        for b in range(inner)
    ]
    return lax.ppermute(values, "fsdp", pairs)


def move_ctx(values, chip_step, core_step):
    chips = lax.axis_size("ctx") // 2
    pairs = [
        (x * 2 + c, (x + chip_step) % chips * 2 + (c + core_step) % 2)
        for x in range(chips)
        for c in range(2)
    ]
    return lax.ppermute(values, "ctx", pairs)


def put(buffer, values, place, axis):
    return lax.dynamic_update_index_in_dim(buffer, values, place, axis)


def pick(buffer, place, axis):
    return lax.dynamic_index_in_dim(buffer, place, axis, keepdims=False)


def gather_weight(shard):
    outer, inner = split_fsdp()
    place = lax.axis_index("fsdp")
    a, b = place // inner, place % inner
    held = put(jnp.zeros((outer,) + shard.shape, shard.dtype), shard, a, 0)
    for step in range(1, outer):
        held = put(held, move_fsdp(shard, step, 0), (a + outer - step) % outer, 0)
    if inner == 2:
        other = move_fsdp(held, 0, 1)
        first = b == 0
        whole = jnp.stack([jnp.where(first, held, other), jnp.where(first, other, held)], 1)
    else:
        whole = put(jnp.zeros((outer, inner) + shard.shape, shard.dtype), held, b, 1)
        for step in range(1, inner):
            whole = put(whole, move_fsdp(held, 0, step), (b + inner - step) % inner, 1)
    return whole.reshape((outer * inner,) + shard.shape)


def scatter_fsdp(parts, sent_type):
    outer, inner = split_fsdp()
    place = lax.axis_index("fsdp")
    a, b = place // inner, place % inner
    parts = parts.reshape((outer, inner) + parts.shape[1:])
    held = pick(parts, b, 1).astype(jnp.float32)
    for step in range(1, inner):
        sent = pick(parts, (b + step) % inner, 1).astype(sent_type)
        held = held + move_fsdp(sent, 0, step).astype(jnp.float32)
    summed = pick(held, a, 0)
    for step in range(1, outer):
        sent = pick(held, (a + step) % outer, 0).astype(sent_type)
        summed = summed + move_fsdp(sent, step, 0).astype(jnp.float32)
    return summed


def gather_rows(values):
    groups = lax.axis_size("ctx")
    chips = groups // 2
    place = lax.axis_index("ctx")
    x, core = place // 2, place % 2
    whole = jnp.zeros((groups,) + values.shape, values.dtype)
    for step in range(chips):
        got = values if step == 0 else move_ctx(values, step, 0)
        origin = (x + chips - step) % chips * 2
        whole = put(whole, got, origin + core, 0)
        whole = put(whole, move_ctx(got, 0, 1), origin + 1 - core, 0)
    return whole.reshape((groups * values.shape[0],) + values.shape[1:])


def reduce_rows(parts):
    groups = lax.axis_size("ctx")
    chips = groups // 2
    place = lax.axis_index("ctx")
    x, core = place // 2, place % 2
    parts = parts.reshape((chips, 2, parts.shape[0] // groups) + parts.shape[1:])
    sent = pick(parts, 1 - core, 1).astype(jnp.bfloat16)
    held = pick(parts, core, 1).astype(jnp.float32) + move_ctx(sent, 0, 1).astype(jnp.float32)
    summed = pick(held, x, 0)
    for step in range(1, chips):
        sent = pick(held, (x + step) % chips, 0).astype(jnp.bfloat16)
        summed = summed + move_ctx(sent, step, 0).astype(jnp.float32)
    return summed


def sum_ctx(values):
    chips = lax.axis_size("ctx") // 2
    total = values + move_ctx(values, 0, 1)
    whole = total
    for step in range(1, chips):
        whole = whole + move_ctx(total, step, 0)
    return whole


def project(inputs, weight):
    return jnp.dot(inputs, weight, preferred_element_type=jnp.float32)


def project_back(grad_low, weight):
    return contract_cols(grad_low, weight)


def weight_grad(inputs, grad_low):
    shards = lax.axis_size("fsdp")
    full = contract_rows(inputs, grad_low)
    return scatter_fsdp(
        full.reshape(shards, full.shape[0] // shards, full.shape[1]), jnp.bfloat16
    )


BLOCK = 256
MASKED = -1000000000.0


def masked_scores(queries, keys, ids_row_ref, ids_col_ref, start, stop):
    scores = contract_cols(keys, queries)
    same = ids_col_ref[:stop, :] == ids_row_ref[:, start:stop]
    key_place = lax.broadcasted_iota(jnp.int32, scores.shape, 0)
    query_place = lax.broadcasted_iota(jnp.int32, scores.shape, 1) + start
    return jnp.where(same & (key_place <= query_place), scores, MASKED)


def attend_kernel(heads, block, factor, qkv_ref, ids_row_ref, ids_col_ref, out_ref, lse_ref):
    rows = qkv_ref.shape[0]
    width = heads * HD
    for start in range(0, rows, block):
        stop = start + block
        for head in range(heads):
            lo, hi = head * HD, (head + 1) * HD
            queries = qkv_ref[start:stop, lo:hi] * jnp.asarray(factor, jnp.bfloat16)
            keys = qkv_ref[:stop, width + lo : width + hi]
            values = qkv_ref[:stop, 2 * width + lo : 2 * width + hi]
            scores = masked_scores(queries, keys, ids_row_ref, ids_col_ref, start, stop)
            top = jnp.max(scores, axis=0, keepdims=True)
            expo = jnp.exp(scores - top)
            summed = jnp.sum(expo, axis=0, keepdims=True)
            probs_low = (expo * (1.0 / summed)).astype(jnp.bfloat16)
            out_ref[start:stop, lo:hi] = contract_rows(values, probs_low).T.astype(jnp.bfloat16)
            lse_ref[head : head + 1, start:stop] = top + jnp.log(summed)


def attend_back_kernel(
    heads, block, factor, qkv_ref, grad_ref, lse_ref, ids_row_ref, ids_col_ref, out_ref, key_acc, value_acc
):
    rows = qkv_ref.shape[0]
    width = heads * HD
    for head in range(heads):
        lo, hi = head * HD, (head + 1) * HD
        for start in reversed(range(0, rows, block)):
            stop = start + block
            queries = qkv_ref[start:stop, lo:hi] * jnp.asarray(factor, jnp.bfloat16)
            keys = qkv_ref[:stop, width + lo : width + hi]
            values = qkv_ref[:stop, 2 * width + lo : 2 * width + hi]
            grads = grad_ref[start:stop, lo:hi]
            scores = masked_scores(queries, keys, ids_row_ref, ids_col_ref, start, stop)
            probs = jnp.exp(scores - lse_ref[head : head + 1, start:stop])
            grad_probs = contract_cols(values, grads)
            delta = jnp.sum(probs * grad_probs, axis=0, keepdims=True)
            grad_scores = (probs * (grad_probs - delta)).astype(jnp.bfloat16)
            query_grad = contract_rows(keys, grad_scores).T * factor
            out_ref[start:stop, lo:hi] = query_grad.astype(jnp.bfloat16)
            key_grad = jnp.dot(grad_scores, queries, preferred_element_type=jnp.float32)
            value_grad = jnp.dot(
                probs.astype(jnp.bfloat16), grads, preferred_element_type=jnp.float32
            )
            if stop == rows:
                key_acc[...] = key_grad
                value_acc[...] = value_grad
            else:
                key_acc[:stop, :] += key_grad
                value_acc[:stop, :] += value_grad
        out_ref[:, width + lo : width + hi] = key_acc[...].astype(jnp.bfloat16)
        out_ref[:, 2 * width + lo : 2 * width + hi] = value_acc[...].astype(jnp.bfloat16)


def attend(qkv, seq_ids, heads, factor):
    rows = qkv.shape[0]
    block = min(BLOCK, rows)
    return pl.pallas_call(
        functools.partial(attend_kernel, heads, block, factor),
        out_shape=(
            jax.ShapeDtypeStruct((rows, heads * HD), jnp.bfloat16),
            jax.ShapeDtypeStruct((heads, rows), jnp.float32),
        ),
        compiler_params=pltpu.CompilerParams(vmem_limit_bytes=40 * 2**20),
        cost_estimate=pl.CostEstimate(
            flops=4 * rows * rows * 256 * heads,
            bytes_accessed=8 * rows * heads * HD,
            transcendentals=rows * rows * heads,
        ),
        name="attend",
    )(qkv, seq_ids[None, :], seq_ids[:, None])


def attend_back(qkv, grads, log_sums, seq_ids, heads, factor):
    rows = qkv.shape[0]
    block = min(BLOCK, rows)
    return pl.pallas_call(
        functools.partial(attend_back_kernel, heads, block, factor),
        out_shape=jax.ShapeDtypeStruct(qkv.shape, jnp.bfloat16),
        scratch_shapes=[pltpu.VMEM((rows, HD), jnp.float32)] * 2,
        compiler_params=pltpu.CompilerParams(vmem_limit_bytes=40 * 2**20),
        cost_estimate=pl.CostEstimate(
            flops=10 * rows * rows * 256 * heads,
            bytes_accessed=14 * rows * heads * HD,
            transcendentals=rows * rows * heads,
        ),
        name="attend_back",
    )(qkv, grads, log_sums, seq_ids[None, :], seq_ids[:, None])


def mlp_kernel(
    in_ref,
    grad_ref,
    up_ref,
    shift_ref,
    down_ref,
    act_ref,
    pre_ref,
    sums_ref,
    out_ref,
    back_ref,
    out_acc,
    back_acc,
):
    step = pl.program_id(0)
    u = jnp.dot(in_ref[...], up_ref[...], preferred_element_type=jnp.float32) + shift_ref[...]
    square = u * u
    bent = jnp.tanh(0.7978845608028654 * (u * (1.0 + 0.044715 * square)))
    half = 0.5 * (1.0 + bent)
    act = (u * half).astype(jnp.bfloat16)
    act_ref[...] = act
    slope = half + 0.5 * u * (1.0 - bent * bent) * (
        0.7978845608028654 * (1.0 + 0.134145 * square)
    )
    grad_pre = (contract_cols(grad_ref[...], down_ref[...]) * slope).astype(jnp.bfloat16)
    pre_ref[...] = grad_pre
    sums_ref[...] = jnp.sum(grad_pre.astype(jnp.float32), axis=0, keepdims=True)
    out_part = jnp.dot(act, down_ref[...], preferred_element_type=jnp.float32)
    back_part = contract_cols(grad_pre, up_ref[...])

    @pl.when(step == 0)
    def _():
        out_acc[...] = out_part
        back_acc[...] = back_part

    @pl.when(step > 0)
    def _():
        out_acc[...] += out_part
        back_acc[...] += back_part

    @pl.when(step == pl.num_programs(0) - 1)
    def _():
        out_ref[...] = out_acc[...].astype(jnp.bfloat16)
        back_ref[...] = back_acc[...].astype(jnp.bfloat16)


def mlp(inputs, grads, up, shift, down):
    rows, model = inputs.shape
    hidden = up.shape[1]
    block = min(256, hidden)
    whole = pl.BlockSpec((rows, model), lambda i: (0, 0))
    columns = pl.BlockSpec((rows, block), lambda i: (0, i))
    line = pl.BlockSpec((1, block), lambda i: (0, i))
    return pl.pallas_call(
        mlp_kernel,
        grid=(hidden // block,),
        in_specs=[
            whole,
            whole,
            pl.BlockSpec((model, block), lambda i: (0, i)),
            line,
            pl.BlockSpec((block, model), lambda i: (i, 0)),
        ],
        out_specs=(columns, columns, line, whole, whole),
        out_shape=(
            jax.ShapeDtypeStruct((rows, hidden), jnp.bfloat16),
            jax.ShapeDtypeStruct((rows, hidden), jnp.bfloat16),
            jax.ShapeDtypeStruct((1, hidden), jnp.float32),
            jax.ShapeDtypeStruct((rows, model), jnp.bfloat16),
            jax.ShapeDtypeStruct((rows, model), jnp.bfloat16),
        ),
        scratch_shapes=[pltpu.VMEM((rows, model), jnp.float32)] * 2,
        compiler_params=pltpu.CompilerParams(vmem_limit_bytes=52 * 2**20),
        cost_estimate=pl.CostEstimate(
            flops=8 * rows * model * hidden,
            bytes_accessed=8 * rows * model + 4 * rows * hidden + 4 * model * hidden,
            transcendentals=rows * hidden,
        ),
        name="mlp",
    )(inputs, grads, up, shift[None, :], down)


MESH = pl.DeviceIdType.MESH
PLANES = 4


def remote(source, target, sent, landed, device):
    return pltpu.make_async_remote_copy(
        src_ref=source,
        dst_ref=target,
        send_sem=sent,
        recv_sem=landed,
        device_id=device,
        device_id_type=MESH,
    )


def seat():
    place = lax.axis_index("fsdp")
    ctx = lax.axis_index("ctx")
    z, y = place // 2, lax.rem(place, 2)
    x, core = ctx // 2, lax.rem(ctx, 2)
    return place, ctx, z, y, x, core


def centre_of(values):
    centre = values - jnp.mean(values, axis=-1, keepdims=True)
    spread = jnp.mean(centre * centre, axis=-1, keepdims=True)
    return centre * lax.rsqrt(spread + eps)


class RowGather:
    def __init__(self, target, sent, landed):
        self.target, self.sent, self.landed = target, sent, landed
        self.place, self.ctx, z, y, x, core = seat()
        self.mate = self.ctx + 1 - 2 * core
        self.across = self.ctx + 2 - 4 * x
        self.rows = target.shape[0] // 4
        self.sends = []

    def at(self, ctx):
        return self.target.at[pl.ds(pl.multiple_of(ctx * self.rows, self.rows), self.rows), :]

    def move(self, ctx, slot, device):
        return remote(
            self.at(ctx), self.at(ctx), self.sent.at[slot], self.landed.at[slot],
            (self.place, device),
        )

    def send(self, ctx, slot, device):
        copy = self.move(ctx, slot, device)
        copy.start()
        self.sends.append(copy)

    def begin(self):
        self.send(self.ctx, 1, self.across)
        self.send(self.ctx, 0, self.mate)

    def forward(self):
        self.move(self.across, 1, self.across).wait_recv()
        self.send(self.across, 2, self.mate)

    def end(self):
        opposite = self.across + self.mate - self.ctx
        self.move(self.mate, 0, self.mate).wait_recv()
        self.move(opposite, 2, self.mate).wait_recv()
        for copy in self.sends:
            copy.wait_send()


CHUNK = 512


class RowReduce:
    def __init__(self, total, mate_out, mate_in, cross_out, cross_in, sent, landed):
        self.total, self.mate_out, self.mate_in = total, mate_out, mate_in
        self.cross_out, self.cross_in, self.sent, self.landed = cross_out, cross_in, sent, landed
        self.place, self.ctx, z, y, self.x, self.core = seat()
        self.rows = total.shape[0] // 4

    def part(self, side, core):
        first = pl.multiple_of((side * 2 + core) * self.rows, self.rows)
        return self.total[pl.ds(first, self.rows), :]

    def mate_copy(self, slot):
        return remote(
            self.mate_out.at[slot], self.mate_in.at[slot], self.sent.at[slot], self.landed.at[slot],
            (self.place, self.ctx + 1 - 2 * self.core),
        )

    def cross_copy(self):
        return remote(
            self.cross_out, self.cross_in, self.sent.at[2], self.landed.at[2],
            (self.place, self.ctx + 2 - 4 * self.x),
        )

    def begin(self):
        for slot, side in ((0, 1 - self.x), (1, self.x)):
            self.mate_out[slot] = self.part(side, 1 - self.core).astype(jnp.bfloat16)
            self.mate_copy(slot).start()

    def relay(self):
        self.mate_copy(0).wait_recv()
        self.cross_out[...] = (
            self.part(1 - self.x, self.core) + self.mate_in[0].astype(jnp.float32)
        ).astype(jnp.bfloat16)
        self.cross_copy().start()

    def finish(self):
        self.mate_copy(1).wait_recv()
        held = self.part(self.x, self.core) + self.mate_in[1].astype(jnp.float32)
        self.cross_copy().wait_recv()
        return held + self.cross_in[...].astype(jnp.float32)

    def settle(self):
        for slot in range(2):
            self.mate_copy(slot).wait_send()
        self.cross_copy().wait_send()


class Scatter:
    def __init__(self, keep, out, yin, zin, sent, landed):
        self.keep, self.yout, self.yin, self.zout, self.zin = keep, out, yin, out, zin
        self.sent, self.landed = sent, landed
        self.place, self.ctx, self.z, self.y, x, core = seat()

    def store(self, plane, even, odd):
        first = self.y == 0
        self.keep[plane] = jnp.where(first, even, odd)
        self.yout[plane] = jnp.where(first, odd, even).astype(jnp.bfloat16)

    def ycopy(self):
        return remote(
            self.yout, self.yin, self.sent.at[0], self.landed.at[0], (self.place + 1 - 2 * self.y, self.ctx)
        )

    def zcopy(self, step):
        return remote(
            self.zout.at[step - 1], self.zin.at[step - 1], self.sent.at[step], self.landed.at[step],
            (lax.rem(self.z + step, PLANES) * 2 + self.y, self.ctx),
        )

    def begin(self):
        self.ycopy().start()

    def relay(self):
        self.ycopy().wait()
        for step in (2, 1, 3):
            plane = lax.rem(self.z + step, PLANES)
            self.zout[step - 1] = (self.keep[plane] + self.yin[plane].astype(jnp.float32)).astype(
                jnp.bfloat16
            )
            self.zcopy(step).start()

    def finish(self):
        total = self.keep[self.z] + self.yin[self.z].astype(jnp.float32)
        for step in (1, 3, 2):
            self.zcopy(step).wait_recv()
            total = total + self.zin[step - 1].astype(jnp.float32)
        return total

    def settle(self):
        for step in (1, 2, 3):
            self.zcopy(step).wait_send()


class PlaneScatter:
    def __init__(self, keep, out, yin, zin, sent, landed, zlanded):
        self.keep, self.yout, self.yin, self.zout, self.zin = keep, out, yin, out, zin
        self.sent, self.landed, self.zlanded = sent, landed, zlanded
        self.place, self.ctx, self.z, self.y, x, core = seat()

    def store(self, block, even, odd):
        first = self.y == 0
        self.keep[block] = jnp.where(first, even, odd)
        self.yout[block] = jnp.where(first, odd, even).astype(jnp.bfloat16)

    def ycopy(self, block):
        return remote(
            self.yout.at[block], self.yin.at[block], self.sent.at[0, block], self.landed.at[block],
            (self.place + 1 - 2 * self.y, self.ctx),
        )

    def zcopy(self, block):
        slot = lax.rem(self.z - block + PLANES, PLANES) - 1
        return remote(
            self.zout.at[block], self.zin.at[slot], self.sent.at[1, block], self.zlanded.at[slot],
            (block * 2 + self.y, self.ctx),
        )

    def begin(self, block):
        self.ycopy(block).start()

    def relay(self, block):
        self.ycopy(block).wait()

        @pl.when(self.z != block)
        def _():
            self.zout[block] = (self.keep[block] + self.yin[block].astype(jnp.float32)).astype(jnp.bfloat16)
            self.zcopy(block).start()

    def finish(self):
        total = self.keep[self.z] + self.yin[self.z].astype(jnp.float32)
        for slot in range(3):
            remote(
                self.zin.at[slot], self.zin.at[slot], self.sent.at[1, 0], self.zlanded.at[slot],
                (self.place + 1 - 2 * self.y, self.ctx),
            ).wait_recv()
            total = total + self.zin[slot].astype(jnp.float32)
        return total

    def settle(self):
        for block in range(PLANES):

            @pl.when(self.z != block)
            def _():
                self.zcopy(block).wait_send()


def norm_back(values, grads):
    centre = values - jnp.mean(values, axis=-1, keepdims=True)
    scale = lax.rsqrt(jnp.mean(centre * centre, axis=-1, keepdims=True) + eps)
    unit = centre * scale
    along = jnp.mean(grads * unit, axis=-1, keepdims=True)
    return (grads - jnp.mean(grads, axis=-1, keepdims=True) - unit * along) * scale


def block_kernel(
    heads, factor,
    x_ref, cot_ref, ids_row_ref, gain1_ref, shift1_ref, qv_ref, oshift_ref, gain2_ref, shift2_ref, dshift_ref,
    ushift_ref, qkvw_ref, outw_ref, upw_ref, downw_ref,
    output_ref, input_grad_ref, qkv_grad_ref, out_grad_ref, up_grad_ref, down_grad_ref, sums_ref,
    up_all, down_all, qkvw_all, outw_all, grad_all, vec_ref, h_one_all, qkv_ref, mixed_ref, lse_ref,
    resid_ref, h_two_all, ids_col_ref, small_ref, small_all,
    out_acc, back_acc, up_sums, resid_all, grad_heads, grad_qkv, key_acc, value_acc, act_ref, grad_pre_ref,
    mate_out, mate_in, cross_out, cross_in,
    up_keep, up_out, up_yin, up_zin, down_keep, down_out, down_yin, down_zin,
    out_keep, out_out, out_yin, out_zin, qkv_keep, qkv_out, qkv_yin, qkv_zin,
    vec_out, vec_in, vec_ctx,
    zsent, zlanded, ysent, ylanded, local_sem, gather_sent, gather_landed,
    red_sent, red_landed, up_sent, up_landed, down_sent, down_landed, down_zlanded, out_sent,
    out_landed, qkv_sent, qkv_landed, vec_sent, vec_landed, ctx_sent, ctx_landed,
):
    place, ctx, z, y, x, core = seat()
    flip = place + 1 - 2 * y
    mate = ctx + 1 - 2 * core
    across = ctx + 2 - 4 * x
    rows = x_ref.shape[0]
    width = heads * HD
    cap = h_two_all.shape[0]

    wide = lambda ref: ref[...].astype(jnp.float32).reshape(-1, 128)
    small_ref[...] = jnp.concatenate(
        [
            wide(gain1_ref), wide(shift1_ref), wide(qv_ref), wide(oshift_ref), wide(gain2_ref),
            wide(shift2_ref), wide(dshift_ref), wide(ushift_ref), jnp.zeros((4, 128), jnp.float32),
        ],
        axis=0,
    ).astype(jnp.bfloat16)
    barrier = pltpu.get_barrier_semaphore()

    for step in range(1, 8):
        pl.semaphore_signal(
            barrier, inc=1, device_id=(lax.rem(place + step, 8), ctx), device_id_type=MESH
        )
    for step in range(1, 4):
        pl.semaphore_signal(
            barrier, inc=1, device_id=(place, lax.rem(ctx + step, 4)), device_id_type=MESH
        )
    pl.semaphore_wait(barrier, 10)

    half = upw_ref.shape[0] // 2
    pieces = (
        (small_ref, small_all, 0, small_ref.shape[0]),
        (qkvw_ref, qkvw_all, 0, qkvw_ref.shape[1]),
        (outw_ref, outw_all, 0, outw_ref.shape[0]),
        (upw_ref, up_all, 0, half),
        (upw_ref, up_all, half, half),
        (downw_ref, down_all, 0, half),
        (downw_ref, down_all, half, half),
    )

    def spot(piece, shard):
        source, target, start, count = pieces[piece]
        if piece == 1:
            return target.at[:, pl.ds(pl.multiple_of(shard * count, count), count), :]
        first = pl.multiple_of(shard * source.shape[0] + start, count)
        return target.at[pl.ds(first, count), :]

    def zcopy(piece, shard, right, hop, source=None):
        slot = (0 if right else 3) + hop - 1
        spot_ = spot(piece, shard)
        device = (place + 2 if right else place - 2, ctx)
        return remote(
            spot_ if source is None else source, spot_, zsent.at[piece, slot], zlanded.at[piece, slot], device
        )

    def ycopy(piece, shard, slot, source=None):
        spot_ = spot(piece, shard)
        return remote(
            spot_ if source is None else source, spot_, ysent.at[piece, slot], ylanded.at[piece, slot],
            (flip, ctx),
        )

    def own(piece):
        source, target, start, count = pieces[piece]
        return source if piece == 1 else source.at[pl.ds(start, count), :]

    def can(right):
        return z < PLANES - 1 if right else z > 0

    def arrived(right, hop):
        return z >= hop if right else z < PLANES - hop

    def local(piece):
        return pltpu.make_async_copy(own(piece), spot(piece, place), local_sem.at[piece])

    def launch(piece):
        for right in (True, False):

            @pl.when(can(right))
            def _():
                zcopy(piece, place, right, 1, own(piece)).start()

        ycopy(piece, place, 6, own(piece)).start()
        local(piece).start()

    def origin(right, hop):
        return place - 2 * hop if right else place + 2 * hop

    def pump(piece, hop):
        for right in (True, False):

            @pl.when(arrived(right, hop))
            def _():
                shard = origin(right, hop)
                zcopy(piece, shard, right, hop).wait_recv()
                if hop < PLANES - 1:

                    @pl.when(can(right))
                    def _():
                        zcopy(piece, shard, right, hop + 1).start()

                ycopy(piece, shard, (0 if right else 3) + hop - 1).start()

    def collect_own(piece):
        local(piece).wait()
        ycopy(piece, flip, 6).wait_recv()

    def collect_hop(piece, hop):
        for right in (True, False):

            @pl.when(arrived(right, hop))
            def _():
                shard = origin(right, hop) + flip - place
                ycopy(piece, shard, (0 if right else 3) + hop - 1).wait_recv()

    def collect(piece):
        collect_own(piece)
        for hop in range(1, PLANES):
            collect_hop(piece, hop)

    def settle(piece):
        ycopy(piece, place, 6, own(piece)).wait_send()
        for hop in range(1, PLANES):
            for right in (True, False):

                @pl.when(arrived(right, hop))
                def _():
                    ycopy(piece, origin(right, hop), (0 if right else 3) + hop - 1).wait_send()

        for hop in range(0, PLANES - 1):
            for right in (True, False):
                have = can(right) if hop == 0 else can(right) & arrived(right, hop)

                @pl.when(have)
                def _():
                    zcopy(piece, origin(right, hop), right, hop + 1).wait_send()

    for piece in (0, 1, 2):
        launch(piece)
    h_one = RowGather(h_one_all, gather_sent.at[0], gather_landed.at[0])
    h_two = RowGather(h_two_all, gather_sent.at[1], gather_landed.at[1])
    grads = RowGather(grad_all, gather_sent.at[2], gather_landed.at[2])
    own_rows = pl.ds(pl.multiple_of(ctx * rows, rows), rows)

    ids_wide = jnp.broadcast_to(ids_row_ref[...].astype(jnp.float32), (8, ids_row_ref.shape[1]))
    ids_col_ref[...] = ids_wide.T[:, 0:1].astype(jnp.int32)
    norm_one = centre_of(x_ref[...].astype(jnp.float32))
    for hop in (1, 2, 3):
        pump(0, hop)
    collect(0)
    count = small_ref.shape[0]

    def shard_vectors(shard):
        return small_all[pl.ds(pl.multiple_of(shard * count, count), count), :].astype(jnp.float32)

    vec_ref[...] = jnp.concatenate([shard_vectors(q) for q in range(8)], axis=1)
    low_vec, high_vec = shard_vectors(2 * ctx), shard_vectors(2 * ctx + 1)
    vec_ref[8:9, :] = jnp.concatenate(
        [low_vec[8 + i : 9 + i] for i in range(4)] + [high_vec[8 + i : 9 + i] for i in range(4)], axis=1
    )
    h_one_all[own_rows, :] = (norm_one * vec_ref[0:1, :] + vec_ref[1:2, :]).astype(jnp.bfloat16)
    h_one.begin()
    live = (ids_col_ref[own_rows, :] >= 0).astype(jnp.float32)
    grad_all[own_rows, :] = (cot_ref[...].astype(jnp.float32) * live).astype(jnp.bfloat16)
    pump(1, 1)
    pump(2, 1)
    pump(1, 2)
    for piece in (3, 4, 5, 6):
        launch(piece)
    pump(2, 2)
    pump(1, 3)
    pump(2, 3)
    pump(3, 1)
    h_one.forward()
    grads.begin()
    collect(1)
    pump(4, 1)
    h_one.end()
    shifts = (
        jnp.concatenate([low_vec[2:3], high_vec[2:3]], axis=1),
        None,
        jnp.concatenate([low_vec[3:4], high_vec[3:4]], axis=1),
    )

    @pl.loop(0, 4)
    def _(step):
        some = pl.ds(pl.multiple_of(step * 256, 256), 256)
        for i in range(3):
            part = jnp.dot(h_one_all[some, :], qkvw_all[i], preferred_element_type=jnp.float32)
            if shifts[i] is not None:
                part = part + shifts[i]
            qkv_ref[some, i * width : (i + 1) * width] = part.astype(jnp.bfloat16)

    def send_mate(side):
        return remote(
            mate_out.at[0, side], mate_in.at[0, side], red_sent.at[3, side], red_landed.at[3, side], (place, mate)
        )

    send_cross = remote(
        cross_out.at[0], cross_in.at[0], red_sent.at[3, 2], red_landed.at[3, 2], (place, across)
    )

    def attend_rows(block):
        start, stop = block * rows, (block + 1) * rows
        for head in range(heads):
            lo, hi = head * HD, (head + 1) * HD
            queries = qkv_ref[start:stop, lo:hi] * jnp.asarray(factor, jnp.bfloat16)
            keys = qkv_ref[:stop, width + lo : width + hi]
            values = qkv_ref[:stop, 2 * width + lo : 2 * width + hi]
            scores = masked_scores(queries, keys, ids_row_ref, ids_col_ref, start, stop)
            top = jnp.max(scores, axis=0, keepdims=True)
            expo = jnp.exp(scores - top)
            summed = jnp.sum(expo, axis=0, keepdims=True)
            probs_low = (expo * (1.0 / summed)).astype(jnp.bfloat16)
            mixed_ref[start:stop, lo:hi] = contract_rows(values, probs_low).T.astype(jnp.bfloat16)
            lse_ref[head : head + 1, start:stop] = top + jnp.log(summed)

    def project_rows(block):
        side, owner_core = block // 2, block % 2
        part = jnp.dot(
            mixed_ref[block * rows : (block + 1) * rows, :], outw_all[...],
            preferred_element_type=jnp.float32,
        )

        @pl.when(core != owner_core)
        def _():
            mate_out[0, side] = part.astype(jnp.bfloat16)
            send_mate(side).start()

        @pl.when(core == owner_core)
        def _():
            out_acc[side * rows : (side + 1) * rows, :] = part

    def pass_rows(block):
        side, owner_core = block // 2, block % 2

        @pl.when(core == owner_core)
        def _():
            send_mate(side).wait_recv()
            total = out_acc[side * rows : (side + 1) * rows, :] + mate_in[0, side].astype(jnp.float32)

            @pl.when(x == side)
            def _():
                resid_ref[...] = total

            @pl.when(x != side)
            def _():
                cross_out[0] = total.astype(jnp.bfloat16)
                send_cross.start()

    attend_rows(3)
    pump(5, 1)
    pump(6, 1)
    collect(2)
    project_rows(3)
    attend_rows(1)
    project_rows(1)
    pass_rows(3)
    pump(3, 2)
    grads.forward()
    attend_rows(2)
    project_rows(2)
    pass_rows(1)
    pump(4, 2)
    attend_rows(0)
    project_rows(0)
    pass_rows(2)
    pass_rows(0)
    pump(5, 2)
    send_cross.wait_recv()
    resid = (
        x_ref[...].astype(jnp.float32)
        + (resid_ref[...] + cross_in[0].astype(jnp.float32))
        + vec_ref[4:5, :]
    )
    resid_ref[...] = resid
    h_two_all[own_rows, :] = (centre_of(resid) * vec_ref[5:6, :] + vec_ref[6:7, :]).astype(jnp.bfloat16)
    h_two.begin()
    pump(6, 2)
    out_acc[...] = jnp.zeros_like(out_acc)
    back_acc[...] = jnp.zeros_like(back_acc)
    pump(3, 3)
    pump(4, 3)
    send_cross.wait_send()
    for side in range(2):
        send_mate(side).wait_send()
    h_two.forward()
    pump(5, 3)
    pump(6, 3)
    for piece in (3, 4):
        collect(piece)
    for piece in (5, 6):
        collect_own(piece)
    h_two.end()
    grads.end()

    down_scatter = PlaneScatter(
        down_keep, down_out, down_yin, down_zin, down_sent, down_landed, down_zlanded
    )

    def up_scatter(block):
        return Scatter(
            up_keep.at[block], up_out.at[block], up_yin.at[block], up_zin.at[block],
            up_sent.at[block], up_landed.at[block],
        )

    def row_reduce(total, use):
        room = use % 2
        return RowReduce(
            total, mate_out.at[room], mate_in.at[room], cross_out.at[room], cross_in.at[room],
            red_sent.at[use], red_landed.at[use],
        )

    back = row_reduce(back_acc, 0)

    def plane_of(step):
        return lax.rem(step // 2 + z // 2, 2) * 2 + lax.rem(step + z, 2)

    @pl.loop(0, 4)
    def _(step):
        block = plane_of(step)
        for hop in range(1, PLANES):

            @pl.when(step == hop)
            def _():
                for piece in (5, 6):
                    collect_hop(piece, hop)

        some = pl.ds(pl.multiple_of(block * 256, 256), 256)
        up = up_all[:, some]
        down = down_all[some, :]
        sums = []
        for chunk in range(cap // CHUNK):
            here = slice(chunk * CHUNK, (chunk + 1) * CHUNK)
            u = jnp.dot(h_two_all[here, :], up, preferred_element_type=jnp.float32) + vec_ref[8:9, some]
            square = u * u
            bent = jnp.tanh(0.7978845608028654 * (u * (1.0 + 0.044715 * square)))
            half = 0.5 * (1.0 + bent)
            act = (u * half).astype(jnp.bfloat16)
            act_ref[here, :] = act
            slope = half + 0.5 * u * (1.0 - bent * bent) * (
                0.7978845608028654 * (1.0 + 0.134145 * square)
            )
            grad_pre = (contract_cols(grad_all[here, :], down) * slope).astype(jnp.bfloat16)
            grad_pre_ref[here, :] = grad_pre
            sums.append(jnp.sum(grad_pre.astype(jnp.float32), axis=0, keepdims=True))
            out_acc[here, :] += jnp.dot(act, down, preferred_element_type=jnp.float32)
            back_acc[here, :] += contract_cols(grad_pre, up)
        up_sums[block] = sum(sums)

        @pl.when(step == 3)
        def _():
            back.begin()

        down_part = contract_rows(act_ref[...], grad_all[...])
        down_scatter.store(block, down_part[:128], down_part[128:])
        down_scatter.begin(block)
        up_part = contract_rows(grad_pre_ref[...], h_two_all[...])
        scatter = up_scatter(block)
        for plane in range(PLANES):
            lo = plane * 256
            scatter.store(plane, up_part[:, lo : lo + 128], up_part[:, lo + 128 : lo + 256])
        scatter.begin()

    outs = row_reduce(out_acc, 1)
    outs.begin()
    back.relay()
    down_scatter.relay(plane_of(0))
    up_scatter(plane_of(0)).relay()
    down_scatter.relay(plane_of(1))
    up_scatter(plane_of(1)).relay()
    resid = resid_ref[...]
    grad_out = cot_ref[...].astype(jnp.float32) * (
        ids_col_ref[pl.ds(pl.multiple_of(ctx * rows, rows), rows), :] >= 0
    ).astype(jnp.float32)
    vec_out[...] = jnp.zeros_like(vec_out)

    def put_vector(row, vector):
        for q in range(8):
            vec_out[q, row : row + 1, :] = vector[:, q * 128 : (q + 1) * 128]

    def column_sum(values):
        return jnp.sum(values, axis=0, keepdims=True)

    put_vector(7, column_sum(grad_out))
    grad_h_two = back.finish()
    put_vector(6, column_sum(grad_h_two))
    put_vector(5, column_sum(grad_h_two * centre_of(resid)))
    grad_back = grad_out + norm_back(resid, grad_h_two * vec_ref[5:6, :])
    input_grad_ref[...] = grad_back
    resid_low = grad_back.astype(jnp.bfloat16)
    resid_all[pl.ds(pl.multiple_of(ctx * rows, rows), rows), :] = resid_low
    gather = RowGather(resid_all, gather_sent.at[3], gather_landed.at[3])
    gather.begin()
    outs.relay()
    put_vector(4, column_sum(resid_low.astype(jnp.float32)))
    for block in range(4):
        for i in range(2):
            vec_out[2 * ctx + block // 2, 8 + block % 2 * 2 + i : 9 + block % 2 * 2 + i, :] = up_sums[block][
                :, i * 128 : (i + 1) * 128
            ]
    down_scatter.relay(plane_of(2))
    up_scatter(plane_of(2)).relay()
    gather.forward()
    gather.end()
    grad_heads[...] = contract_cols(resid_all[...], outw_all[...]).astype(jnp.bfloat16)
    down_scatter.relay(plane_of(3))
    up_scatter(plane_of(3)).relay()
    out_scatter = Scatter(out_keep, out_out, out_yin, out_zin, out_sent, out_landed)
    out_part = contract_rows(mixed_ref[...], resid_all[...])
    for plane in range(PLANES):
        lo = plane * 64
        out_scatter.store(plane, out_part[lo : lo + 32], out_part[lo + 32 : lo + 64])
    out_scatter.begin()

    def attend_back_head(head):
        pair, side = head // 2, head % 2
        lo, hi = head * HD, (head + 1) * HD
        for start in reversed(range(0, cap, rows)):
            stop = start + rows
            queries = qkv_ref[start:stop, lo:hi] * jnp.asarray(factor, jnp.bfloat16)
            keys = qkv_ref[:stop, width + lo : width + hi]
            values = qkv_ref[:stop, 2 * width + lo : 2 * width + hi]
            grads = grad_heads[start:stop, lo:hi]
            scores = masked_scores(queries, keys, ids_row_ref, ids_col_ref, start, stop)
            probs = jnp.exp(scores - lse_ref[head : head + 1, start:stop])
            grad_probs = contract_cols(values, grads)
            delta = jnp.sum(probs * grad_probs, axis=0, keepdims=True)
            grad_scores = (probs * (grad_probs - delta)).astype(jnp.bfloat16)
            query_grad = contract_rows(keys, grad_scores).T * factor
            grad_qkv[pair, start:stop, side * HD : side * HD + HD] = query_grad.astype(jnp.bfloat16)
            key_grad = jnp.dot(grad_scores, queries, preferred_element_type=jnp.float32)
            value_grad = jnp.dot(probs.astype(jnp.bfloat16), grads, preferred_element_type=jnp.float32)
            if stop == cap:
                key_acc[...] = key_grad
                value_acc[...] = value_grad
            else:
                key_acc[:stop, :] += key_grad
                value_acc[:stop, :] += value_grad
        lo = 128 + side * HD
        grad_qkv[pair, :, lo : lo + HD] = key_acc[...].astype(jnp.bfloat16)
        grad_qkv[pair, :, lo + 128 : lo + 128 + HD] = value_acc[...].astype(jnp.bfloat16)

    def qkv_scatter(pair):
        return Scatter(
            qkv_keep.at[pair], qkv_out.at[pair], qkv_yin.at[pair], qkv_zin.at[pair],
            qkv_sent.at[pair], qkv_landed.at[pair],
        )

    def pair_grads(pair):
        part = contract_rows(grad_qkv[pair], h_one_all[...])
        scatter = qkv_scatter(pair)
        for plane in range(PLANES):
            lo = plane * 256
            scatter.store(plane, part[:, lo : lo + 128], part[:, lo + 128 : lo + 256])
        scatter.begin()
        sums = column_sum(grad_qkv[pair].astype(jnp.float32))
        vec_out[2 * ctx + pair, 2:3, :] = sums[:, :128]
        vec_out[2 * ctx + pair, 3:4, :] = sums[:, 256:]

    def pair_back(pair):
        weight = jnp.concatenate(
            [qkvw_all[i, :, pair * 128 : pair * 128 + 128] for i in range(3)], axis=1
        )
        for chunk in range(4):
            here = slice(chunk * 256, (chunk + 1) * 256)
            part = contract_cols(grad_qkv[pair, here, :], weight)
            if pair == 0:
                back_acc[here, :] = part
            else:
                back_acc[here, :] += part

    attend_back_head(0)
    attend_back_head(1)
    pair_grads(0)
    pair_back(0)
    out_scatter.relay()
    output_ref[...] = (resid_ref[...] + outs.finish() + vec_ref[7:8, :]).astype(jnp.bfloat16)
    attend_back_head(2)
    attend_back_head(3)
    pair_back(1)
    back.settle()
    last = row_reduce(back_acc, 2)
    last.begin()
    pair_grads(1)
    last.relay()
    qkv_scatter(0).relay()
    for block in range(4):
        up_grad_ref[:, block * 256 : (block + 1) * 256] = up_scatter(block).finish().T
    down_grad_ref[...] = down_scatter.finish()
    out_grad_ref[...] = out_scatter.finish()
    values = x_ref[...].astype(jnp.float32)
    qkv_scatter(1).relay()
    grad_h_one = last.finish()
    put_vector(0, column_sum(grad_h_one * centre_of(values)))
    put_vector(1, column_sum(grad_h_one))

    def vec_copy(step):
        target = lax.rem(place + step, 8)
        return remote(
            vec_out.at[target], vec_in.at[step - 1], vec_sent.at[step - 1], vec_landed.at[step - 1],
            (target, ctx),
        )

    def ctx_copy(step):
        return remote(
            vec_ctx.at[ctx], vec_ctx.at[ctx], ctx_sent.at[step - 1], ctx_landed.at[step - 1],
            (place, lax.rem(ctx + step, 4)),
        )

    for step in range(1, 8):
        vec_copy(step).start()
    input_grad_ref[...] += norm_back(values, grad_h_one * vec_ref[0:1, :])
    total = vec_out[place]
    for step in range(1, 8):
        vec_copy(step).wait_recv()
        total = total + vec_in[step - 1]
    vec_ctx[ctx] = total
    for step in range(1, 4):
        ctx_copy(step).start()
    for pair in range(2):
        done = qkv_scatter(pair).finish().T
        for i in range(3):
            qkv_grad_ref[i, :, pair * 128 : pair * 128 + 128] = done[:, i * 128 : (i + 1) * 128]
    for step in range(1, 4):
        source = lax.rem(ctx + 4 - step, 4)
        remote(
            vec_ctx.at[source], vec_ctx.at[source], ctx_sent.at[step - 1], ctx_landed.at[step - 1],
            (place, source),
        ).wait_recv()
    sums_ref[...] = ((vec_ctx[0] + vec_ctx[1]) + vec_ctx[2]) + vec_ctx[3]
    for use in (outs, last):
        use.settle()
    for block in range(4):
        up_scatter(block).settle()
    down_scatter.settle()
    out_scatter.settle()
    for pair in range(2):
        qkv_scatter(pair).settle()
    for step in range(1, 8):
        vec_copy(step).wait_send()
    for step in range(1, 4):
        ctx_copy(step).wait_send()
    for piece in range(7):
        settle(piece)


def block_pass(
    block_input, cotangent, doc_ids, ln1_gain, ln1_bias, qv_bias, out_bias, ln2_gain, ln2_bias, down_bias,
    up_bias, qkv_weight, out_weight, up_weight, down_weight, heads, factor,
):
    rows, model = block_input.shape
    cap = doc_ids.shape[1]
    width = heads * HD
    hidden = up_weight.shape[1]
    low, wide = jnp.bfloat16, jnp.float32
    anywhere = pl.BlockSpec(memory_space=pl.ANY)
    vmem = pl.BlockSpec(memory_space=pltpu.VMEM)
    shape = jax.ShapeDtypeStruct
    room, sems = pltpu.VMEM, pltpu.SemaphoreType.DMA

    def scatter_room(*lead_and_tail):
        lead, tail = lead_and_tail
        return [
            room(lead + (4,) + tail, wide),
            room(lead + (4,) + tail, low),
            room(lead + (4,) + tail, low),
            room(lead + (3,) + tail, low),
        ]

    return pl.pallas_call(
        functools.partial(block_kernel, heads, factor),
        out_shape=(
            shape((rows, model), low),
            shape((rows, model), wide),
            shape((3, model // 8, width), wide),
            shape((width // 8, model), wide),
            shape((model // 8, hidden), wide),
            shape((hidden // 8, model), wide),
            shape((16, 128), wide),
        ),
        in_specs=[vmem] * 11 + [anywhere] * 4,
        out_specs=(vmem,) * 7,
        scratch_shapes=[
            room((model, hidden), low),
            room((hidden, model), low),
            room((3, model, width), low),
            room((width, model), low),
            room((cap, model), low),
            room((16, model), wide),
            room((cap, model), low),
            room((cap, 3 * width), low),
            room((cap, width), low),
            room((heads, cap), wide),
            room((rows, model), wide),
            room((cap, model), low),
            room((cap, 1), jnp.int32),
            room((16, 128), low),
            room((8 * 16, 128), low),
            room((cap, model), wide),
            room((cap, model), wide),
            room((4, 1, 256), wide),
            room((cap, model), low),
            room((cap, width), low),
            room((2, cap, 384), low),
            room((cap, HD), wide),
            room((cap, HD), wide),
            room((cap, 256), low),
            room((cap, 256), low),
            room((2, 2, rows, model), low),
            room((2, 2, rows, model), low),
            room((2, rows, model), low),
            room((2, rows, model), low),
        ]
        + scatter_room((4,), (256, 128))
        + [
            room((4, 128, model), wide),
            room((4, 128, model), low),
            room((4, 128, model), low),
            room((3, 128, model), low),
        ]
        + scatter_room((), (32, model))
        + scatter_room((2,), (384, 128))
        + [
            room((8, 16, 128), wide),
            room((7, 16, 128), wide),
            room((4, 16, 128), wide),
            sems((7, 6)),
            sems((7, 6)),
            sems((7, 7)),
            sems((7, 7)),
            sems((7,)),
            sems((4, 3)),
            sems((4, 3)),
            sems((4, 3)),
            sems((4, 3)),
            sems((4, 4)),
            sems((4, 4)),
            sems((2, 4)),
            sems((4,)),
            sems((3,)),
            sems((4,)),
            sems((4,)),
            sems((2, 4)),
            sems((2, 4)),
            sems((7,)),
            sems((7,)),
            sems((3,)),
            sems((3,)),
        ],
        compiler_params=pltpu.CompilerParams(
            collective_id=1, has_side_effects=True, vmem_limit_bytes=62 * 2**20
        ),
        cost_estimate=pl.CostEstimate(
            flops=24 * cap * model * hidden,
            bytes_accessed=32 * 2**20,
            transcendentals=2 * cap * cap * heads,
        ),
        name="block_pass",
    )(
        block_input, cotangent, doc_ids, ln1_gain, ln1_bias, qv_bias, out_bias, ln2_gain, ln2_bias, down_bias,
        up_bias, qkv_weight, out_weight, up_weight, down_weight,
    )


def finish_kernel(*refs):
    wide_in, sums_ref = refs[:6], refs[6]
    wide_out, vectors, sem = refs[7:13], refs[13:21], refs[21]
    copies = [
        pltpu.make_async_copy(source, target, sem.at[i])
        for i, (source, target) in enumerate(zip(wide_in, wide_out))
    ]
    for copy in copies:
        copy.start()
    gain1, shift1, qv, oshift, gain2, shift2, dshift, ushift = vectors
    for ref, row in ((gain1, 0), (shift1, 1), (oshift, 4), (gain2, 5), (shift2, 6), (dshift, 7)):
        ref[...] = sums_ref[row]
    qv[...] = sums_ref[2:4, :]
    for i in range(4):
        ushift[i * 128 : (i + 1) * 128] = sums_ref[8 + i]
    for copy in copies:
        copy.wait()


def finish_pass(arrays, sums):
    anywhere = pl.BlockSpec(memory_space=pl.ANY)
    vmem = pl.BlockSpec(memory_space=pltpu.VMEM)
    shape = jax.ShapeDtypeStruct
    piece = sums.shape[1]
    sizes = [(piece,), (piece,), (2, piece), (piece,), (piece,), (piece,), (piece,), (4 * piece,)]
    return pl.pallas_call(
        finish_kernel,
        out_shape=tuple(shape(a.shape, a.dtype) for a in arrays)
        + tuple(shape(size, jnp.float32) for size in sizes),
        in_specs=[vmem] * 7,
        out_specs=(anywhere,) * 6 + (vmem,) * 8,
        scratch_shapes=[pltpu.SemaphoreType.DMA((6,))],
        name="finish_pass",
    )(*arrays, sums)


def on_device_general(
    block_input,
    ln1_gain,
    ln1_bias,
    qkv_weight,
    qv_bias,
    out_weight,
    out_bias,
    ln2_gain,
    ln2_bias,
    up_weight,
    up_bias,
    down_weight,
    down_bias,
    doc_ids,
    cotangent,
):
    shards = lax.axis_size("fsdp")
    small = jnp.concatenate(
        [
            ln1_gain,
            ln1_bias,
            qv_bias[0],
            qv_bias[1],
            out_bias,
            ln2_gain,
            ln2_bias,
            down_bias,
            up_bias,
        ]
    )
    rows = block_input.shape[0]
    model = block_input.shape[1]
    groups = lax.axis_size("ctx")
    place = lax.axis_index("ctx")
    capacity = rows * groups
    width = qkv_weight.shape[2]
    heads_here = width // HD
    hidden_here = up_weight.shape[1]
    factor = 1.0 / HD**0.5
    group_ids = doc_ids[0]
    own_ids = lax.dynamic_slice_in_dim(group_ids, place * rows, rows)
    input_all = gather_rows(block_input)
    qkv_rows = qkv_weight.shape[0]
    small_rows = -(-small.shape[0] // (3 * width * 16)) * 16
    first = jnp.concatenate(
        [
            qkv_weight.reshape(qkv_rows, 3 * width),
            jnp.pad(small, (0, small_rows * 3 * width - small.shape[0])).reshape(
                small_rows, 3 * width
            ),
        ]
    )
    first_all = gather_weight(first)
    small_all = first_all[:, qkv_rows:].reshape(shards, -1)[:, : small.shape[0]]
    piece = model // shards
    gain_one, shift_one, query_shift, value_shift, out_shift, gain_two, shift_two, down_shift = (
        small_all[:, i * piece : (i + 1) * piece].reshape(model) for i in range(8)
    )
    up_shift = small_all[:, 8 * piece :].reshape(-1)
    qv_full = jnp.stack([query_shift, value_shift])
    qkv_flat = first_all[:, :qkv_rows].reshape(model, 3 * width)
    out_full = gather_weight(out_weight).reshape(width, model)
    up_full = gather_weight(up_weight).reshape(model, hidden_here)
    down_full = gather_weight(down_weight).reshape(hidden_here, model)
    cot_all = gather_rows(cotangent)
    qv_here = lax.dynamic_slice_in_dim(qv_full.astype(jnp.float32), place * width, width, 1)
    qkv_shift = jnp.concatenate([qv_here[0], jnp.zeros((width,), jnp.float32), qv_here[1]])
    up_here = lax.dynamic_slice_in_dim(
        up_shift.astype(jnp.float32), place * hidden_here, hidden_here, 0
    )
    input_float = block_input.astype(jnp.float32)
    norm_one_all = normalize(input_all.astype(jnp.float32))
    h_one_all = (norm_one_all * gain_one + shift_one).astype(jnp.bfloat16)
    qkv_proj = project(h_one_all, qkv_flat)
    qkv = (qkv_proj + qkv_shift).astype(jnp.bfloat16)
    mixed_all, log_sums = attend(qkv, group_ids, heads_here, factor)
    out_part = project(mixed_all, out_full)
    resid = input_float + reduce_rows(out_part) + out_shift
    norm_two = normalize(resid)
    h_two = (norm_two * gain_two + shift_two).astype(jnp.bfloat16)
    h_two_all = gather_rows(h_two)
    live = (own_ids >= 0).astype(jnp.float32)
    grad_out = cotangent.astype(jnp.float32) * live[:, None]
    grad_low = grad_out.astype(jnp.bfloat16)
    down_shift_grad = jnp.sum(grad_low.astype(jnp.float32), axis=0)
    grad_all = jnp.where(group_ids[:, None] >= 0, cot_all, jnp.zeros_like(cot_all))
    act_low, grad_pre, up_sums, down_part, back_part = mlp(
        h_two_all, grad_all, up_full, up_here, down_full
    )
    grad_h_two = reduce_rows(back_part)
    output = (resid + reduce_rows(down_part) + down_shift).astype(jnp.bfloat16)
    down_grad = weight_grad(act_low, grad_all)
    up_grad = weight_grad(h_two_all, grad_pre)
    up_sums = up_sums[0]
    up_shift_grad = lax.dynamic_update_slice_in_dim(
        jnp.zeros((FF,), jnp.float32), up_sums, place * hidden_here, 0
    )
    gain_two_grad = jnp.sum(grad_h_two * norm_two, axis=0)
    shift_two_grad = jnp.sum(grad_h_two, axis=0)
    unused_two, norm_back_two = jax.vjp(normalize, resid)
    grad_resid = grad_out + norm_back_two(grad_h_two * gain_two.astype(jnp.float32))[0]
    resid_low = grad_resid.astype(jnp.bfloat16)
    out_shift_grad = jnp.sum(resid_low.astype(jnp.float32), axis=0)
    resid_all = gather_rows(resid_low)
    out_grad = weight_grad(mixed_all, resid_all)
    grad_heads = project_back(resid_all, out_full).astype(jnp.bfloat16)
    grad_qkv = attend_back(qkv, grad_heads, log_sums, group_ids, heads_here, factor)
    qkv_grad = weight_grad(h_one_all, grad_qkv).reshape(qkv_weight.shape[0], 3, width)
    column_sums = jnp.sum(grad_qkv.astype(jnp.float32), axis=0).reshape(3, width)
    qv_local = jnp.stack([column_sums[0], column_sums[2]])
    qv_grad = lax.dynamic_update_slice_in_dim(
        jnp.zeros((2, model), jnp.float32), qv_local, place * width, 1
    )
    grad_h_one_part = project_back(grad_qkv, qkv_flat)
    gain_one_grad = jnp.sum(grad_h_one_part * norm_one_all, axis=0)
    shift_one_grad = jnp.sum(grad_h_one_part, axis=0)
    grad_h_one = reduce_rows(grad_h_one_part)
    unused_one, norm_back_one = jax.vjp(normalize, input_float)
    input_grad = grad_resid + norm_back_one(grad_h_one * gain_one.astype(jnp.float32))[0]
    packed = jnp.concatenate(
        [
            part.reshape(shards, -1)
            for part in (
                gain_one_grad,
                shift_one_grad,
                qv_grad[0],
                qv_grad[1],
                out_shift_grad,
                gain_two_grad,
                shift_two_grad,
                down_shift_grad,
                up_shift_grad,
            )
        ],
        1,
    )
    sums = sum_ctx(scatter_fsdp(packed.reshape(shards, -1, 128), jnp.float32)).reshape(-1)
    (
        gain_one_sum,
        shift_one_sum,
        query_sum,
        value_sum,
        out_shift_sum,
        gain_two_sum,
        shift_two_sum,
        down_shift_sum,
    ) = (sums[i * piece : (i + 1) * piece] for i in range(8))
    qv_sum = jnp.stack([query_sum, value_sum])
    up_shift_sum = sums[8 * piece :]
    return (
        output,
        input_grad,
        gain_one_sum,
        shift_one_sum,
        qkv_grad,
        qv_sum,
        out_grad,
        out_shift_sum,
        gain_two_sum,
        shift_two_sum,
        up_grad,
        up_shift_sum,
        down_grad,
        down_shift_sum,
    )


def on_device(
    block_input,
    ln1_gain,
    ln1_bias,
    qkv_weight,
    qv_bias,
    out_weight,
    out_bias,
    ln2_gain,
    ln2_bias,
    up_weight,
    up_bias,
    down_weight,
    down_bias,
    doc_ids,
    cotangent,
):
    model = block_input.shape[1]
    if lax.axis_size("fsdp") != 8 or lax.axis_size("ctx") != 4:
        return on_device_general(
            block_input, ln1_gain, ln1_bias, qkv_weight, qv_bias, out_weight, out_bias, ln2_gain,
            ln2_bias, up_weight, up_bias, down_weight, down_bias, doc_ids, cotangent,
        )
    width = qkv_weight.shape[2]
    heads_here = width // HD
    factor = 1.0 / HD**0.5
    *grads, sums = block_pass(
        block_input, cotangent, doc_ids, ln1_gain, ln1_bias, qv_bias, out_bias, ln2_gain, ln2_bias,
        down_bias, up_bias, qkv_weight.transpose(1, 0, 2), out_weight, up_weight, down_weight, heads_here,
        factor,
    )
    (
        output, input_grad, qkv_grad, out_grad, up_grad, down_grad, gain_one_sum, shift_one_sum, qv_sum,
        out_shift_sum, gain_two_sum, shift_two_sum, down_shift_sum, up_shift_sum,
    ) = finish_pass(grads, sums)
    return (
        output,
        input_grad,
        gain_one_sum,
        shift_one_sum,
        qkv_grad.transpose(1, 0, 2),
        qv_sum,
        out_grad,
        out_shift_sum,
        gain_two_sum,
        shift_two_sum,
        up_grad,
        up_shift_sum,
        down_grad,
        down_shift_sum,
    )


def solution(mesh):
    placed = (
        P(("fsdp", "ctx"), None),
        P("fsdp"),
        P("fsdp"),
        P("fsdp", None, "ctx"),
        P(None, "fsdp"),
        P(("ctx", "fsdp"), None),
        P("fsdp"),
        P("fsdp"),
        P("fsdp"),
        P("fsdp", "ctx"),
        P("fsdp"),
        P(("ctx", "fsdp"), None),
        P("fsdp"),
        P("fsdp", None),
        P(("fsdp", "ctx"), None),
    )
    return jax.shard_map(
        on_device,
        mesh=mesh,
        in_specs=placed,
        out_specs=(
            P(("fsdp", "ctx"), None),
            P(("fsdp", "ctx"), None),
            P("fsdp"),
            P("fsdp"),
            P("fsdp", None, "ctx"),
            P(None, "fsdp"),
            P(("ctx", "fsdp"), None),
            P("fsdp"),
            P("fsdp"),
            P("fsdp"),
            P("fsdp", "ctx"),
            P("fsdp"),
            P(("ctx", "fsdp"), None),
            P("fsdp"),
        ),
        check_vma=False,
    )
```

```python
import functools

import jax
import jax.numpy as jnp
from jax import lax
from jax.experimental import pallas as pl
from jax.experimental.pallas import tpu as pltpu
from jax.sharding import PartitionSpec as P

HD = 64
FF = 4096


eps = 1e-05


def normalize(values):
    centre = values - jnp.mean(values, axis=-1, keepdims=True)
    spread = jnp.mean(centre * centre, axis=-1, keepdims=True)
    return centre * lax.rsqrt(spread + eps)


def contract_rows(left, right):
    return lax.dot_general(
        left, right, (((0,), (0,)), ((), ())), preferred_element_type=jnp.float32
    )


def contract_cols(left, right):
    return lax.dot_general(
        left, right, (((1,), (1,)), ((), ())), preferred_element_type=jnp.float32
    )


def split_fsdp():
    total = lax.axis_size("fsdp")
    inner = 2 if total <= 8 else 8
    return total // inner, inner


def move_fsdp(values, outer_step, inner_step):
    outer, inner = split_fsdp()
    pairs = [
        (a * inner + b, (a + outer_step) % outer * inner + (b + inner_step) % inner)
        for a in range(outer)
        for b in range(inner)
    ]
    return lax.ppermute(values, "fsdp", pairs)


def move_ctx(values, chip_step, core_step):
    chips = lax.axis_size("ctx") // 2
    pairs = [
        (x * 2 + c, (x + chip_step) % chips * 2 + (c + core_step) % 2)
        for x in range(chips)
        for c in range(2)
    ]
    return lax.ppermute(values, "ctx", pairs)


def put(buffer, values, place, axis):
    return lax.dynamic_update_index_in_dim(buffer, values, place, axis)


def pick(buffer, place, axis):
    return lax.dynamic_index_in_dim(buffer, place, axis, keepdims=False)


def gather_weight(shard):
    outer, inner = split_fsdp()
    place = lax.axis_index("fsdp")
    a, b = place // inner, place % inner
    held = put(jnp.zeros((outer,) + shard.shape, shard.dtype), shard, a, 0)
    for step in range(1, outer):
        held = put(held, move_fsdp(shard, step, 0), (a + outer - step) % outer, 0)
    if inner == 2:
        other = move_fsdp(held, 0, 1)
        first = b == 0
        whole = jnp.stack([jnp.where(first, held, other), jnp.where(first, other, held)], 1)
    else:
        whole = put(jnp.zeros((outer, inner) + shard.shape, shard.dtype), held, b, 1)
        for step in range(1, inner):
            whole = put(whole, move_fsdp(held, 0, step), (b + inner - step) % inner, 1)
    return whole.reshape((outer * inner,) + shard.shape)


def scatter_fsdp(parts, sent_type):
    outer, inner = split_fsdp()
    place = lax.axis_index("fsdp")
    a, b = place // inner, place % inner
    parts = parts.reshape((outer, inner) + parts.shape[1:])
    held = pick(parts, b, 1).astype(jnp.float32)
    for step in range(1, inner):
        sent = pick(parts, (b + step) % inner, 1).astype(sent_type)
        held = held + move_fsdp(sent, 0, step).astype(jnp.float32)
    summed = pick(held, a, 0)
    for step in range(1, outer):
        sent = pick(held, (a + step) % outer, 0).astype(sent_type)
        summed = summed + move_fsdp(sent, step, 0).astype(jnp.float32)
    return summed


def gather_rows(values):
    groups = lax.axis_size("ctx")
    chips = groups // 2
    place = lax.axis_index("ctx")
    x, core = place // 2, place % 2
    whole = jnp.zeros((groups,) + values.shape, values.dtype)
    for step in range(chips):
        got = values if step == 0 else move_ctx(values, step, 0)
        origin = (x + chips - step) % chips * 2
        whole = put(whole, got, origin + core, 0)
        whole = put(whole, move_ctx(got, 0, 1), origin + 1 - core, 0)
    return whole.reshape((groups * values.shape[0],) + values.shape[1:])


def reduce_rows(parts):
    groups = lax.axis_size("ctx")
    chips = groups // 2
    place = lax.axis_index("ctx")
    x, core = place // 2, place % 2
    parts = parts.reshape((chips, 2, parts.shape[0] // groups) + parts.shape[1:])
    sent = pick(parts, 1 - core, 1).astype(jnp.bfloat16)
    held = pick(parts, core, 1).astype(jnp.float32) + move_ctx(sent, 0, 1).astype(jnp.float32)
    summed = pick(held, x, 0)
    for step in range(1, chips):
        sent = pick(held, (x + step) % chips, 0).astype(jnp.bfloat16)
        summed = summed + move_ctx(sent, step, 0).astype(jnp.float32)
    return summed


def sum_ctx(values):
    chips = lax.axis_size("ctx") // 2
    total = values + move_ctx(values, 0, 1)
    whole = total
    for step in range(1, chips):
        whole = whole + move_ctx(total, step, 0)
    return whole


def project(inputs, weight):
    return jnp.dot(inputs, weight, preferred_element_type=jnp.float32)


def project_back(grad_low, weight):
    return contract_cols(grad_low, weight)


def weight_grad(inputs, grad_low):
    shards = lax.axis_size("fsdp")
    full = contract_rows(inputs, grad_low)
    return scatter_fsdp(
        full.reshape(shards, full.shape[0] // shards, full.shape[1]), jnp.bfloat16
    )


BLOCK = 256
MASKED = -1000000000.0


def masked_scores(queries, keys, ids_row_ref, ids_col_ref, start, stop):
    scores = contract_cols(keys, queries)
    same = ids_col_ref[:stop, :] == ids_row_ref[:, start:stop]
    key_place = lax.broadcasted_iota(jnp.int32, scores.shape, 0)
    query_place = lax.broadcasted_iota(jnp.int32, scores.shape, 1) + start
    return jnp.where(same & (key_place <= query_place), scores, MASKED)


def attend_kernel(heads, block, factor, qkv_ref, ids_row_ref, ids_col_ref, out_ref, lse_ref):
    rows = qkv_ref.shape[0]
    width = heads * HD
    for start in range(0, rows, block):
        stop = start + block
        for head in range(heads):
            lo, hi = head * HD, (head + 1) * HD
            queries = qkv_ref[start:stop, lo:hi] * jnp.asarray(factor, jnp.bfloat16)
            keys = qkv_ref[:stop, width + lo : width + hi]
            values = qkv_ref[:stop, 2 * width + lo : 2 * width + hi]
            scores = masked_scores(queries, keys, ids_row_ref, ids_col_ref, start, stop)
            top = jnp.max(scores, axis=0, keepdims=True)
            expo = jnp.exp(scores - top)
            summed = jnp.sum(expo, axis=0, keepdims=True)
            probs_low = (expo * (1.0 / summed)).astype(jnp.bfloat16)
            out_ref[start:stop, lo:hi] = contract_rows(values, probs_low).T.astype(jnp.bfloat16)
            lse_ref[head : head + 1, start:stop] = top + jnp.log(summed)


def attend_back_kernel(
    heads, block, factor, qkv_ref, grad_ref, lse_ref, ids_row_ref, ids_col_ref, out_ref, key_acc, value_acc
):
    rows = qkv_ref.shape[0]
    width = heads * HD
    for head in range(heads):
        lo, hi = head * HD, (head + 1) * HD
        for start in reversed(range(0, rows, block)):
            stop = start + block
            queries = qkv_ref[start:stop, lo:hi] * jnp.asarray(factor, jnp.bfloat16)
            keys = qkv_ref[:stop, width + lo : width + hi]
            values = qkv_ref[:stop, 2 * width + lo : 2 * width + hi]
            grads = grad_ref[start:stop, lo:hi]
            scores = masked_scores(queries, keys, ids_row_ref, ids_col_ref, start, stop)
            probs = jnp.exp(scores - lse_ref[head : head + 1, start:stop])
            grad_probs = contract_cols(values, grads)
            delta = jnp.sum(probs * grad_probs, axis=0, keepdims=True)
            grad_scores = (probs * (grad_probs - delta)).astype(jnp.bfloat16)
            query_grad = contract_rows(keys, grad_scores).T * factor
            out_ref[start:stop, lo:hi] = query_grad.astype(jnp.bfloat16)
            key_grad = jnp.dot(grad_scores, queries, preferred_element_type=jnp.float32)
            value_grad = jnp.dot(
                probs.astype(jnp.bfloat16), grads, preferred_element_type=jnp.float32
            )
            if stop == rows:
                key_acc[...] = key_grad
                value_acc[...] = value_grad
            else:
                key_acc[:stop, :] += key_grad
                value_acc[:stop, :] += value_grad
        out_ref[:, width + lo : width + hi] = key_acc[...].astype(jnp.bfloat16)
        out_ref[:, 2 * width + lo : 2 * width + hi] = value_acc[...].astype(jnp.bfloat16)


def attend(qkv, seq_ids, heads, factor):
    rows = qkv.shape[0]
    block = min(BLOCK, rows)
    return pl.pallas_call(
        functools.partial(attend_kernel, heads, block, factor),
        out_shape=(
            jax.ShapeDtypeStruct((rows, heads * HD), jnp.bfloat16),
            jax.ShapeDtypeStruct((heads, rows), jnp.float32),
        ),
        compiler_params=pltpu.CompilerParams(vmem_limit_bytes=40 * 2**20),
        cost_estimate=pl.CostEstimate(
            flops=4 * rows * rows * 256 * heads,
            bytes_accessed=8 * rows * heads * HD,
            transcendentals=rows * rows * heads,
        ),
        name="attend",
    )(qkv, seq_ids[None, :], seq_ids[:, None])


def attend_back(qkv, grads, log_sums, seq_ids, heads, factor):
    rows = qkv.shape[0]
    block = min(BLOCK, rows)
    return pl.pallas_call(
        functools.partial(attend_back_kernel, heads, block, factor),
        out_shape=jax.ShapeDtypeStruct(qkv.shape, jnp.bfloat16),
        scratch_shapes=[pltpu.VMEM((rows, HD), jnp.float32)] * 2,
        compiler_params=pltpu.CompilerParams(vmem_limit_bytes=40 * 2**20),
        cost_estimate=pl.CostEstimate(
            flops=10 * rows * rows * 256 * heads,
            bytes_accessed=14 * rows * heads * HD,
            transcendentals=rows * rows * heads,
        ),
        name="attend_back",
    )(qkv, grads, log_sums, seq_ids[None, :], seq_ids[:, None])


def mlp_kernel(
    in_ref,
    grad_ref,
    up_ref,
    shift_ref,
    down_ref,
    act_ref,
    pre_ref,
    sums_ref,
    out_ref,
    back_ref,
    out_acc,
    back_acc,
):
    step = pl.program_id(0)
    u = jnp.dot(in_ref[...], up_ref[...], preferred_element_type=jnp.float32) + shift_ref[...]
    square = u * u
    bent = jnp.tanh(0.7978845608028654 * (u * (1.0 + 0.044715 * square)))
    half = 0.5 * (1.0 + bent)
    act = (u * half).astype(jnp.bfloat16)
    act_ref[...] = act
    slope = half + 0.5 * u * (1.0 - bent * bent) * (
        0.7978845608028654 * (1.0 + 0.134145 * square)
    )
    grad_pre = (contract_cols(grad_ref[...], down_ref[...]) * slope).astype(jnp.bfloat16)
    pre_ref[...] = grad_pre
    sums_ref[...] = jnp.sum(grad_pre.astype(jnp.float32), axis=0, keepdims=True)
    out_part = jnp.dot(act, down_ref[...], preferred_element_type=jnp.float32)
    back_part = contract_cols(grad_pre, up_ref[...])

    @pl.when(step == 0)
    def _():
        out_acc[...] = out_part
        back_acc[...] = back_part

    @pl.when(step > 0)
    def _():
        out_acc[...] += out_part
        back_acc[...] += back_part

    @pl.when(step == pl.num_programs(0) - 1)
    def _():
        out_ref[...] = out_acc[...].astype(jnp.bfloat16)
        back_ref[...] = back_acc[...].astype(jnp.bfloat16)


def mlp(inputs, grads, up, shift, down):
    rows, model = inputs.shape
    hidden = up.shape[1]
    block = min(256, hidden)
    whole = pl.BlockSpec((rows, model), lambda i: (0, 0))
    columns = pl.BlockSpec((rows, block), lambda i: (0, i))
    line = pl.BlockSpec((1, block), lambda i: (0, i))
    return pl.pallas_call(
        mlp_kernel,
        grid=(hidden // block,),
        in_specs=[
            whole,
            whole,
            pl.BlockSpec((model, block), lambda i: (0, i)),
            line,
            pl.BlockSpec((block, model), lambda i: (i, 0)),
        ],
        out_specs=(columns, columns, line, whole, whole),
        out_shape=(
            jax.ShapeDtypeStruct((rows, hidden), jnp.bfloat16),
            jax.ShapeDtypeStruct((rows, hidden), jnp.bfloat16),
            jax.ShapeDtypeStruct((1, hidden), jnp.float32),
            jax.ShapeDtypeStruct((rows, model), jnp.bfloat16),
            jax.ShapeDtypeStruct((rows, model), jnp.bfloat16),
        ),
        scratch_shapes=[pltpu.VMEM((rows, model), jnp.float32)] * 2,
        compiler_params=pltpu.CompilerParams(vmem_limit_bytes=52 * 2**20),
        cost_estimate=pl.CostEstimate(
            flops=8 * rows * model * hidden,
            bytes_accessed=8 * rows * model + 4 * rows * hidden + 4 * model * hidden,
            transcendentals=rows * hidden,
        ),
        name="mlp",
    )(inputs, grads, up, shift[None, :], down)


MESH = pl.DeviceIdType.MESH
PLANES = 4


def remote(source, target, sent, landed, device):
    return pltpu.make_async_remote_copy(
        src_ref=source,
        dst_ref=target,
        send_sem=sent,
        recv_sem=landed,
        device_id=device,
        device_id_type=MESH,
    )


def seat():
    place = lax.axis_index("fsdp")
    ctx = lax.axis_index("ctx")
    z, y = place // 2, lax.rem(place, 2)
    x, core = ctx // 2, lax.rem(ctx, 2)
    return place, ctx, z, y, x, core


def centre_of(values):
    centre = values - jnp.mean(values, axis=-1, keepdims=True)
    spread = jnp.mean(centre * centre, axis=-1, keepdims=True)
    return centre * lax.rsqrt(spread + eps)


class RowGather:
    def __init__(self, target, sent, landed):
        self.target, self.sent, self.landed = target, sent, landed
        self.place, self.ctx, z, y, x, core = seat()
        self.mate = self.ctx + 1 - 2 * core
        self.across = self.ctx + 2 - 4 * x
        self.rows = target.shape[0] // 4
        self.sends = []

    def at(self, ctx):
        return self.target.at[pl.ds(pl.multiple_of(ctx * self.rows, self.rows), self.rows), :]

    def move(self, ctx, slot, device):
        return remote(
            self.at(ctx), self.at(ctx), self.sent.at[slot], self.landed.at[slot],
            (self.place, device),
        )

    def send(self, ctx, slot, device):
        copy = self.move(ctx, slot, device)
        copy.start()
        self.sends.append(copy)

    def begin(self):
        self.send(self.ctx, 1, self.across)
        self.send(self.ctx, 0, self.mate)

    def forward(self):
        self.move(self.across, 1, self.across).wait_recv()
        self.send(self.across, 2, self.mate)

    def end(self):
        opposite = self.across + self.mate - self.ctx
        self.move(self.mate, 0, self.mate).wait_recv()
        self.move(opposite, 2, self.mate).wait_recv()
        for copy in self.sends:
            copy.wait_send()


CHUNK = 512


class RowReduce:
    def __init__(self, total, mate_out, mate_in, cross_out, cross_in, sent, landed):
        self.total, self.mate_out, self.mate_in = total, mate_out, mate_in
        self.cross_out, self.cross_in, self.sent, self.landed = cross_out, cross_in, sent, landed
        self.place, self.ctx, z, y, self.x, self.core = seat()
        self.rows = total.shape[0] // 4

    def part(self, side, core):
        first = pl.multiple_of((side * 2 + core) * self.rows, self.rows)
        return self.total[pl.ds(first, self.rows), :]

    def mate_copy(self, slot):
        return remote(
            self.mate_out.at[slot], self.mate_in.at[slot], self.sent.at[slot], self.landed.at[slot],
            (self.place, self.ctx + 1 - 2 * self.core),
        )

    def cross_copy(self):
        return remote(
            self.cross_out, self.cross_in, self.sent.at[2], self.landed.at[2],
            (self.place, self.ctx + 2 - 4 * self.x),
        )

    def begin_slot(self, slot):
        side = self.x if slot else 1 - self.x
        self.mate_out[slot] = self.part(side, 1 - self.core).astype(jnp.bfloat16)
        self.mate_copy(slot).start()

    def begin(self):
        self.begin_slot(0)
        self.begin_slot(1)

    def relay(self):
        self.mate_copy(0).wait_recv()
        self.cross_out[...] = (
            self.part(1 - self.x, self.core) + self.mate_in[0].astype(jnp.float32)
        ).astype(jnp.bfloat16)
        self.cross_copy().start()

    def finish(self):
        self.mate_copy(1).wait_recv()
        held = self.part(self.x, self.core) + self.mate_in[1].astype(jnp.float32)
        self.cross_copy().wait_recv()
        return held + self.cross_in[...].astype(jnp.float32)

    def settle(self):
        for slot in range(2):
            self.mate_copy(slot).wait_send()
        self.cross_copy().wait_send()


class Scatter:
    def __init__(self, keep, out, yin, zin, sent, landed):
        self.keep, self.yout, self.yin, self.zout, self.zin = keep, out, yin, out, zin
        self.sent, self.landed = sent, landed
        self.place, self.ctx, self.z, self.y, x, core = seat()

    def store(self, plane, even, odd):
        first = self.y == 0
        self.keep[plane] = jnp.where(first, even, odd)
        self.yout[plane] = jnp.where(first, odd, even).astype(jnp.bfloat16)

    def ycopy(self):
        return remote(
            self.yout, self.yin, self.sent.at[0], self.landed.at[0], (self.place + 1 - 2 * self.y, self.ctx)
        )

    def zcopy(self, step):
        return remote(
            self.zout.at[step - 1], self.zin.at[step - 1], self.sent.at[step], self.landed.at[step],
            (lax.rem(self.z + step, PLANES) * 2 + self.y, self.ctx),
        )

    def begin(self):
        self.ycopy().start()

    def relay(self):
        self.ycopy().wait()
        for step in (2, 1, 3):
            plane = lax.rem(self.z + step, PLANES)
            self.zout[step - 1] = (self.keep[plane] + self.yin[plane].astype(jnp.float32)).astype(
                jnp.bfloat16
            )
            self.zcopy(step).start()

    def finish(self):
        total = self.keep[self.z] + self.yin[self.z].astype(jnp.float32)
        for step in (1, 3, 2):
            self.zcopy(step).wait_recv()
            total = total + self.zin[step - 1].astype(jnp.float32)
        return total

    def settle(self):
        for step in (1, 2, 3):
            self.zcopy(step).wait_send()


class PlaneScatter:
    def __init__(self, keep, out, yin, zin, sent, landed, zlanded):
        self.keep, self.yout, self.yin, self.zout, self.zin = keep, out, yin, out, zin
        self.sent, self.landed, self.zlanded = sent, landed, zlanded
        self.place, self.ctx, self.z, self.y, x, core = seat()

    def store(self, block, even, odd):
        first = self.y == 0
        self.keep[block] = jnp.where(first, even, odd)
        self.yout[block] = jnp.where(first, odd, even).astype(jnp.bfloat16)

    def ycopy(self, block):
        return remote(
            self.yout.at[block], self.yin.at[block], self.sent.at[0, block], self.landed.at[block],
            (self.place + 1 - 2 * self.y, self.ctx),
        )

    def zcopy(self, block):
        slot = lax.rem(self.z - block + PLANES, PLANES) - 1
        return remote(
            self.zout.at[block], self.zin.at[slot], self.sent.at[1, block], self.zlanded.at[slot],
            (block * 2 + self.y, self.ctx),
        )

    def begin(self, block):
        self.ycopy(block).start()

    def relay(self, block):
        self.ycopy(block).wait()

        @pl.when(self.z != block)
        def _():
            self.zout[block] = (self.keep[block] + self.yin[block].astype(jnp.float32)).astype(jnp.bfloat16)
            self.zcopy(block).start()

    def finish(self):
        total = self.keep[self.z] + self.yin[self.z].astype(jnp.float32)
        for slot in range(3):
            remote(
                self.zin.at[slot], self.zin.at[slot], self.sent.at[1, 0], self.zlanded.at[slot],
                (self.place + 1 - 2 * self.y, self.ctx),
            ).wait_recv()
            total = total + self.zin[slot].astype(jnp.float32)
        return total

    def settle(self):
        for block in range(PLANES):

            @pl.when(self.z != block)
            def _():
                self.zcopy(block).wait_send()


def norm_back(values, grads):
    centre = values - jnp.mean(values, axis=-1, keepdims=True)
    scale = lax.rsqrt(jnp.mean(centre * centre, axis=-1, keepdims=True) + eps)
    unit = centre * scale
    along = jnp.mean(grads * unit, axis=-1, keepdims=True)
    return (grads - jnp.mean(grads, axis=-1, keepdims=True) - unit * along) * scale


def block_kernel(
    heads, factor,
    x_ref, cot_ref, ids_row_ref, gain1_ref, shift1_ref, qv_ref, oshift_ref, gain2_ref, shift2_ref, dshift_ref,
    ushift_ref, qkvw_ref, outw_ref, upw_ref, downw_ref,
    output_ref, input_grad_ref, qkv_grad_ref, out_grad_ref, up_grad_ref, down_grad_ref, sums_ref,
    up_all, down_all, qkvw_all, outw_all, grad_all, vec_ref, h_one_all, qkv_ref, mixed_ref, lse_ref,
    resid_ref, h_two_all, ids_col_ref, small_ref, small_all,
    out_acc, back_acc, up_sums, resid_all, grad_heads, grad_qkv, key_acc, value_acc, act_ref, grad_pre_ref,
    mate_out, mate_in, cross_out, cross_in,
    up_keep, up_out, up_yin, up_zin, down_keep, down_out, down_yin, down_zin,
    out_keep, out_out, out_yin, out_zin, qkv_keep, qkv_out, qkv_yin, qkv_zin,
    vec_out, vec_in, vec_ctx,
    zsent, zlanded, ysent, ylanded, local_sem, gather_sent, gather_landed,
    red_sent, red_landed, up_sent, up_landed, down_sent, down_landed, down_zlanded, out_sent,
    out_landed, qkv_sent, qkv_landed, vec_sent, vec_landed, ctx_sent, ctx_landed,
):
    place, ctx, z, y, x, core = seat()
    flip = place + 1 - 2 * y
    mate = ctx + 1 - 2 * core
    across = ctx + 2 - 4 * x
    rows = x_ref.shape[0]
    width = heads * HD
    cap = h_two_all.shape[0]

    wide = lambda ref: ref[...].astype(jnp.float32).reshape(-1, 128)
    small_ref[...] = jnp.concatenate(
        [
            wide(gain1_ref), wide(shift1_ref), wide(qv_ref), wide(oshift_ref), wide(gain2_ref),
            wide(shift2_ref), wide(dshift_ref), wide(ushift_ref), jnp.zeros((4, 128), jnp.float32),
        ],
        axis=0,
    ).astype(jnp.bfloat16)
    barrier = pltpu.get_barrier_semaphore()

    for step in range(1, 8):
        pl.semaphore_signal(
            barrier, inc=1, device_id=(lax.rem(place + step, 8), ctx), device_id_type=MESH
        )
    for step in range(1, 4):
        pl.semaphore_signal(
            barrier, inc=1, device_id=(place, lax.rem(ctx + step, 4)), device_id_type=MESH
        )
    pl.semaphore_wait(barrier, 10)

    half = upw_ref.shape[0] // 2
    pieces = (
        (small_ref, small_all, 0, small_ref.shape[0]),
        (qkvw_ref, qkvw_all, 0, qkvw_ref.shape[1]),
        (outw_ref, outw_all, 0, outw_ref.shape[0]),
        (upw_ref, up_all, 0, half),
        (upw_ref, up_all, half, half),
        (downw_ref, down_all, 0, half),
        (downw_ref, down_all, half, half),
    )

    def spot(piece, shard):
        source, target, start, count = pieces[piece]
        if piece == 1:
            return target.at[:, pl.ds(pl.multiple_of(shard * count, count), count), :]
        first = pl.multiple_of(shard * source.shape[0] + start, count)
        return target.at[pl.ds(first, count), :]

    def zcopy(piece, shard, right, hop, source=None):
        slot = (0 if right else 3) + hop - 1
        spot_ = spot(piece, shard)
        device = (place + 2 if right else place - 2, ctx)
        return remote(
            spot_ if source is None else source, spot_, zsent.at[piece, slot], zlanded.at[piece, slot], device
        )

    def ycopy(piece, shard, slot, source=None):
        spot_ = spot(piece, shard)
        return remote(
            spot_ if source is None else source, spot_, ysent.at[piece, slot], ylanded.at[piece, slot],
            (flip, ctx),
        )

    def own(piece):
        source, target, start, count = pieces[piece]
        return source if piece == 1 else source.at[pl.ds(start, count), :]

    def can(right):
        return z < PLANES - 1 if right else z > 0

    def arrived(right, hop):
        return z >= hop if right else z < PLANES - hop

    def local(piece):
        return pltpu.make_async_copy(own(piece), spot(piece, place), local_sem.at[piece])

    def launch_z(piece):
        for right in (True, False):

            @pl.when(can(right))
            def _():
                zcopy(piece, place, right, 1, own(piece)).start()

    def launch_y(piece):
        ycopy(piece, place, 6, own(piece)).start()
        local(piece).start()

    def origin(right, hop):
        return place - 2 * hop if right else place + 2 * hop

    def pump(piece, hop):
        for right in (True, False):

            @pl.when(arrived(right, hop))
            def _():
                shard = origin(right, hop)
                zcopy(piece, shard, right, hop).wait_recv()
                if hop < PLANES - 1:

                    @pl.when(can(right))
                    def _():
                        zcopy(piece, shard, right, hop + 1).start()

                ycopy(piece, shard, (0 if right else 3) + hop - 1).start()

    def collect_own(piece):
        local(piece).wait()
        ycopy(piece, flip, 6).wait_recv()

    def collect_hop(piece, hop):
        for right in (True, False):

            @pl.when(arrived(right, hop))
            def _():
                shard = origin(right, hop) + flip - place
                ycopy(piece, shard, (0 if right else 3) + hop - 1).wait_recv()

    def collect(piece):
        collect_own(piece)
        for hop in range(1, PLANES):
            collect_hop(piece, hop)

    def settle(piece):
        ycopy(piece, place, 6, own(piece)).wait_send()
        for hop in range(1, PLANES):
            for right in (True, False):

                @pl.when(arrived(right, hop))
                def _():
                    ycopy(piece, origin(right, hop), (0 if right else 3) + hop - 1).wait_send()

        for hop in range(0, PLANES - 1):
            for right in (True, False):
                have = can(right) if hop == 0 else can(right) & arrived(right, hop)

                @pl.when(have)
                def _():
                    zcopy(piece, origin(right, hop), right, hop + 1).wait_send()

    for piece in (0, 1, 2):
        launch_z(piece)
        launch_y(piece)
    h_one = RowGather(h_one_all, gather_sent.at[0], gather_landed.at[0])
    h_two = RowGather(h_two_all, gather_sent.at[1], gather_landed.at[1])
    grads = RowGather(grad_all, gather_sent.at[2], gather_landed.at[2])
    own_rows = pl.ds(pl.multiple_of(ctx * rows, rows), rows)

    ids_wide = jnp.broadcast_to(ids_row_ref[...].astype(jnp.float32), (8, ids_row_ref.shape[1]))
    ids_col_ref[...] = ids_wide.T[:, 0:1].astype(jnp.int32)
    norm_one = centre_of(x_ref[...].astype(jnp.float32))
    for hop in (1, 2, 3):
        pump(0, hop)
    collect(0)
    count = small_ref.shape[0]

    def shard_vectors(shard):
        return small_all[pl.ds(pl.multiple_of(shard * count, count), count), :].astype(jnp.float32)

    vec_ref[...] = jnp.concatenate([shard_vectors(q) for q in range(8)], axis=1)
    low_vec, high_vec = shard_vectors(2 * ctx), shard_vectors(2 * ctx + 1)
    vec_ref[8:9, :] = jnp.concatenate(
        [low_vec[8 + i : 9 + i] for i in range(4)] + [high_vec[8 + i : 9 + i] for i in range(4)], axis=1
    )
    h_one_all[own_rows, :] = (norm_one * vec_ref[0:1, :] + vec_ref[1:2, :]).astype(jnp.bfloat16)
    h_one.begin()
    live = (ids_col_ref[own_rows, :] >= 0).astype(jnp.float32)
    grad_all[own_rows, :] = (cot_ref[...].astype(jnp.float32) * live).astype(jnp.bfloat16)
    pump(1, 1)
    pump(2, 1)
    pump(1, 2)
    pump(2, 2)
    for piece in (3, 4, 5, 6):
        launch_z(piece)
    pump(1, 3)
    pump(2, 3)
    for piece in (3, 4, 5, 6):
        launch_y(piece)
    pump(3, 1)
    h_one.forward()
    grads.begin()
    collect(1)
    pump(4, 1)
    h_one.end()
    shifts = (
        jnp.concatenate([low_vec[2:3], high_vec[2:3]], axis=1),
        None,
        jnp.concatenate([low_vec[3:4], high_vec[3:4]], axis=1),
    )

    @pl.loop(0, 4)
    def _(step):
        some = pl.ds(pl.multiple_of(step * 256, 256), 256)
        for i in range(3):
            part = jnp.dot(h_one_all[some, :], qkvw_all[i], preferred_element_type=jnp.float32)
            if shifts[i] is not None:
                part = part + shifts[i]
            qkv_ref[some, i * width : (i + 1) * width] = part.astype(jnp.bfloat16)

    def send_mate(side):
        return remote(
            mate_out.at[0, side], mate_in.at[0, side], red_sent.at[3, side], red_landed.at[3, side], (place, mate)
        )

    send_cross = remote(
        cross_out.at[0], cross_in.at[0], red_sent.at[3, 2], red_landed.at[3, 2], (place, across)
    )

    def attend_rows(block, first=0, end=heads):
        start, stop = block * rows, (block + 1) * rows
        for head in range(first, end):
            lo, hi = head * HD, (head + 1) * HD
            queries = qkv_ref[start:stop, lo:hi] * jnp.asarray(factor, jnp.bfloat16)
            keys = qkv_ref[:stop, width + lo : width + hi]
            values = qkv_ref[:stop, 2 * width + lo : 2 * width + hi]
            scores = masked_scores(queries, keys, ids_row_ref, ids_col_ref, start, stop)
            top = jnp.max(scores, axis=0, keepdims=True)
            expo = jnp.exp(scores - top)
            summed = jnp.sum(expo, axis=0, keepdims=True)
            probs_low = (expo * (1.0 / summed)).astype(jnp.bfloat16)
            mixed_ref[start:stop, lo:hi] = contract_rows(values, probs_low).T.astype(jnp.bfloat16)
            lse_ref[head : head + 1, start:stop] = top + jnp.log(summed)

    def project_rows(block):
        side, owner_core = block // 2, block % 2
        part = jnp.dot(
            mixed_ref[block * rows : (block + 1) * rows, :], outw_all[...],
            preferred_element_type=jnp.float32,
        )

        @pl.when(core != owner_core)
        def _():
            mate_out[0, side] = part.astype(jnp.bfloat16)
            send_mate(side).start()

        @pl.when(core == owner_core)
        def _():
            out_acc[side * rows : (side + 1) * rows, :] = part

    def pass_rows(block):
        side, owner_core = block // 2, block % 2

        @pl.when(core == owner_core)
        def _():
            send_mate(side).wait_recv()
            total = out_acc[side * rows : (side + 1) * rows, :] + mate_in[0, side].astype(jnp.float32)

            @pl.when(x == side)
            def _():
                resid_ref[...] = total

            @pl.when(x != side)
            def _():
                cross_out[0] = total.astype(jnp.bfloat16)
                send_cross.start()

    attend_rows(1)
    pump(5, 1)
    pump(6, 1)
    collect(2)
    project_rows(1)
    attend_rows(2)
    project_rows(2)
    pass_rows(1)
    pump(3, 2)
    attend_rows(0)
    project_rows(0)
    pass_rows(2)
    grads.forward()
    attend_rows(3, 0, 2)
    pass_rows(0)
    pump(4, 2)
    attend_rows(3, 2, 4)
    project_rows(3)
    pump(5, 2)
    pass_rows(3)
    send_cross.wait_recv()
    resid = (
        x_ref[...].astype(jnp.float32)
        + (resid_ref[...] + cross_in[0].astype(jnp.float32))
        + vec_ref[4:5, :]
    )
    resid_ref[...] = resid
    h_two_all[own_rows, :] = (centre_of(resid) * vec_ref[5:6, :] + vec_ref[6:7, :]).astype(jnp.bfloat16)
    h_two.begin()
    pump(6, 2)
    out_acc[...] = jnp.zeros_like(out_acc)
    back_acc[...] = jnp.zeros_like(back_acc)
    pump(3, 3)
    pump(4, 3)
    send_cross.wait_send()
    for side in range(2):
        send_mate(side).wait_send()
    h_two.forward()
    pump(5, 3)
    pump(6, 3)
    for piece in (3, 4):
        collect(piece)
    for piece in (5, 6):
        collect_own(piece)
    h_two.end()
    grads.end()

    down_scatter = PlaneScatter(
        down_keep, down_out, down_yin, down_zin, down_sent, down_landed, down_zlanded
    )

    def up_scatter(block):
        return Scatter(
            up_keep.at[block], up_out.at[block], up_yin.at[block], up_zin.at[block],
            up_sent.at[block], up_landed.at[block],
        )

    def row_reduce(total, use):
        room = use % 2
        return RowReduce(
            total, mate_out.at[room], mate_in.at[room], cross_out.at[room], cross_in.at[room],
            red_sent.at[use], red_landed.at[use],
        )

    back = row_reduce(back_acc, 0)

    def plane_of(step):
        return lax.rem(step // 2 + z // 2, 2) * 2 + lax.rem(step + z, 2)

    up_sums[...] = jnp.zeros_like(up_sums)

    def block_rows(block, slot, here):
        some = pl.ds(pl.multiple_of(block * 256, 256), 256)
        up = up_all[:, some]
        down = down_all[some, :]
        u = jnp.dot(h_two_all[here, :], up, preferred_element_type=jnp.float32) + vec_ref[8:9, some]
        square = u * u
        bent = jnp.tanh(u * (0.7978845608028654 + 0.035677408136300125 * square))
        half = 0.5 + 0.5 * bent
        wide_act = u * half
        act = wide_act.astype(jnp.bfloat16)
        act_ref[slot, here, :] = act
        slope = half + wide_act * (1.0 - bent) * (0.7978845608028654 + 0.1070322244089 * square)
        grad_pre = (contract_cols(grad_all[here, :], down) * slope).astype(jnp.bfloat16)
        grad_pre_ref[slot, here, :] = grad_pre
        up_sums[block] += jnp.sum(grad_pre.astype(jnp.float32), axis=0, keepdims=True)
        out_acc[here, :] += jnp.dot(act, down, preferred_element_type=jnp.float32)
        back_acc[here, :] += contract_cols(grad_pre, up)

    def block_grads(block, slot):
        down_part = contract_rows(act_ref[slot], grad_all[...])
        down_scatter.store(block, down_part[:128], down_part[128:])
        down_scatter.begin(block)
        up_part = contract_rows(grad_pre_ref[slot], h_two_all[...])
        scatter = up_scatter(block)
        for plane in range(PLANES):
            lo = plane * 256
            scatter.store(plane, up_part[:, lo : lo + 128], up_part[:, lo + 128 : lo + 256])
        scatter.begin()

    @pl.loop(0, 2)
    def _(step):
        @pl.when(step == 1)
        def _():
            for piece in (5, 6):
                collect_hop(piece, 1)

        block = plane_of(step)
        for chunk in range(cap // CHUNK):
            block_rows(block, step, slice(chunk * CHUNK, (chunk + 1) * CHUNK))
        block_grads(block, step)

    for piece in (5, 6):
        collect_hop(piece, 2)
        collect_hop(piece, 3)

    @pl.loop(0, 4)
    def _(turn):
        side = jnp.where(turn < 2, 1 - x, x)
        owner_core = jnp.where(lax.rem(turn, 2) == 0, 1 - core, core)
        here = pl.ds(pl.multiple_of((side * 2 + owner_core) * rows, rows), rows)
        for step in (2, 3):
            block_rows(plane_of(step), step - 2, here)

        for slot in range(2):

            @pl.when(turn == 2 * slot)
            def _():
                back.begin_slot(slot)

        @pl.when(turn == 1)
        def _():
            back.relay()

        @pl.when(turn == 2)
        def _():
            down_scatter.relay(plane_of(0))
            up_scatter(plane_of(0)).relay()

    outs = row_reduce(out_acc, 1)
    outs.begin()
    for step in (2, 3):
        block_grads(plane_of(step), step - 2)
    down_scatter.relay(plane_of(1))
    up_scatter(plane_of(1)).relay()
    resid = resid_ref[...]
    grad_out = cot_ref[...].astype(jnp.float32) * (
        ids_col_ref[pl.ds(pl.multiple_of(ctx * rows, rows), rows), :] >= 0
    ).astype(jnp.float32)
    vec_out[...] = jnp.zeros_like(vec_out)

    def put_vector(row, vector):
        for q in range(8):
            vec_out[q, row : row + 1, :] = vector[:, q * 128 : (q + 1) * 128]

    def column_sum(values):
        return jnp.sum(values, axis=0, keepdims=True)

    put_vector(7, column_sum(grad_out))
    grad_h_two = back.finish()
    put_vector(6, column_sum(grad_h_two))
    put_vector(5, column_sum(grad_h_two * centre_of(resid)))
    grad_back = grad_out + norm_back(resid, grad_h_two * vec_ref[5:6, :])
    input_grad_ref[...] = grad_back
    resid_low = grad_back.astype(jnp.bfloat16)
    resid_all[pl.ds(pl.multiple_of(ctx * rows, rows), rows), :] = resid_low
    gather = RowGather(resid_all, gather_sent.at[3], gather_landed.at[3])
    gather.begin()
    outs.relay()
    put_vector(4, column_sum(resid_low.astype(jnp.float32)))
    for block in range(4):
        for i in range(2):
            vec_out[2 * ctx + block // 2, 8 + block % 2 * 2 + i : 9 + block % 2 * 2 + i, :] = up_sums[block][
                :, i * 128 : (i + 1) * 128
            ]
    for piece in (3, 4, 5, 6):
        settle(piece)
    probs_all = (up_all, down_all, h_two_all, grad_all)

    def attend_again(head):
        lo, hi = head * HD, (head + 1) * HD
        for start in range(0, cap, rows):
            stop = start + rows
            queries = qkv_ref[start:stop, lo:hi] * jnp.asarray(factor, jnp.bfloat16)
            keys = qkv_ref[:stop, width + lo : width + hi]
            scores = masked_scores(queries, keys, ids_row_ref, ids_col_ref, start, stop)
            probs = jnp.exp(scores - lse_ref[head : head + 1, start:stop])
            probs_all[head][:stop, start:stop] = probs.astype(jnp.bfloat16)

    for head in range(heads):
        attend_again(head)
        if head == 1:
            down_scatter.relay(plane_of(2))
            up_scatter(plane_of(2)).relay()
    gather.forward()
    gather.end()
    grad_heads[...] = contract_cols(resid_all[...], outw_all[...]).astype(jnp.bfloat16)
    down_scatter.relay(plane_of(3))
    up_scatter(plane_of(3)).relay()
    out_scatter = Scatter(out_keep, out_out, out_yin, out_zin, out_sent, out_landed)
    out_part = contract_rows(mixed_ref[...], resid_all[...])
    for plane in range(PLANES):
        lo = plane * 64
        out_scatter.store(plane, out_part[lo : lo + 32], out_part[lo + 32 : lo + 64])
    out_scatter.begin()

    def attend_back_head(head):
        pair, side = head // 2, head % 2
        lo, hi = head * HD, (head + 1) * HD
        for start in reversed(range(0, cap, rows)):
            stop = start + rows
            queries = qkv_ref[start:stop, lo:hi] * jnp.asarray(factor, jnp.bfloat16)
            keys = qkv_ref[:stop, width + lo : width + hi]
            values = qkv_ref[:stop, 2 * width + lo : 2 * width + hi]
            grads = grad_heads[start:stop, lo:hi]
            probs_low = probs_all[head][:stop, start:stop]
            probs = probs_low.astype(jnp.float32)
            grad_probs = contract_cols(values, grads)
            delta = jnp.sum(probs * grad_probs, axis=0, keepdims=True)
            grad_scores = (probs * (grad_probs - delta)).astype(jnp.bfloat16)
            query_grad = contract_rows(keys, grad_scores).T * factor
            grad_qkv[pair, start:stop, side * HD : side * HD + HD] = query_grad.astype(jnp.bfloat16)
            key_grad = jnp.dot(grad_scores, queries, preferred_element_type=jnp.float32)
            value_grad = jnp.dot(probs_low, grads, preferred_element_type=jnp.float32)
            if stop == cap:
                key_acc[...] = key_grad
                value_acc[...] = value_grad
            else:
                key_acc[:stop, :] += key_grad
                value_acc[:stop, :] += value_grad
        lo = 128 + side * HD
        grad_qkv[pair, :, lo : lo + HD] = key_acc[...].astype(jnp.bfloat16)
        grad_qkv[pair, :, lo + 128 : lo + 128 + HD] = value_acc[...].astype(jnp.bfloat16)

    def qkv_scatter(pair):
        return Scatter(
            qkv_keep.at[pair], qkv_out.at[pair], qkv_yin.at[pair], qkv_zin.at[pair],
            qkv_sent.at[pair], qkv_landed.at[pair],
        )

    def pair_grads(pair):
        part = contract_rows(grad_qkv[pair], h_one_all[...])
        scatter = qkv_scatter(pair)
        for plane in range(PLANES):
            lo = plane * 256
            scatter.store(plane, part[:, lo : lo + 128], part[:, lo + 128 : lo + 256])
        scatter.begin()
        sums = column_sum(grad_qkv[pair].astype(jnp.float32))
        vec_out[2 * ctx + pair, 2:3, :] = sums[:, :128]
        vec_out[2 * ctx + pair, 3:4, :] = sums[:, 256:]

    def pair_back(pair):
        weight = jnp.concatenate(
            [qkvw_all[i, :, pair * 128 : pair * 128 + 128] for i in range(3)], axis=1
        )
        for chunk in range(4):
            here = slice(chunk * 256, (chunk + 1) * 256)
            part = contract_cols(grad_qkv[pair, here, :], weight)
            if pair == 0:
                back_acc[here, :] = part
            else:
                back_acc[here, :] += part

    attend_back_head(0)
    attend_back_head(1)
    pair_grads(0)
    pair_back(0)
    out_scatter.relay()
    output_ref[...] = (resid_ref[...] + outs.finish() + vec_ref[7:8, :]).astype(jnp.bfloat16)
    attend_back_head(2)
    attend_back_head(3)
    pair_back(1)
    back.settle()
    last = row_reduce(back_acc, 2)
    last.begin()
    pair_grads(1)
    last.relay()
    qkv_scatter(0).relay()
    for block in range(4):
        up_grad_ref[:, block * 256 : (block + 1) * 256] = up_scatter(block).finish().T
    down_grad_ref[...] = down_scatter.finish()
    out_grad_ref[...] = out_scatter.finish()
    values = x_ref[...].astype(jnp.float32)
    qkv_scatter(1).relay()
    grad_h_one = last.finish()
    put_vector(0, column_sum(grad_h_one * centre_of(values)))
    put_vector(1, column_sum(grad_h_one))

    def vec_copy(step):
        target = lax.rem(place + step, 8)
        return remote(
            vec_out.at[target], vec_in.at[step - 1], vec_sent.at[step - 1], vec_landed.at[step - 1],
            (target, ctx),
        )

    def ctx_copy(step):
        return remote(
            vec_ctx.at[ctx], vec_ctx.at[ctx], ctx_sent.at[step - 1], ctx_landed.at[step - 1],
            (place, lax.rem(ctx + step, 4)),
        )

    for step in range(1, 8):
        vec_copy(step).start()
    input_grad_ref[...] += norm_back(values, grad_h_one * vec_ref[0:1, :])
    total = vec_out[place]
    for step in range(1, 8):
        vec_copy(step).wait_recv()
        total = total + vec_in[step - 1]
    vec_ctx[ctx] = total
    for step in range(1, 4):
        ctx_copy(step).start()
    for pair in range(2):
        done = qkv_scatter(pair).finish().T
        for i in range(3):
            qkv_grad_ref[i, :, pair * 128 : pair * 128 + 128] = done[:, i * 128 : (i + 1) * 128]
    for step in range(1, 4):
        source = lax.rem(ctx + 4 - step, 4)
        remote(
            vec_ctx.at[source], vec_ctx.at[source], ctx_sent.at[step - 1], ctx_landed.at[step - 1],
            (place, source),
        ).wait_recv()
    sums_ref[...] = ((vec_ctx[0] + vec_ctx[1]) + vec_ctx[2]) + vec_ctx[3]
    for use in (outs, last):
        use.settle()
    for block in range(4):
        up_scatter(block).settle()
    down_scatter.settle()
    out_scatter.settle()
    for pair in range(2):
        qkv_scatter(pair).settle()
    for step in range(1, 8):
        vec_copy(step).wait_send()
    for step in range(1, 4):
        ctx_copy(step).wait_send()
    for piece in range(3):
        settle(piece)


def block_pass(
    block_input, cotangent, doc_ids, ln1_gain, ln1_bias, qv_bias, out_bias, ln2_gain, ln2_bias, down_bias,
    up_bias, qkv_weight, out_weight, up_weight, down_weight, heads, factor,
):
    rows, model = block_input.shape
    cap = doc_ids.shape[1]
    width = heads * HD
    hidden = up_weight.shape[1]
    low, wide = jnp.bfloat16, jnp.float32
    anywhere = pl.BlockSpec(memory_space=pl.ANY)
    vmem = pl.BlockSpec(memory_space=pltpu.VMEM)
    shape = jax.ShapeDtypeStruct
    room, sems = pltpu.VMEM, pltpu.SemaphoreType.DMA

    def scatter_room(*lead_and_tail):
        lead, tail = lead_and_tail
        return [
            room(lead + (4,) + tail, wide),
            room(lead + (4,) + tail, low),
            room(lead + (4,) + tail, low),
            room(lead + (3,) + tail, low),
        ]

    return pl.pallas_call(
        functools.partial(block_kernel, heads, factor),
        out_shape=(
            shape((rows, model), low),
            shape((rows, model), wide),
            shape((3, model // 8, width), wide),
            shape((width // 8, model), wide),
            shape((model // 8, hidden), wide),
            shape((hidden // 8, model), wide),
            shape((16, 128), wide),
        ),
        in_specs=[vmem] * 11 + [anywhere] * 4,
        out_specs=(vmem,) * 7,
        scratch_shapes=[
            room((model, hidden), low),
            room((hidden, model), low),
            room((3, model, width), low),
            room((width, model), low),
            room((cap, model), low),
            room((16, model), wide),
            room((cap, model), low),
            room((cap, 3 * width), low),
            room((cap, width), low),
            room((heads, cap), wide),
            room((rows, model), wide),
            room((cap, model), low),
            room((cap, 1), jnp.int32),
            room((16, 128), low),
            room((8 * 16, 128), low),
            room((cap, model), wide),
            room((cap, model), wide),
            room((4, 1, 256), wide),
            room((cap, model), low),
            room((cap, width), low),
            room((2, cap, 384), low),
            room((cap, HD), wide),
            room((cap, HD), wide),
            room((2, cap, 256), low),
            room((2, cap, 256), low),
            room((2, 2, rows, model), low),
            room((2, 2, rows, model), low),
            room((2, rows, model), low),
            room((2, rows, model), low),
        ]
        + scatter_room((4,), (256, 128))
        + [
            room((4, 128, model), wide),
            room((4, 128, model), low),
            room((4, 128, model), low),
            room((3, 128, model), low),
        ]
        + scatter_room((), (32, model))
        + scatter_room((2,), (384, 128))
        + [
            room((8, 16, 128), wide),
            room((7, 16, 128), wide),
            room((4, 16, 128), wide),
            sems((7, 6)),
            sems((7, 6)),
            sems((7, 7)),
            sems((7, 7)),
            sems((7,)),
            sems((4, 3)),
            sems((4, 3)),
            sems((4, 3)),
            sems((4, 3)),
            sems((4, 4)),
            sems((4, 4)),
            sems((2, 4)),
            sems((4,)),
            sems((3,)),
            sems((4,)),
            sems((4,)),
            sems((2, 4)),
            sems((2, 4)),
            sems((7,)),
            sems((7,)),
            sems((3,)),
            sems((3,)),
        ],
        compiler_params=pltpu.CompilerParams(
            collective_id=1, has_side_effects=True, vmem_limit_bytes=62 * 2**20
        ),
        cost_estimate=pl.CostEstimate(
            flops=24 * cap * model * hidden,
            bytes_accessed=32 * 2**20,
            transcendentals=2 * cap * cap * heads,
        ),
        name="block_pass",
    )(
        block_input, cotangent, doc_ids, ln1_gain, ln1_bias, qv_bias, out_bias, ln2_gain, ln2_bias, down_bias,
        up_bias, qkv_weight, out_weight, up_weight, down_weight,
    )


def finish_kernel(*refs):
    wide_in, sums_ref = refs[:6], refs[6]
    wide_out, vectors, sem = refs[7:13], refs[13:21], refs[21]
    copies = [
        pltpu.make_async_copy(source, target, sem.at[i])
        for i, (source, target) in enumerate(zip(wide_in, wide_out))
    ]
    for copy in copies:
        copy.start()
    gain1, shift1, qv, oshift, gain2, shift2, dshift, ushift = vectors
    for ref, row in ((gain1, 0), (shift1, 1), (oshift, 4), (gain2, 5), (shift2, 6), (dshift, 7)):
        ref[...] = sums_ref[row]
    qv[...] = sums_ref[2:4, :]
    for i in range(4):
        ushift[i * 128 : (i + 1) * 128] = sums_ref[8 + i]
    for copy in copies:
        copy.wait()


def finish_pass(arrays, sums):
    anywhere = pl.BlockSpec(memory_space=pl.ANY)
    vmem = pl.BlockSpec(memory_space=pltpu.VMEM)
    shape = jax.ShapeDtypeStruct
    piece = sums.shape[1]
    sizes = [(piece,), (piece,), (2, piece), (piece,), (piece,), (piece,), (piece,), (4 * piece,)]
    return pl.pallas_call(
        finish_kernel,
        out_shape=tuple(shape(a.shape, a.dtype) for a in arrays)
        + tuple(shape(size, jnp.float32) for size in sizes),
        in_specs=[vmem] * 7,
        out_specs=(anywhere,) * 6 + (vmem,) * 8,
        scratch_shapes=[pltpu.SemaphoreType.DMA((6,))],
        name="finish_pass",
    )(*arrays, sums)


def on_device_general(
    block_input,
    ln1_gain,
    ln1_bias,
    qkv_weight,
    qv_bias,
    out_weight,
    out_bias,
    ln2_gain,
    ln2_bias,
    up_weight,
    up_bias,
    down_weight,
    down_bias,
    doc_ids,
    cotangent,
):
    shards = lax.axis_size("fsdp")
    small = jnp.concatenate(
        [
            ln1_gain,
            ln1_bias,
            qv_bias[0],
            qv_bias[1],
            out_bias,
            ln2_gain,
            ln2_bias,
            down_bias,
            up_bias,
        ]
    )
    rows = block_input.shape[0]
    model = block_input.shape[1]
    groups = lax.axis_size("ctx")
    place = lax.axis_index("ctx")
    capacity = rows * groups
    width = qkv_weight.shape[2]
    heads_here = width // HD
    hidden_here = up_weight.shape[1]
    factor = 1.0 / HD**0.5
    group_ids = doc_ids[0]
    own_ids = lax.dynamic_slice_in_dim(group_ids, place * rows, rows)
    input_all = gather_rows(block_input)
    qkv_rows = qkv_weight.shape[0]
    small_rows = -(-small.shape[0] // (3 * width * 16)) * 16
    first = jnp.concatenate(
        [
            qkv_weight.reshape(qkv_rows, 3 * width),
            jnp.pad(small, (0, small_rows * 3 * width - small.shape[0])).reshape(
                small_rows, 3 * width
            ),
        ]
    )
    first_all = gather_weight(first)
    small_all = first_all[:, qkv_rows:].reshape(shards, -1)[:, : small.shape[0]]
    piece = model // shards
    gain_one, shift_one, query_shift, value_shift, out_shift, gain_two, shift_two, down_shift = (
        small_all[:, i * piece : (i + 1) * piece].reshape(model) for i in range(8)
    )
    up_shift = small_all[:, 8 * piece :].reshape(-1)
    qv_full = jnp.stack([query_shift, value_shift])
    qkv_flat = first_all[:, :qkv_rows].reshape(model, 3 * width)
    out_full = gather_weight(out_weight).reshape(width, model)
    up_full = gather_weight(up_weight).reshape(model, hidden_here)
    down_full = gather_weight(down_weight).reshape(hidden_here, model)
    cot_all = gather_rows(cotangent)
    qv_here = lax.dynamic_slice_in_dim(qv_full.astype(jnp.float32), place * width, width, 1)
    qkv_shift = jnp.concatenate([qv_here[0], jnp.zeros((width,), jnp.float32), qv_here[1]])
    up_here = lax.dynamic_slice_in_dim(
        up_shift.astype(jnp.float32), place * hidden_here, hidden_here, 0
    )
    input_float = block_input.astype(jnp.float32)
    norm_one_all = normalize(input_all.astype(jnp.float32))
    h_one_all = (norm_one_all * gain_one + shift_one).astype(jnp.bfloat16)
    qkv_proj = project(h_one_all, qkv_flat)
    qkv = (qkv_proj + qkv_shift).astype(jnp.bfloat16)
    mixed_all, log_sums = attend(qkv, group_ids, heads_here, factor)
    out_part = project(mixed_all, out_full)
    resid = input_float + reduce_rows(out_part) + out_shift
    norm_two = normalize(resid)
    h_two = (norm_two * gain_two + shift_two).astype(jnp.bfloat16)
    h_two_all = gather_rows(h_two)
    live = (own_ids >= 0).astype(jnp.float32)
    grad_out = cotangent.astype(jnp.float32) * live[:, None]
    grad_low = grad_out.astype(jnp.bfloat16)
    down_shift_grad = jnp.sum(grad_low.astype(jnp.float32), axis=0)
    grad_all = jnp.where(group_ids[:, None] >= 0, cot_all, jnp.zeros_like(cot_all))
    act_low, grad_pre, up_sums, down_part, back_part = mlp(
        h_two_all, grad_all, up_full, up_here, down_full
    )
    grad_h_two = reduce_rows(back_part)
    output = (resid + reduce_rows(down_part) + down_shift).astype(jnp.bfloat16)
    down_grad = weight_grad(act_low, grad_all)
    up_grad = weight_grad(h_two_all, grad_pre)
    up_sums = up_sums[0]
    up_shift_grad = lax.dynamic_update_slice_in_dim(
        jnp.zeros((FF,), jnp.float32), up_sums, place * hidden_here, 0
    )
    gain_two_grad = jnp.sum(grad_h_two * norm_two, axis=0)
    shift_two_grad = jnp.sum(grad_h_two, axis=0)
    unused_two, norm_back_two = jax.vjp(normalize, resid)
    grad_resid = grad_out + norm_back_two(grad_h_two * gain_two.astype(jnp.float32))[0]
    resid_low = grad_resid.astype(jnp.bfloat16)
    out_shift_grad = jnp.sum(resid_low.astype(jnp.float32), axis=0)
    resid_all = gather_rows(resid_low)
    out_grad = weight_grad(mixed_all, resid_all)
    grad_heads = project_back(resid_all, out_full).astype(jnp.bfloat16)
    grad_qkv = attend_back(qkv, grad_heads, log_sums, group_ids, heads_here, factor)
    qkv_grad = weight_grad(h_one_all, grad_qkv).reshape(qkv_weight.shape[0], 3, width)
    column_sums = jnp.sum(grad_qkv.astype(jnp.float32), axis=0).reshape(3, width)
    qv_local = jnp.stack([column_sums[0], column_sums[2]])
    qv_grad = lax.dynamic_update_slice_in_dim(
        jnp.zeros((2, model), jnp.float32), qv_local, place * width, 1
    )
    grad_h_one_part = project_back(grad_qkv, qkv_flat)
    gain_one_grad = jnp.sum(grad_h_one_part * norm_one_all, axis=0)
    shift_one_grad = jnp.sum(grad_h_one_part, axis=0)
    grad_h_one = reduce_rows(grad_h_one_part)
    unused_one, norm_back_one = jax.vjp(normalize, input_float)
    input_grad = grad_resid + norm_back_one(grad_h_one * gain_one.astype(jnp.float32))[0]
    packed = jnp.concatenate(
        [
            part.reshape(shards, -1)
            for part in (
                gain_one_grad,
                shift_one_grad,
                qv_grad[0],
                qv_grad[1],
                out_shift_grad,
                gain_two_grad,
                shift_two_grad,
                down_shift_grad,
                up_shift_grad,
            )
        ],
        1,
    )
    sums = sum_ctx(scatter_fsdp(packed.reshape(shards, -1, 128), jnp.float32)).reshape(-1)
    (
        gain_one_sum,
        shift_one_sum,
        query_sum,
        value_sum,
        out_shift_sum,
        gain_two_sum,
        shift_two_sum,
        down_shift_sum,
    ) = (sums[i * piece : (i + 1) * piece] for i in range(8))
    qv_sum = jnp.stack([query_sum, value_sum])
    up_shift_sum = sums[8 * piece :]
    return (
        output,
        input_grad,
        gain_one_sum,
        shift_one_sum,
        qkv_grad,
        qv_sum,
        out_grad,
        out_shift_sum,
        gain_two_sum,
        shift_two_sum,
        up_grad,
        up_shift_sum,
        down_grad,
        down_shift_sum,
    )


def on_device(
    block_input,
    ln1_gain,
    ln1_bias,
    qkv_weight,
    qv_bias,
    out_weight,
    out_bias,
    ln2_gain,
    ln2_bias,
    up_weight,
    up_bias,
    down_weight,
    down_bias,
    doc_ids,
    cotangent,
):
    model = block_input.shape[1]
    if lax.axis_size("fsdp") != 8 or lax.axis_size("ctx") != 4:
        return on_device_general(
            block_input, ln1_gain, ln1_bias, qkv_weight, qv_bias, out_weight, out_bias, ln2_gain,
            ln2_bias, up_weight, up_bias, down_weight, down_bias, doc_ids, cotangent,
        )
    width = qkv_weight.shape[2]
    heads_here = width // HD
    factor = 1.0 / HD**0.5
    *grads, sums = block_pass(
        block_input, cotangent, doc_ids, ln1_gain, ln1_bias, qv_bias, out_bias, ln2_gain, ln2_bias,
        down_bias, up_bias, qkv_weight.transpose(1, 0, 2), out_weight, up_weight, down_weight, heads_here,
        factor,
    )
    (
        output, input_grad, qkv_grad, out_grad, up_grad, down_grad, gain_one_sum, shift_one_sum, qv_sum,
        out_shift_sum, gain_two_sum, shift_two_sum, down_shift_sum, up_shift_sum,
    ) = finish_pass(grads, sums)
    return (
        output,
        input_grad,
        gain_one_sum,
        shift_one_sum,
        qkv_grad.transpose(1, 0, 2),
        qv_sum,
        out_grad,
        out_shift_sum,
        gain_two_sum,
        shift_two_sum,
        up_grad,
        up_shift_sum,
        down_grad,
        down_shift_sum,
    )


def solution(mesh):
    placed = (
        P(("fsdp", "ctx"), None),
        P("fsdp"),
        P("fsdp"),
        P("fsdp", None, "ctx"),
        P(None, "fsdp"),
        P(("ctx", "fsdp"), None),
        P("fsdp"),
        P("fsdp"),
        P("fsdp"),
        P("fsdp", "ctx"),
        P("fsdp"),
        P(("ctx", "fsdp"), None),
        P("fsdp"),
        P("fsdp", None),
        P(("fsdp", "ctx"), None),
    )
    return jax.shard_map(
        on_device,
        mesh=mesh,
        in_specs=placed,
        out_specs=(
            P(("fsdp", "ctx"), None),
            P(("fsdp", "ctx"), None),
            P("fsdp"),
            P("fsdp"),
            P("fsdp", None, "ctx"),
            P(None, "fsdp"),
            P(("ctx", "fsdp"), None),
            P("fsdp"),
            P("fsdp"),
            P("fsdp"),
            P("fsdp", "ctx"),
            P("fsdp"),
            P(("ctx", "fsdp"), None),
            P("fsdp"),
        ),
        check_vma=False,
    )
```
